256 devices in a mesh: head: 4 (over z_lo), seq: 64 (over y, x, z_hi, core).
Axes of the slice: x: 4, y: 4, z: 8 (z_hi: 2, z_lo: 4; z = z_hi * 4 + z_lo), core: 2. Of those that a mesh axis runs over, the one named last changes fastest.
Arguments:
- query_mla: bfloat16 [256, 24576], P(None, 'head'), may hold values from -6 to 6
- key_mla: bfloat16 [32768, 24576], P('seq', 'head'), may hold values from -6 to 6
- lse: float32 [256, 128], P(None, 'head'), may hold values from 3 to 6
- query_index: bfloat16 [256, 8192], P(None, 'head'), may hold values from -0.5 to 0.5
- key_index: bfloat16 [32768, 128], P('seq'), may hold values from -6 to 6
- head_weight: float32 [256, 64], P(None, 'head'), may hold values from -25 to 25
- query_pos: int32 [256], replicated, may hold values from 8192 to 32767
- key_block: int32 [64], P('seq'), may hold values from 0 to 63, each once
Outputs:
- kl: bfloat16 [256], replicated
- grad_query_index: bfloat16 [256, 8192], P(None, 'head')
- grad_head_weight: bfloat16 [256, 64], P(None, 'head')
- grad_key_index: bfloat16 [32768, 128], P('seq')
The draws below stay inside these ranges and needn't reach their ends.
Inputs may be any that keep to these rules, and one draw needn't show every extreme that they name: key_block is a permutation of 0 to 63; the keys of index d of seq hold the positions key_block[d] * 512 to key_block[d] * 512 + 511.
All inputs are finite; a program needn't handle non-finite values.
Results may differ from the reference program's by a relative error of at most 0.012.
Values may be sent and summed in bfloat16 or wider, within the bound.
A program may use at most 128 MiB of HBM per device.

```python
import jax
import jax.numpy as jnp
from jax import lax

H = 128
DQK = 192
HI = 64
DI = 128
ROWS = 256
KEY_DEV = 512
CONTEXT = 32768
N_SEQ = 64


def draw_head_weight(key, part):
    base_key = jax.random.fold_in(key, 11)
    return jnp.clip(0.75 * jax.random.normal(base_key, (ROWS, HI), jnp.float32), -2.25, 2.25)


def place_ends(values, stream_key, low, largest):
    index_at = [jax.random.randint(jax.random.fold_in(stream_key, axis), (), 0, length) for axis, length in enumerate(values.shape)]
    longest = values.shape.index(max(values.shape))
    beside = index_at[:longest] + [(index_at[longest] + 1) % values.shape[longest]] + index_at[longest + 1:]
    return values.at[tuple(index_at)].set(low).at[tuple(beside)].set(largest)


def shard_levels(rng, shape, cuts, least, top_value):
    gain = 1.0
    for dim, shards_of in cuts:
        steps = jax.random.uniform(jax.random.fold_in(jax.random.fold_in(rng, 6), dim), (shards_of,), jnp.float32, least / len(cuts), top_value / len(cuts))
        gain = gain * jnp.repeat(jnp.exp(steps), shape[dim] // shards_of).reshape((-1,) + (1,) * (len(shape) - 1 - dim))
    return gain


def noise(key, extent, spread, limit, shards=(), kind=jnp.bfloat16):
    values = jax.random.normal(key, extent, jnp.float32) * spread
    if len(shards) > 0:
        values = shard_levels(key, extent, shards, -0.22, 0.18) * values
    return jnp.clip(values, min=-limit, max=limit).astype(kind)


def setup_inputs(seed: int = 0) -> dict:
    seeds = jax.random.split(jax.random.key(seed), 9)
    query_mla = noise(seeds[0], (ROWS, H * DQK), 1.0, 6.0, ((1, 4),))
    key_mla = noise(seeds[1], (CONTEXT, H * DQK), 1.0, 6.0, ((0, 64), (1, 4)))
    lse = jnp.clip(3.0 + 3.0 * jax.random.uniform(seeds[2], (ROWS, H), jnp.float32) ** shard_levels(seeds[2], (ROWS, H), ((1, 4),), -0.2, 0.2), 3.0, 6.0)
    query_index = noise(seeds[3], (ROWS, HI * DI), DI ** -0.5, 0.5, ((1, 4),))
    key_index = noise(seeds[4], (CONTEXT, DI), 1.0, 6.0, ((0, 64),))
    head_weight = draw_head_weight(jax.random.fold_in(seeds[8], 71), 0)
    query_pos = place_ends(jax.random.randint(seeds[6], (ROWS,), CONTEXT // 4, CONTEXT), jax.random.fold_in(seeds[6], 1), CONTEXT // 4, CONTEXT - 1).astype(jnp.int32)
    key_block = jax.random.permutation(seeds[7], N_SEQ).astype(jnp.int32)
    return {"query_mla": query_mla, "key_mla": key_mla, "lse": lse, "query_index": query_index, "key_index": key_index, "head_weight": head_weight, "query_pos": query_pos, "key_block": key_block}


def reference(query_mla, key_mla, lse, query_index, key_index, head_weight, query_pos, key_block):
    positions = (jnp.repeat(key_block, KEY_DEV) * KEY_DEV + jnp.tile(jnp.arange(KEY_DEV, dtype=jnp.int32), N_SEQ)).astype(jnp.int32)
    valid = positions[None, :] <= query_pos[:, None]
    queries = query_mla.reshape(ROWS, H, DQK)
    mla_keys = key_mla.reshape(CONTEXT, H, DQK)

    def add_head(carried, head_index):
        q_head = lax.dynamic_index_in_dim(queries, head_index, 1, keepdims=False)
        k_head = lax.dynamic_index_in_dim(mla_keys, head_index, 1, keepdims=False)
        score = jnp.dot(q_head, k_head.T, preferred_element_type=jnp.float32) * (DQK ** -0.5)
        shifts = lax.dynamic_index_in_dim(lse, head_index, 1, keepdims=False)
        return carried + jnp.where(valid, jnp.exp(score - shifts[:, None]), 0.0), None

    attention, _ = lax.scan(add_head, jnp.zeros((ROWS, CONTEXT), jnp.float32), jnp.arange(H, dtype=jnp.int32))
    indexer_q = query_index.reshape(ROWS, HI, DI)

    def index_dots(head_index):
        q_head = lax.dynamic_index_in_dim(indexer_q, head_index, 1, keepdims=False)
        return jnp.dot(q_head, key_index.T, preferred_element_type=jnp.float32), q_head

    def add_logit(carried, head_index):
        dots, _ = index_dots(head_index)
        weights = lax.dynamic_index_in_dim(head_weight, head_index, 1, keepdims=False)
        return carried + weights[:, None] * jnp.maximum(dots, 0.0), None

    logit, _ = lax.scan(add_logit, jnp.zeros((ROWS, CONTEXT), jnp.float32), jnp.arange(HI, dtype=jnp.int32))
    total = jnp.sum(attention, axis=1)
    target = attention / total[:, None]
    masked = jnp.where(valid, logit, -1e30)
    peak = jnp.max(masked, axis=1)
    norm = jnp.sum(jnp.where(valid, jnp.exp(masked - peak[:, None]), 0.0), axis=1)
    log_prob = masked - peak[:, None] - jnp.log(norm)[:, None]
    prob = jnp.where(valid, jnp.exp(log_prob), 0.0)
    log_target = jnp.log(jnp.where(valid, attention, 1.0)) - jnp.log(total)[:, None]
    kl = jnp.sum(jnp.where(valid, target * (log_target - log_prob), 0.0), axis=1).astype(jnp.bfloat16)
    dlogit = jnp.where(valid, prob - target, 0.0).astype(jnp.bfloat16)
    grad_rows = dlogit.astype(jnp.float32)

    def backward(carried, head_index):
        dots, q_head = index_dots(head_index)
        weights = lax.dynamic_index_in_dim(head_weight, head_index, 1, keepdims=False)
        grad_weight = jnp.sum(grad_rows * jnp.maximum(dots, 0.0), axis=1)
        opened = dots > 0
        gated = jnp.where(opened, dlogit, 0).astype(jnp.bfloat16)
        grad_query = jnp.dot(gated, key_index, preferred_element_type=jnp.float32) * weights[:, None]
        coef = jnp.where(opened, grad_rows * weights[:, None], 0.0).astype(jnp.bfloat16)
        grad_key = carried + jnp.dot(coef.T, q_head, preferred_element_type=jnp.float32)
        return grad_key, (grad_weight, grad_query)

    grad_key, (grad_weights, grad_queries) = lax.scan(backward, jnp.zeros((CONTEXT, DI), jnp.float32), jnp.arange(HI, dtype=jnp.int32))
    grad_head_weight = grad_weights.T.astype(jnp.bfloat16)
    grad_query_index = jnp.transpose(grad_queries, (1, 0, 2)).reshape(ROWS, HI * DI).astype(jnp.bfloat16)
    return kl, grad_query_index, grad_head_weight, grad_key.astype(jnp.bfloat16)
```

```python
import functools
import math

import jax
import jax.numpy as jnp
from jax import lax
from jax.experimental import pallas as pl
from jax.experimental.pallas import tpu as pltpu
from jax.sharding import PartitionSpec as P

MESH = pl.DeviceIdType.MESH
F32 = jnp.float32
BF16 = jnp.bfloat16

GROUPS = 4
PLANE = 16
ROWS = 64
HALF = 32
KEYS = 512
PAIRS = 16
WIDE = 192
LANES = 128
CHUNKS = 8
CHUNK_PAIRS = PAIRS // CHUNKS
CHUNK = CHUNK_PAIRS * 2 * WIDE
NT = (((1,), (1,)), ((), ()))
TN = (((0,), (0,)), ((), ()))
NN = (((1,), (0,)), ((), ()))
LOG2E = math.log2(math.e)


def dot(a, b, dims):
    return lax.dot_general(a, b, dims, preferred_element_type=F32)


def body(
    qm, km, lse, qi, ki, wpack, hw, qpos, kb,
    kl_out, gq_out, gw_out, gk_out,
    qbuf, kbuf, acc, blk, att_s, att_r, qall, wall, dots, wq, lacc, ebuf, abuf,
    st_mine, st_all, st_two, gb, part, g2, r2, g3, r3, qfin, prod, gwb, gk_s, gk_r,
    ld, qloc, qz, wz, qx, qc, at, st1, st2, kls, d1, d2, d3, d4, d4c, gws, gwc, gks, gkt,
):
    h = lax.axis_index("head")
    s = lax.axis_index("seq")
    core = s % 2
    zh = (s // 2) % 2
    yx = s // 4

    def at_plane(p):
        return (h, p * 4 + zh * 2 + core)

    def at_head(g):
        return (g, s)

    partner = (h, yx * 4 + zh * 2 + (1 - core))

    def rc(src, dst, sems, k, dev):
        return pltpu.make_async_remote_copy(
            src_ref=src, dst_ref=dst, send_sem=sems.at[0, k], recv_sem=sems.at[1, k],
            device_id=dev, device_id_type=MESH,
        )

    def loop(lo, hi, f):
        def step(k, carry):
            f(k)
            return carry

        lax.fori_loop(lo, hi, step, 0)

    def group_of(r):
        return (h + r) % GROUPS

    bar = pltpu.get_barrier_semaphore()

    def hello(dev):
        pl.semaphore_signal(bar, inc=1, device_id=dev, device_id_type=MESH)

    loop(1, PLANE, lambda p: hello(at_plane((yx + p) % PLANE)))
    for r in range(GROUPS):
        if r:
            hello(at_head((h + r) % GROUPS))
        hello(((h + r) % GROUPS, yx * 4 + (1 - zh) * 2 + core))
    hello(partner)
    hello((h, yx * 4 + (1 - zh) * 2 + (1 - core)))

    def chunk_copies(k):
        cols = pl.ds(pl.multiple_of(k * CHUNK, LANES), CHUNK)
        return (
            pltpu.make_async_copy(qm.at[:, cols], qbuf.at[:, cols], ld.at[0, k]),
            pltpu.make_async_copy(km.at[:, cols], kbuf.at[:, cols], ld.at[1, k]),
        )

    def start_chunk(k):
        for c in chunk_copies(k):
            c.start()

    loop(0, CHUNKS, start_chunk)

    def own_head(k):
        cols = pl.ds(pl.multiple_of(k * LANES, LANES), LANES)
        return pltpu.make_async_copy(qi.at[h, :, :, cols], qall.at[0, k], qloc.at[k])

    loop(0, PLANE, lambda k: own_head(k).start())
    my_cols = pl.ds(pl.multiple_of(yx * LANES, LANES), LANES)
    fin_copy = pltpu.make_async_copy(qi.at[:, core, :, my_cols], qfin, qloc.at[PLANE])
    fin_copy.start()

    acc[...] = jnp.zeros_like(acc)
    scale = WIDE ** -0.5 * LOG2E

    def attend(k):
        for c in chunk_copies(k):
            c.wait()
        for j in range(CHUNK_PAIRS):
            pair = k * CHUNK_PAIRS + j
            base = pair * (2 * WIDE)
            lo = pl.ds(pl.multiple_of(base, LANES), 2 * LANES)
            hi = pl.ds(pl.multiple_of(base + LANES, LANES), 2 * LANES)
            lane = lax.broadcasted_iota(jnp.int32, (256, 2 * LANES), 1)
            q_a = jnp.where(lane < WIDE, qbuf[:, lo], 0).astype(BF16)
            q_b = jnp.where(lane >= 2 * LANES - WIDE, qbuf[:, hi], 0).astype(BF16)
            ls = lse[pair]
            s_a = dot(kbuf[:, lo], q_a, NT)
            s_b = dot(kbuf[:, hi], q_b, NT)
            acc[...] += jnp.exp2(s_a * scale - ls[0:1, :]) + jnp.exp2(s_b * scale - ls[1:2, :])

    loop(0, 4, attend)

    pl.semaphore_wait(bar, PLANE - 1 + GROUPS - 1 + GROUPS + 2)

    wall[0] = wpack[h]

    def q_send(r):
        g = (h + r) % GROUPS
        slot = (GROUPS - r) % GROUPS
        mine = qi.at[g, core, :, my_cols]
        return (
            rc(mine, qall.at[slot, yx, core], qz, r, at_head(g)),
            rc(wpack.at[g], wall.at[slot], wz, r, at_head(g)),
        )

    def q_came(r):
        g = (h + r) % GROUPS
        slot = (GROUPS - r) % GROUPS
        return (
            rc(qall.at[slot, yx, core], qall.at[slot, yx, core], qz, r, at_head(g)),
            rc(wall.at[slot], wall.at[slot], wz, r, at_head(g)),
        )

    for r in range(1, GROUPS):
        for c in q_send(r):
            c.start()

    loop(4, CHUNKS, attend)

    left = lax.broadcasted_iota(jnp.int32, (256, LANES), 1) < ROWS

    for t in range(2):
        x = acc[0:256, t * LANES:(t + 1) * LANES]
        y = acc[256:512, t * LANES:(t + 1) * LANES]
        b0 = jnp.where(left, x, pltpu.roll(y, ROWS, 1))
        b1 = jnp.where(left, pltpu.roll(x, ROWS, 1), y)
        blk[2 * t] = b0
        blk[2 * t + 1] = b1
        att_s[2 * t] = b0.astype(BF16)
        att_s[2 * t + 1] = b1.astype(BF16)

    for r in range(1, GROUPS):
        for c in q_came(r):
            c.wait_recv()

    def q_plane(p):
        return rc(
            qall.at[1:GROUPS, yx, core], qall.at[1:GROUPS, yx, core], qx, p,
            at_plane((yx + p) % PLANE),
        )

    def q_core(p):
        src = (yx - p + PLANE) % PLANE
        return rc(qall.at[1:GROUPS, src, core], qall.at[1:GROUPS, src, core], qc, p, partner)

    def q_plane_came(p):
        src = (yx - p + PLANE) % PLANE
        return rc(
            qall.at[1:GROUPS, src, core], qall.at[1:GROUPS, src, core], qx, p,
            at_plane((yx + p) % PLANE),
        )

    def q_core_came(p):
        src = (yx - p + PLANE) % PLANE
        there = qall.at[1:GROUPS, src, 1 - core]
        return rc(there, there, qc, p, partner)

    loop(1, PLANE, lambda p: q_plane(p).start())
    q_core(0).start()

    def att_send(r):
        g = (h + r) % GROUPS
        return rc(att_s.at[g], att_r.at[r], at, r, at_head(g))

    for r in (2, 1, 3):
        att_send(r).start()

    lacc[...] = jnp.zeros_like(lacc)

    def index_quad(r, q):
        qq = qall[r, pl.ds(4 * q, 4)].reshape(4 * ROWS, LANES)
        d = dot(ki[...], qq, NT)
        cols = pl.ds(pl.multiple_of((r * 4 + q) * 2 * LANES, LANES), 2 * LANES)
        dots[:, cols] = d.astype(BF16)
        w0 = wall[r, pl.ds(2 * q, 1), :]
        w1 = wall[r, pl.ds(2 * q + 1, 1), :]
        lacc[...] += w0 * jnp.maximum(d[:, :LANES], 0.0) + w1 * jnp.maximum(d[:, LANES:], 0.0)

    loop(0, PLANE, lambda k: own_head(k).wait())
    for q in range(4):
        index_quad(0, q)

    def pass_on(p):
        q_plane_came(p).wait_recv()
        q_core(p).start()

    loop(1, PLANE, pass_on)
    loop(0, PLANE, lambda p: q_core_came(p).wait_recv())

    for r in range(1, GROUPS):
        for q in range(4):
            index_quad(r, q)

    for r in range(1, GROUPS):
        rc(att_r.at[r], att_r.at[r], at, r, at_head((h + r) % GROUPS)).wait_recv()
    a = blk[h] + att_r[1].astype(F32) + att_r[2].astype(F32) + att_r[3].astype(F32)
    ra = pltpu.roll(a, ROWS, 1)
    first = jnp.where(left, a, ra)
    second = jnp.where(left, ra, a)
    base = kb[0] * KEYS
    limit = qpos[h]
    for i, half in enumerate((first, second)):
        row = lax.broadcasted_iota(jnp.int32, (256, LANES), 0) + (base + i * 256)
        ok = row <= limit
        abuf[i * 256:(i + 1) * 256] = jnp.where(ok, half, 0.0)
        lg = lacc[i * 256:(i + 1) * 256]
        lg = lg + pltpu.roll(lg, ROWS, 1)
        lacc[i * 256:(i + 1) * 256] = jnp.where(ok, lg, -1e30)
    lm = lacc[...]
    peak = jnp.max(lm, axis=0, keepdims=True)
    rowid = lax.broadcasted_iota(jnp.int32, (KEYS, LANES), 0) + base
    ok = rowid <= limit
    rel = lm - peak
    e = jnp.where(ok, jnp.exp(rel), 0.0)
    ebuf[...] = e
    av = abuf[...]
    norm = jnp.sum(e, axis=0, keepdims=True)
    total = jnp.sum(av, axis=0, keepdims=True)
    cross = jnp.sum(
        jnp.where(ok, av * (jnp.log(jnp.where(ok, av, 1.0)) - rel), 0.0), axis=0, keepdims=True
    )
    pad = jnp.zeros((4, LANES), F32)
    tile = jnp.concatenate([peak, norm, total, cross, pad], axis=0)
    st_mine[...] = tile
    st_all[yx] = tile

    def st_send(p):
        return rc(st_mine, st_all.at[yx], st1, p, at_plane((yx + p) % PLANE))

    def st_came(p):
        src = (yx - p + PLANE) % PLANE
        return rc(st_all.at[src], st_all.at[src], st1, p, at_plane((yx + p) % PLANE))

    loop(1, PLANE, lambda p: st_send(p).start())

    wcol = jnp.transpose(wall[...].reshape(4 * 8, LANES))
    for r in range(GROUPS):
        for p in range(8):
            qq = qall[r, 2 * p:2 * p + 2].reshape(2 * ROWS, LANES).astype(F32)
            k = r * 8 + p
            wq[k * LANES:(k + 1) * LANES] = (qq * wcol[:, k:k + 1]).astype(BF16)

    def merge(t):
        pk = jnp.max(t[:, 0, :], axis=0, keepdims=True)
        nm = jnp.sum(t[:, 1, :] * jnp.exp(t[:, 0, :] - pk), axis=0, keepdims=True)
        tt = jnp.sum(t[:, 2, :], axis=0, keepdims=True)
        cr = jnp.sum(t[:, 3, :] + t[:, 2, :] * (pk - t[:, 0, :]), axis=0, keepdims=True)
        return pk, nm, tt, cr

    loop(1, PLANE, lambda p: st_came(p).wait_recv())
    tile2 = jnp.concatenate([*merge(st_all[...]), pad], axis=0)
    loop(1, PLANE, lambda p: st_send(p).wait_send())
    st_mine[...] = tile2
    st_two[0] = tile2

    def st_send2(k):
        dev = (h, yx * 4 + ((zh + k // 2) % 2) * 2 + (core + k % 2) % 2)
        return rc(st_mine, st_two.at[k], st2, k, dev)

    for k in (2, 3, 1):
        st_send2(k).start()
    for k in (1, 2, 3):
        st_send2(k).wait_recv()
    peak_g, norm_g, total_g, cross_g = merge(st_two[...])
    inv_t = 1.0 / total_g
    kl = cross_g * inv_t - jnp.log(total_g) + jnp.log(norm_g)
    kl_out[h] = jnp.broadcast_to(kl, (8, LANES))

    def kl_send(r):
        return rc(kl_out.at[h], kl_out.at[h], kls, r, at_head((h + r) % GROUPS))

    def kl_came(r):
        src = (h - r + GROUPS) % GROUPS
        return rc(kl_out.at[src], kl_out.at[src], kls, r, at_head((h + r) % GROUPS))

    for r in range(1, GROUPS):
        kl_send(r).start()

    grow = jnp.exp(peak - peak_g) / norm_g
    dl = (ebuf[...] * grow - abuf[...] * inv_t).astype(BF16)
    dl2 = jnp.concatenate([dl, dl], axis=1)
    zero = jnp.zeros_like(dl2)

    def g_send(r):
        return rc(gb.at[1 - core, r], part.at[r], d1, r, partner)

    for r in range(GROUPS):
        for q in range(4):
            lo = (r * 4 + q) * 2 * LANES
            g = jnp.where(dots[:, lo:lo + 2 * LANES] > 0, dl2, zero)
            dots[:, lo:lo + 2 * LANES] = g
            big = dot(g, ki[...], TN).astype(BF16).reshape(4, 2, HALF, LANES)
            gb[0, r, 4 * q:4 * q + 4] = big[:, 0]
            gb[1, r, 4 * q:4 * q + 4] = big[:, 1]
        g_send(r).start()

    for r in range(GROUPS):
        g_send(r).wait_recv()
        g2[:, r] = (gb[core, r].astype(F32) + part[r].astype(F32)).astype(BF16)

    def d2_send(p):
        to = (yx + p) % PLANE
        return rc(g2.at[to], r2.at[p], d2, p, at_plane(to))

    loop(1, PLANE, lambda p: d2_send(p).start())

    gk = jnp.zeros((KEYS, LANES), F32)
    for r in range(GROUPS):
        gk += dot(dots[:, r * 1024:(r + 1) * 1024], wq[r * 1024:(r + 1) * 1024], NN)
    gk_s[...] = gk.astype(BF16).reshape(4, LANES, LANES)

    def gk_send(r):
        g = (h + r) % GROUPS
        return rc(gk_s.at[g], gk_r.at[r], gks, r, at_head(g))

    for r in (2, 1, 3):
        gk_send(r).start()

    loop(1, PLANE, lambda p: d2_send(p).wait_recv())
    tot = g2[yx].astype(F32)
    for p in range(1, PLANE):
        tot += r2[p].astype(F32)
    g3[...] = tot.astype(BF16)

    def d3_send(r, other):
        k = 2 * r + other
        dev = ((h + r) % GROUPS, yx * 4 + ((zh + other) % 2) * 2 + core)
        return rc(g3.at[r], r3.at[k], d3, k, dev)

    for r, other in ((0, 1), (1, 1), (2, 1), (3, 1), (2, 0), (1, 0), (3, 0)):
        d3_send(r, other).start()

    for r in range(1, GROUPS):
        gk_send(r).wait_recv()
    mine = gk_s[h].astype(F32)
    for r in range(1, GROUPS):
        mine += gk_r[r].astype(F32)
    gk_out[h] = mine.astype(BF16)

    def gk_share(r):
        return rc(gk_out.at[h], gk_out.at[h], gkt, r, at_head((h + r) % GROUPS))

    def gk_came(r):
        src = (h - r + GROUPS) % GROUPS
        return rc(gk_out.at[src], gk_out.at[src], gkt, r, at_head((h + r) % GROUPS))

    for r in (2, 1, 3):
        gk_share(r).start()

    fin_copy.wait()
    for r, other in ((2, 0), (1, 0), (3, 0), (0, 1), (1, 1), (2, 1), (3, 1)):
        d3_send(r, other).wait_recv()
    onehot = lax.broadcasted_iota(jnp.int32, (HALF, PLANE), 1) == yx
    for r in range(GROUPS):
        g = (h - r + GROUPS) % GROUPS
        near = g3[0] if r == 0 else r3[2 * r]
        full = near.astype(F32) + r3[2 * r + 1].astype(F32)
        w = jnp.sum(jnp.where(onehot, hw[g, core], 0.0), axis=1, keepdims=True)
        gq_out[g, core, :, my_cols] = (full * w).astype(BF16)
        prod[g] = full * qfin[g].astype(F32)
    gw_row = jnp.sum(jnp.transpose(prod[...].reshape(LANES, LANES)), axis=0, keepdims=True)
    gwb[core, yx] = jnp.broadcast_to(gw_row, (8, LANES))

    def cols_of(p):
        return pl.ds(pl.multiple_of(p * LANES, LANES), LANES)

    def d4_pair(src_yx, dev, k):
        there = gq_out.at[:, core, :, cols_of(src_yx)]
        return rc(there, there, d4, k, dev), rc(gwb.at[core, src_yx], gwb.at[core, src_yx], gws, k, dev)

    def d4_start(p):
        for c in d4_pair(yx, at_plane((yx + p) % PLANE), p):
            c.start()

    def d4_on(src_yx, k):
        there = gq_out.at[:, core, :, cols_of(src_yx)]
        return (
            rc(there, there, d4c, k, partner),
            rc(gwb.at[core, src_yx], gwb.at[core, src_yx], gwc, k, partner),
        )

    loop(1, PLANE, d4_start)
    for c in d4_on(yx, 0):
        c.start()

    def d4_pass(p):
        src = (yx - p + PLANE) % PLANE
        for c in d4_pair(src, at_plane((yx + p) % PLANE), p):
            c.wait_recv()
        for c in d4_on(src, p):
            c.start()

    loop(1, PLANE, d4_pass)

    def d4_came(p):
        src = (yx - p + PLANE) % PLANE
        there = gq_out.at[:, 1 - core, :, cols_of(src)]
        rc(there, there, d4c, p, partner).wait_recv()
        rc(gwb.at[1 - core, src], gwb.at[1 - core, src], gwc, p, partner).wait_recv()

    loop(0, PLANE, d4_came)

    table = jnp.transpose(gwb[:, :, 0, :].reshape(2 * PLANE, LANES))
    for g in range(GROUPS):
        for c in range(2):
            gw_out[g, c] = table[g * HALF:(g + 1) * HALF, c * PLANE:(c + 1) * PLANE]

    for r in range(1, GROUPS):
        kl_came(r).wait_recv()
        gk_came(r).wait_recv()

    for r in range(1, GROUPS):
        for c in q_send(r):
            c.wait_send()
        att_send(r).wait_send()
        kl_send(r).wait_send()
        gk_send(r).wait_send()
        gk_share(r).wait_send()
        st_send2(r).wait_send()
    for r in range(GROUPS):
        g_send(r).wait_send()
        for other in range(2):
            if r or other:
                d3_send(r, other).wait_send()

    def drain(p):
        q_plane(p).wait_send()
        d2_send(p).wait_send()
        for c in d4_pair(yx, at_plane((yx + p) % PLANE), p):
            c.wait_send()

    loop(1, PLANE, drain)

    def drain2(p):
        q_core(p).wait_send()
        src = (yx - p + PLANE) % PLANE
        for c in d4_on(src, p):
            c.wait_send()

    loop(0, PLANE, drain2)


def local(query_mla, key_mla, lse, query_index, key_index, head_weight, query_pos, key_block):
    lse_rows = (lse.T * LOG2E).reshape(PAIRS, 2, 256)
    wpack = head_weight.T.reshape(PLANE, GROUPS, ROWS).transpose(1, 0, 2).reshape(GROUPS, 8, LANES)
    pos = query_pos.reshape(GROUPS, 1, ROWS)
    pos = jnp.concatenate([pos, pos], axis=2)
    hbm = pl.BlockSpec(memory_space=pltpu.HBM)
    vmem = pl.BlockSpec(memory_space=pltpu.VMEM)
    dma = pltpu.SemaphoreType.DMA
    V = pltpu.VMEM
    kl, gq, gw, gk = pl.pallas_call(
        body,
        out_shape=(
            jax.ShapeDtypeStruct((GROUPS, 8, LANES), F32),
            jax.ShapeDtypeStruct((GROUPS, 2, HALF, PLANE * LANES), BF16),
            jax.ShapeDtypeStruct((GROUPS, 2, HALF, PLANE), F32),
            jax.ShapeDtypeStruct((GROUPS, LANES, LANES), BF16),
        ),
        in_specs=[hbm, hbm, vmem, hbm, vmem, vmem, vmem, vmem, pl.BlockSpec(memory_space=pltpu.SMEM)],
        out_specs=(vmem, vmem, vmem, vmem),
        scratch_shapes=[
            V((256, 6144), BF16), V((KEYS, 6144), BF16), V((KEYS, 256), F32),
            V((GROUPS, 256, LANES), F32), V((GROUPS, 256, LANES), BF16), V((GROUPS, 256, LANES), BF16),
            V((GROUPS, PLANE, 2, HALF, LANES), BF16), V((GROUPS, 8, LANES), F32),
            V((KEYS, 64 * ROWS), BF16), V((64 * ROWS, LANES), BF16), V((KEYS, LANES), F32),
            V((KEYS, LANES), F32), V((KEYS, LANES), F32),
            V((8, LANES), F32), V((PLANE, 8, LANES), F32), V((4, 8, LANES), F32),
            V((2, GROUPS, PLANE, HALF, LANES), BF16), V((GROUPS, PLANE, HALF, LANES), BF16),
            V((PLANE, GROUPS, HALF, LANES), BF16), V((PLANE, GROUPS, HALF, LANES), BF16),
            V((GROUPS, HALF, LANES), BF16), V((8, HALF, LANES), BF16),
            V((GROUPS, HALF, LANES), BF16), V((GROUPS, HALF, LANES), F32),
            V((2, PLANE, 8, LANES), F32), V((GROUPS, LANES, LANES), BF16), V((GROUPS, LANES, LANES), BF16),
            dma((2, CHUNKS)), dma((PLANE + 1,)), dma((2, 4)), dma((2, 4)), dma((2, PLANE)), dma((2, PLANE)),
            dma((2, 4)), dma((2, PLANE)), dma((2, 4)), dma((2, 4)), dma((2, 4)), dma((2, PLANE)),
            dma((2, 8)), dma((2, PLANE)), dma((2, PLANE)), dma((2, PLANE)), dma((2, PLANE)),
            dma((2, 4)), dma((2, 4)),
        ],
        compiler_params=pltpu.CompilerParams(
            collective_id=0, has_side_effects=True, vmem_limit_bytes=60 * 1024 * 1024
        ),
    )(
        query_mla, key_mla, lse_rows, query_index.reshape(GROUPS, 2, HALF, PLANE * LANES), key_index,
        wpack, head_weight.reshape(GROUPS, 2, HALF, PLANE), pos, key_block,
    )
    return (
        kl[:, 0, :ROWS].reshape(256).astype(BF16),
        gq.reshape(256, PLANE * LANES),
        gw.reshape(256, PLANE).astype(BF16),
        gk.reshape(KEYS, LANES),
    )


def solution(mesh):
    return jax.shard_map(
        local,
        mesh=mesh,
        in_specs=(
            P(None, "head"), P("seq", "head"), P(None, "head"), P(None, "head"),
            P("seq", None), P(None, "head"), P(), P("seq"),
        ),
        out_specs=(P(), P(None, "head"), P(None, "head"), P("seq", None)),
        check_vma=False,
    )
```

```python
import functools
import math

import jax
import jax.numpy as jnp
from jax import lax
from jax.experimental import pallas as pl
from jax.experimental.pallas import tpu as pltpu
from jax.sharding import PartitionSpec as P

MESH = pl.DeviceIdType.MESH
F32 = jnp.float32
BF16 = jnp.bfloat16

GROUPS = 4
PLANE = 16
ROWS = 64
HALF = 32
KEYS = 512
PAIRS = 16
WIDE = 192
LANES = 128
CHUNKS = 8
CHUNK_PAIRS = PAIRS // CHUNKS
CHUNK = CHUNK_PAIRS * 2 * WIDE
NT = (((1,), (1,)), ((), ()))
TN = (((0,), (0,)), ((), ()))
NN = (((1,), (0,)), ((), ()))
LOG2E = math.log2(math.e)


def dot(a, b, dims):
    return lax.dot_general(a, b, dims, preferred_element_type=F32)


def body(
    qm, km, lse_h, qi, ki_h, hw_h, qpos_h, kb,
    kl_out, gq_out, gw_out, gk_out,
    qbuf, kbuf, acc, blk, att_s, att_r, qall, wall, dots, wq, lacc, ebuf, abuf,
    st_mine, st_all, st_two, gb, part, g2, r2, g3, r3, qfin, prod, gwb, gk_s, gk_r,
    lse, wpack, hw, klb, lse_t, ki, hw_t, qpos,
    small, ld, qloc, qz, wz, qx, qc, at, st1, st2, kls, d1, d2, d3, d4, d4c, gws, gwc, gks, gkt,
):
    h = lax.axis_index("head")
    s = lax.axis_index("seq")
    core = s % 2
    zh = (s // 2) % 2
    yx = s // 4

    def at_plane(p):
        return (h, p * 4 + zh * 2 + core)

    def at_head(g):
        return (g, s)

    partner = (h, yx * 4 + zh * 2 + (1 - core))

    def rc(src, dst, sems, k, dev):
        return pltpu.make_async_remote_copy(
            src_ref=src, dst_ref=dst, send_sem=sems.at[0, k], recv_sem=sems.at[1, k],
            device_id=dev, device_id_type=MESH,
        )

    def loop(lo, hi, f):
        def step(k, carry):
            f(k)
            return carry

        lax.fori_loop(lo, hi, step, 0)

    def group_of(r):
        return (h + r) % GROUPS

    smalls = [
        pltpu.make_async_copy(src, dst, small.at[k])
        for k, (src, dst) in enumerate(
            ((lse_h, lse_t), (hw_h, hw_t), (ki_h, ki), (qpos_h, qpos))
        )
    ]
    for c in smalls:
        c.start()

    bar = pltpu.get_barrier_semaphore()

    def hello(dev):
        pl.semaphore_signal(bar, inc=1, device_id=dev, device_id_type=MESH)

    loop(1, PLANE, lambda p: hello(at_plane((yx + p) % PLANE)))
    for r in range(GROUPS):
        if r:
            hello(at_head((h + r) % GROUPS))
        hello(((h + r) % GROUPS, yx * 4 + (1 - zh) * 2 + core))
    hello(partner)
    hello((h, yx * 4 + (1 - zh) * 2 + (1 - core)))

    def chunk_copies(k):
        cols = pl.ds(pl.multiple_of(k * CHUNK, LANES), CHUNK)
        return (
            pltpu.make_async_copy(qm.at[:, cols], qbuf.at[:, cols], ld.at[0, k]),
            pltpu.make_async_copy(km.at[:, cols], kbuf.at[:, cols], ld.at[1, k]),
        )

    def start_chunk(k):
        for c in chunk_copies(k):
            c.start()

    loop(0, CHUNKS, start_chunk)

    def own_head(k):
        cols = pl.ds(pl.multiple_of(k * LANES, LANES), LANES)
        return pltpu.make_async_copy(qi.at[h, :, :, cols], qall.at[0, k], qloc.at[k])

    loop(0, PLANE, lambda k: own_head(k).start())
    my_cols = pl.ds(pl.multiple_of(yx * LANES, LANES), LANES)
    fin_copy = pltpu.make_async_copy(qi.at[:, core, :, my_cols], qfin, qloc.at[PLANE])
    fin_copy.start()

    for c in smalls:
        c.wait()
    for p in range(PAIRS):
        lse[p] = lse_t[2 * p:2 * p + 2, :] * LOG2E
    left8 = lax.broadcasted_iota(jnp.int32, (8, LANES), 1) < ROWS
    for t in range(2):
        both = hw_t[:, t * LANES:(t + 1) * LANES]
        even = jnp.concatenate([both[2 * p:2 * p + 1] for p in range(8)], axis=0)
        odd = jnp.concatenate([both[2 * p + 1:2 * p + 2] for p in range(8)], axis=0)
        wpack[2 * t] = jnp.where(left8, even, pltpu.roll(odd, ROWS, 1))
        wpack[2 * t + 1] = jnp.where(left8, pltpu.roll(even, ROWS, 1), odd)

    acc[...] = jnp.zeros_like(acc)
    scale = WIDE ** -0.5 * LOG2E

    def attend(k):
        for c in chunk_copies(k):
            c.wait()
        for j in range(CHUNK_PAIRS):
            pair = k * CHUNK_PAIRS + j
            base = pair * (2 * WIDE)
            lo = pl.ds(pl.multiple_of(base, LANES), 2 * LANES)
            hi = pl.ds(pl.multiple_of(base + LANES, LANES), 2 * LANES)
            lane = lax.broadcasted_iota(jnp.int32, (256, 2 * LANES), 1)
            q_a = jnp.where(lane < WIDE, qbuf[:, lo], 0).astype(BF16)
            q_b = jnp.where(lane >= 2 * LANES - WIDE, qbuf[:, hi], 0).astype(BF16)
            ls = lse[pair]
            s_a = dot(kbuf[:, lo], q_a, NT)
            s_b = dot(kbuf[:, hi], q_b, NT)
            acc[...] += jnp.exp2(s_a * scale - ls[0:1, :]) + jnp.exp2(s_b * scale - ls[1:2, :])

    loop(0, 4, attend)

    pl.semaphore_wait(bar, PLANE - 1 + GROUPS - 1 + GROUPS + 2)

    wall[0] = wpack[h]

    def q_send(r):
        g = (h + r) % GROUPS
        slot = (GROUPS - r) % GROUPS
        mine = qi.at[g, core, :, my_cols]
        return (
            rc(mine, qall.at[slot, yx, core], qz, r, at_head(g)),
            rc(wpack.at[g], wall.at[slot], wz, r, at_head(g)),
        )

    def q_came(r):
        g = (h + r) % GROUPS
        slot = (GROUPS - r) % GROUPS
        return (
            rc(qall.at[slot, yx, core], qall.at[slot, yx, core], qz, r, at_head(g)),
            rc(wall.at[slot], wall.at[slot], wz, r, at_head(g)),
        )

    for r in range(1, GROUPS):
        for c in q_send(r):
            c.start()

    loop(4, CHUNKS, attend)

    left = lax.broadcasted_iota(jnp.int32, (256, LANES), 1) < ROWS

    for t in range(2):
        x = acc[0:256, t * LANES:(t + 1) * LANES]
        y = acc[256:512, t * LANES:(t + 1) * LANES]
        b0 = jnp.where(left, x, pltpu.roll(y, ROWS, 1))
        b1 = jnp.where(left, pltpu.roll(x, ROWS, 1), y)
        blk[2 * t] = b0
        blk[2 * t + 1] = b1
        att_s[2 * t] = b0.astype(BF16)
        att_s[2 * t + 1] = b1.astype(BF16)

    for r in range(1, GROUPS):
        for c in q_came(r):
            c.wait_recv()

    def q_plane(p):
        return rc(
            qall.at[1:GROUPS, yx, core], qall.at[1:GROUPS, yx, core], qx, p,
            at_plane((yx + p) % PLANE),
        )

    def q_core(p):
        src = (yx - p + PLANE) % PLANE
        return rc(qall.at[1:GROUPS, src, core], qall.at[1:GROUPS, src, core], qc, p, partner)

    def q_plane_came(p):
        src = (yx - p + PLANE) % PLANE
        return rc(
            qall.at[1:GROUPS, src, core], qall.at[1:GROUPS, src, core], qx, p,
            at_plane((yx + p) % PLANE),
        )

    def q_core_came(p):
        src = (yx - p + PLANE) % PLANE
        there = qall.at[1:GROUPS, src, 1 - core]
        return rc(there, there, qc, p, partner)

    loop(1, PLANE, lambda p: q_plane(p).start())
    q_core(0).start()

    def att_send(r):
        g = (h + r) % GROUPS
        return rc(att_s.at[g], att_r.at[r], at, r, at_head(g))

    for r in (2, 1, 3):
        att_send(r).start()

    lacc[...] = jnp.zeros_like(lacc)

    def index_quad(r, q):
        qq = qall[r, pl.ds(4 * q, 4)].reshape(4 * ROWS, LANES)
        d = dot(ki[...], qq, NT)
        cols = pl.ds(pl.multiple_of((r * 4 + q) * 2 * LANES, LANES), 2 * LANES)
        dots[:, cols] = d.astype(BF16)
        w0 = wall[r, pl.ds(2 * q, 1), :]
        w1 = wall[r, pl.ds(2 * q + 1, 1), :]
        lacc[...] += w0 * jnp.maximum(d[:, :LANES], 0.0) + w1 * jnp.maximum(d[:, LANES:], 0.0)

    loop(0, PLANE, lambda k: own_head(k).wait())
    for q in range(4):
        index_quad(0, q)

    def pass_on(p):
        q_plane_came(p).wait_recv()
        q_core(p).start()

    loop(1, PLANE, pass_on)
    loop(0, PLANE, lambda p: q_core_came(p).wait_recv())

    for r in range(1, GROUPS):
        for q in range(4):
            index_quad(r, q)

    for r in range(1, GROUPS):
        rc(att_r.at[r], att_r.at[r], at, r, at_head((h + r) % GROUPS)).wait_recv()
    a = blk[h] + att_r[1].astype(F32) + att_r[2].astype(F32) + att_r[3].astype(F32)
    ra = pltpu.roll(a, ROWS, 1)
    first = jnp.where(left, a, ra)
    second = jnp.where(left, ra, a)
    base = kb[0] * KEYS
    left1 = lax.broadcasted_iota(jnp.int32, (1, LANES), 1) < ROWS
    limit = jnp.where(h < 2, qpos[:, :LANES], qpos[:, LANES:])
    turned = pltpu.roll(limit, ROWS, 1)
    limit = jnp.where(left1 == (h % 2 == 0), limit, turned)
    for i, half in enumerate((first, second)):
        row = lax.broadcasted_iota(jnp.int32, (256, LANES), 0) + (base + i * 256)
        ok = row <= limit
        abuf[i * 256:(i + 1) * 256] = jnp.where(ok, half, 0.0)
        lg = lacc[i * 256:(i + 1) * 256]
        lg = lg + pltpu.roll(lg, ROWS, 1)
        lacc[i * 256:(i + 1) * 256] = jnp.where(ok, lg, -1e30)
    lm = lacc[...]
    peak = jnp.max(lm, axis=0, keepdims=True)
    rowid = lax.broadcasted_iota(jnp.int32, (KEYS, LANES), 0) + base
    ok = rowid <= limit
    rel = lm - peak
    e = jnp.where(ok, jnp.exp(rel), 0.0)
    ebuf[...] = e
    av = abuf[...]
    norm = jnp.sum(e, axis=0, keepdims=True)
    total = jnp.sum(av, axis=0, keepdims=True)
    cross = jnp.sum(
        jnp.where(ok, av * (jnp.log(jnp.where(ok, av, 1.0)) - rel), 0.0), axis=0, keepdims=True
    )
    pad = jnp.zeros((4, LANES), F32)
    tile = jnp.concatenate([peak, norm, total, cross, pad], axis=0)
    st_mine[...] = tile
    st_all[yx] = tile

    def st_send(p):
        return rc(st_mine, st_all.at[yx], st1, p, at_plane((yx + p) % PLANE))

    def st_came(p):
        src = (yx - p + PLANE) % PLANE
        return rc(st_all.at[src], st_all.at[src], st1, p, at_plane((yx + p) % PLANE))

    loop(1, PLANE, lambda p: st_send(p).start())

    hw[...] = jnp.transpose(hw_t[...]).reshape(GROUPS, 2, HALF, PLANE)

    wcol = jnp.transpose(wall[...].reshape(4 * 8, LANES))
    for r in range(GROUPS):
        for p in range(8):
            qq = qall[r, 2 * p:2 * p + 2].reshape(2 * ROWS, LANES).astype(F32)
            k = r * 8 + p
            wq[k * LANES:(k + 1) * LANES] = (qq * wcol[:, k:k + 1]).astype(BF16)

    def merge(t):
        pk = jnp.max(t[:, 0, :], axis=0, keepdims=True)
        nm = jnp.sum(t[:, 1, :] * jnp.exp(t[:, 0, :] - pk), axis=0, keepdims=True)
        tt = jnp.sum(t[:, 2, :], axis=0, keepdims=True)
        cr = jnp.sum(t[:, 3, :] + t[:, 2, :] * (pk - t[:, 0, :]), axis=0, keepdims=True)
        return pk, nm, tt, cr

    loop(1, PLANE, lambda p: st_came(p).wait_recv())
    tile2 = jnp.concatenate([*merge(st_all[...]), pad], axis=0)
    loop(1, PLANE, lambda p: st_send(p).wait_send())
    st_mine[...] = tile2
    st_two[0] = tile2

    def st_send2(k):
        dev = (h, yx * 4 + ((zh + k // 2) % 2) * 2 + (core + k % 2) % 2)
        return rc(st_mine, st_two.at[k], st2, k, dev)

    for k in (2, 3, 1):
        st_send2(k).start()
    for k in (1, 2, 3):
        st_send2(k).wait_recv()
    peak_g, norm_g, total_g, cross_g = merge(st_two[...])
    inv_t = 1.0 / total_g
    kl = cross_g * inv_t - jnp.log(total_g) + jnp.log(norm_g)
    klb[h] = jnp.broadcast_to(kl, (8, LANES))

    def kl_send(r):
        return rc(klb.at[h], klb.at[h], kls, r, at_head((h + r) % GROUPS))

    def kl_came(r):
        src = (h - r + GROUPS) % GROUPS
        return rc(klb.at[src], klb.at[src], kls, r, at_head((h + r) % GROUPS))

    for r in range(1, GROUPS):
        kl_send(r).start()

    grow = jnp.exp(peak - peak_g) / norm_g
    dl = (ebuf[...] * grow - abuf[...] * inv_t).astype(BF16)
    dl2 = jnp.concatenate([dl, dl], axis=1)
    zero = jnp.zeros_like(dl2)

    def g_send(r):
        return rc(gb.at[1 - core, r], part.at[r], d1, r, partner)

    for r in range(GROUPS):
        for q in range(4):
            lo = (r * 4 + q) * 2 * LANES
            g = jnp.where(dots[:, lo:lo + 2 * LANES] > 0, dl2, zero)
            dots[:, lo:lo + 2 * LANES] = g
            big = dot(g, ki[...], TN).astype(BF16).reshape(4, 2, HALF, LANES)
            gb[0, r, 4 * q:4 * q + 4] = big[:, 0]
            gb[1, r, 4 * q:4 * q + 4] = big[:, 1]
        g_send(r).start()

    for r in range(GROUPS):
        g_send(r).wait_recv()
        g2[:, r] = (gb[core, r].astype(F32) + part[r].astype(F32)).astype(BF16)

    def d2_send(p):
        to = (yx + p) % PLANE
        return rc(g2.at[to], r2.at[p], d2, p, at_plane(to))

    loop(1, PLANE, lambda p: d2_send(p).start())

    gk = jnp.zeros((KEYS, LANES), F32)
    for r in range(GROUPS):
        gk += dot(dots[:, r * 1024:(r + 1) * 1024], wq[r * 1024:(r + 1) * 1024], NN)
    gk_s[...] = gk.astype(BF16).reshape(4, LANES, LANES)

    def gk_send(r):
        g = (h + r) % GROUPS
        return rc(gk_s.at[g], gk_r.at[r], gks, r, at_head(g))

    for r in (2, 1, 3):
        gk_send(r).start()

    loop(1, PLANE, lambda p: d2_send(p).wait_recv())
    tot = g2[yx].astype(F32)
    for p in range(1, PLANE):
        tot += r2[p].astype(F32)
    g3[...] = tot.astype(BF16)

    def d3_send(r, other):
        k = 2 * r + other
        dev = ((h + r) % GROUPS, yx * 4 + ((zh + other) % 2) * 2 + core)
        return rc(g3.at[r], r3.at[k], d3, k, dev)

    for r, other in ((0, 1), (1, 1), (2, 1), (3, 1), (2, 0), (1, 0), (3, 0)):
        d3_send(r, other).start()

    for r in range(1, GROUPS):
        gk_send(r).wait_recv()
    mine = gk_s[h].astype(F32)
    for r in range(1, GROUPS):
        mine += gk_r[r].astype(F32)
    gk_out[h] = mine.astype(BF16)

    def gk_share(r):
        return rc(gk_out.at[h], gk_out.at[h], gkt, r, at_head((h + r) % GROUPS))

    def gk_came(r):
        src = (h - r + GROUPS) % GROUPS
        return rc(gk_out.at[src], gk_out.at[src], gkt, r, at_head((h + r) % GROUPS))

    for r in (2, 1, 3):
        gk_share(r).start()

    fin_copy.wait()
    for r, other in ((2, 0), (1, 0), (3, 0), (0, 1), (1, 1), (2, 1), (3, 1)):
        d3_send(r, other).wait_recv()
    onehot = lax.broadcasted_iota(jnp.int32, (HALF, PLANE), 1) == yx
    for r in range(GROUPS):
        g = (h - r + GROUPS) % GROUPS
        near = g3[0] if r == 0 else r3[2 * r]
        full = near.astype(F32) + r3[2 * r + 1].astype(F32)
        w = jnp.sum(jnp.where(onehot, hw[g, core], 0.0), axis=1, keepdims=True)
        gq_out[g, core, :, my_cols] = (full * w).astype(BF16)
        prod[g] = full * qfin[g].astype(F32)
    gw_row = jnp.sum(jnp.transpose(prod[...].reshape(LANES, LANES)), axis=0, keepdims=True)
    gwb[core, yx] = jnp.broadcast_to(gw_row, (8, LANES))

    def cols_of(p):
        return pl.ds(pl.multiple_of(p * LANES, LANES), LANES)

    def d4_pair(src_yx, dev, k):
        there = gq_out.at[:, core, :, cols_of(src_yx)]
        return rc(there, there, d4, k, dev), rc(gwb.at[core, src_yx], gwb.at[core, src_yx], gws, k, dev)

    def d4_start(p):
        for c in d4_pair(yx, at_plane((yx + p) % PLANE), p):
            c.start()

    def d4_on(src_yx, k):
        there = gq_out.at[:, core, :, cols_of(src_yx)]
        return (
            rc(there, there, d4c, k, partner),
            rc(gwb.at[core, src_yx], gwb.at[core, src_yx], gwc, k, partner),
        )

    loop(1, PLANE, d4_start)
    for c in d4_on(yx, 0):
        c.start()

    def d4_pass(p):
        src = (yx - p + PLANE) % PLANE
        for c in d4_pair(src, at_plane((yx + p) % PLANE), p):
            c.wait_recv()
        for c in d4_on(src, p):
            c.start()

    loop(1, PLANE, d4_pass)

    def d4_came(p):
        src = (yx - p + PLANE) % PLANE
        there = gq_out.at[:, 1 - core, :, cols_of(src)]
        rc(there, there, d4c, p, partner).wait_recv()
        rc(gwb.at[1 - core, src], gwb.at[1 - core, src], gwc, p, partner).wait_recv()

    loop(0, PLANE, d4_came)

    t0, t1 = gwb[0, :, 0, :], gwb[1, :, 0, :]
    lane16 = lax.broadcasted_iota(jnp.int32, (PLANE, LANES), 1)
    for t in range(2):
        def back(v, n):
            return pltpu.roll(v, (n - t * ROWS) % LANES, 1)

        lo = jnp.where(lane16 < HALF, back(t0, 0), back(t1, HALF))
        up = jnp.where(lane16 < 3 * HALF, back(t0, HALF), back(t1, ROWS))
        gw_out[:, t * LANES:(t + 1) * LANES] = jnp.where(lane16 < ROWS, lo, up).astype(BF16)

    for r in range(1, GROUPS):
        kl_came(r).wait_recv()
        gk_came(r).wait_recv()
    for t in range(2):
        pair = jnp.where(left1, klb[2 * t, 0:1, :], klb[2 * t + 1, 0:1, :])
        kl_out[:, t * LANES:(t + 1) * LANES] = pair.astype(BF16)

    for r in range(1, GROUPS):
        for c in q_send(r):
            c.wait_send()
        att_send(r).wait_send()
        kl_send(r).wait_send()
        gk_send(r).wait_send()
        gk_share(r).wait_send()
        st_send2(r).wait_send()
    for r in range(GROUPS):
        g_send(r).wait_send()
        for other in range(2):
            if r or other:
                d3_send(r, other).wait_send()

    def drain(p):
        q_plane(p).wait_send()
        d2_send(p).wait_send()
        for c in d4_pair(yx, at_plane((yx + p) % PLANE), p):
            c.wait_send()

    loop(1, PLANE, drain)

    def drain2(p):
        q_core(p).wait_send()
        src = (yx - p + PLANE) % PLANE
        for c in d4_on(src, p):
            c.wait_send()

    loop(0, PLANE, drain2)


def finish(a, b, c, d, a_out, b_out, c_out, d_out, sem):
    copies = [
        pltpu.make_async_copy(src, dst, sem.at[k])
        for k, (src, dst) in enumerate(((b, b_out), (d, d_out), (c, c_out), (a, a_out)))
    ]
    for x in copies:
        x.start()
    for x in copies:
        x.wait()


def local(query_mla, key_mla, lse, query_index, key_index, head_weight, query_pos, key_block):
    hbm = pl.BlockSpec(memory_space=pltpu.HBM)
    vmem = pl.BlockSpec(memory_space=pltpu.VMEM)
    dma = pltpu.SemaphoreType.DMA
    V = pltpu.VMEM
    kl, gq, gw, gk = pl.pallas_call(
        body,
        out_shape=(
            jax.ShapeDtypeStruct((1, 256), BF16),
            jax.ShapeDtypeStruct((GROUPS, 2, HALF, PLANE * LANES), BF16),
            jax.ShapeDtypeStruct((PLANE, 256), BF16),
            jax.ShapeDtypeStruct((GROUPS, LANES, LANES), BF16),
        ),
        in_specs=[hbm] * 7 + [pl.BlockSpec(memory_space=pltpu.SMEM)],
        out_specs=(vmem, vmem, vmem, vmem),
        scratch_shapes=[
            V((256, 6144), BF16), V((KEYS, 6144), BF16), V((KEYS, 256), F32),
            V((GROUPS, 256, LANES), F32), V((GROUPS, 256, LANES), BF16), V((GROUPS, 256, LANES), BF16),
            V((GROUPS, PLANE, 2, HALF, LANES), BF16), V((GROUPS, 8, LANES), F32),
            V((KEYS, 64 * ROWS), BF16), V((64 * ROWS, LANES), BF16), V((KEYS, LANES), F32),
            V((KEYS, LANES), F32), V((KEYS, LANES), F32),
            V((8, LANES), F32), V((PLANE, 8, LANES), F32), V((4, 8, LANES), F32),
            V((2, GROUPS, PLANE, HALF, LANES), BF16), V((GROUPS, PLANE, HALF, LANES), BF16),
            V((PLANE, GROUPS, HALF, LANES), BF16), V((PLANE, GROUPS, HALF, LANES), BF16),
            V((GROUPS, HALF, LANES), BF16), V((8, HALF, LANES), BF16),
            V((GROUPS, HALF, LANES), BF16), V((GROUPS, HALF, LANES), F32),
            V((2, PLANE, 8, LANES), F32), V((GROUPS, LANES, LANES), BF16), V((GROUPS, LANES, LANES), BF16),
            V((PAIRS, 2, 256), F32), V((GROUPS, 8, LANES), F32), V((GROUPS, 2, HALF, PLANE), F32), V((GROUPS, 8, LANES), F32),
            V((32, 256), F32), V((KEYS, LANES), BF16), V((PLANE, 256), F32), V((1, 256), jnp.int32),
            dma((4,)), dma((2, CHUNKS)), dma((PLANE + 1,)), dma((2, 4)), dma((2, 4)), dma((2, PLANE)), dma((2, PLANE)),
            dma((2, 4)), dma((2, PLANE)), dma((2, 4)), dma((2, 4)), dma((2, 4)), dma((2, PLANE)),
            dma((2, 8)), dma((2, PLANE)), dma((2, PLANE)), dma((2, PLANE)), dma((2, PLANE)),
            dma((2, 4)), dma((2, 4)),
        ],
        compiler_params=pltpu.CompilerParams(
            collective_id=0, has_side_effects=True, vmem_limit_bytes=50 * 1024 * 1024
        ),
    )(*(pltpu.with_memory_space_constraint(x, pltpu.HBM) for x in (
        query_mla, key_mla, lse.T, query_index.reshape(GROUPS, 2, HALF, PLANE * LANES), key_index,
        head_weight.T, query_pos.reshape(1, 256),
    )), key_block)
    kl, gq, gw, gk = pl.pallas_call(
        finish,
        out_shape=(
            jax.ShapeDtypeStruct((1, 256), BF16),
            jax.ShapeDtypeStruct((GROUPS, 2, HALF, PLANE * LANES), BF16),
            jax.ShapeDtypeStruct((PLANE, 256), BF16),
            jax.ShapeDtypeStruct((GROUPS, LANES, LANES), BF16),
        ),
        in_specs=[vmem] * 4,
        out_specs=[hbm] * 4,
        scratch_shapes=[dma((4,))],
        compiler_params=pltpu.CompilerParams(vmem_limit_bytes=1024 * 1024),
    )(kl, gq, gw, gk)
    return kl.reshape(256), gq.reshape(256, PLANE * LANES), gw.T, gk.reshape(KEYS, LANES)


def solution(mesh):
    return jax.shard_map(
        local,
        mesh=mesh,
        in_specs=(
            P(None, "head"), P("seq", "head"), P(None, "head"), P(None, "head"),
            P("seq", None), P(None, "head"), P(), P("seq"),
        ),
        out_specs=(P(), P(None, "head"), P(None, "head"), P("seq", None)),
        check_vma=False,
    )
```

```python
import functools
import math

import jax
import jax.numpy as jnp
from jax import lax
from jax.experimental import pallas as pl
from jax.experimental.pallas import tpu as pltpu
from jax.sharding import PartitionSpec as P

MESH = pl.DeviceIdType.MESH
F32 = jnp.float32
BF16 = jnp.bfloat16

GROUPS = 4
PLANE = 16
ROWS = 64
HALF = 32
KEYS = 512
PAIRS = 16
WIDE = 192
LANES = 128
CHUNKS = 8
CHUNK_PAIRS = PAIRS // CHUNKS
CHUNK = CHUNK_PAIRS * 2 * WIDE
NT = (((1,), (1,)), ((), ()))
TN = (((0,), (0,)), ((), ()))
NN = (((1,), (0,)), ((), ()))
ROW_ORDER = (2, 1, 3, 0)
FAR_FIRST = tuple((dy, dx) for dy in ROW_ORDER for dx in (2, 1, 3, 0) if dy or dx)
LOG2E = math.log2(math.e)


def dot(a, b, dims):
    return lax.dot_general(a, b, dims, preferred_element_type=F32)


def body(
    qm, km, lse_h, qi, ki_h, hw_h, qpos_h, kb,
    kl_out, gq_out, gw_out, gk_out,
    qbuf, kbuf, acc, blk, att_s, att_r, qall, wall, dots, wq, lacc, ebuf, abuf,
    st_all, st_two, gb, part, g2, r2, g3, r3, qfin, prod, gwb, gk_s, gk_r,
    lse, wpack, hw, klb, lse_t, ki, hw_t, qpos,
    small, ld, qloc, qz, wz, qx, qc, at, st1, st2, kls, d1, d2, d3, d4, d4c, gws, gks, gkt,
):
    h = lax.axis_index("head")
    s = lax.axis_index("seq")
    core = s % 2
    zh = (s // 2) % 2
    yx = s // 4
    gy = yx // 4
    gx = yx % 4

    def seat(dy, dx):
        return ((gy + dy) % 4) * 4 + (gx + dx) % 4

    def at_plane(dy, dx, other_core=0):
        c = (core + other_core) % 2
        return (h, seat(dy, dx) * 4 + zh * 2 + c)

    def at_head(r):
        return ((h + r) % GROUPS, s)

    partner = at_plane(0, 0, 1)

    def rc(src, dst, sems, dev, k=1):
        return pltpu.make_async_remote_copy(
            src_ref=src, dst_ref=dst, send_sem=sems.at[0], recv_sem=sems.at[k],
            device_id=dev, device_id_type=MESH,
        )

    def came(ref, sems, k=1):
        rc(ref, ref, sems, partner, k).wait_recv()

    sent = []

    def left_with(ref, sems):
        sent.append((ref, sems))

    bar = pltpu.get_barrier_semaphore()

    def hello(dev):
        pl.semaphore_signal(bar, inc=1, device_id=dev, device_id_type=MESH)

    for k in (1, 0):
        hello((h, yx * 4 + (1 - zh) * 2 + (core + k) % 2))
    for dy, dx in FAR_FIRST:
        hello(at_plane(dy, dx))
        hello(at_plane(dy, dx, 1))
    for r in (3, 2, 1):
        hello(at_head(r))
        hello(((h + r) % GROUPS, yx * 4 + (1 - zh) * 2 + core))
    hello(partner)
    smalls = [
        pltpu.make_async_copy(src, dst, small.at[k])
        for k, (src, dst) in enumerate(
            ((lse_h, lse_t), (hw_h, hw_t), (ki_h, ki), (qpos_h, qpos))
        )
    ]
    for c in smalls:
        c.start()

    def loop(lo, hi, f):
        def step(k, carry):
            f(k)
            return carry

        lax.fori_loop(lo, hi, step, 0)

    def chunk_copies(k):
        cols = pl.ds(pl.multiple_of(k * CHUNK, LANES), CHUNK)
        return (
            pltpu.make_async_copy(qm.at[:, cols], qbuf.at[:, cols], ld.at[0, k]),
            pltpu.make_async_copy(km.at[:, cols], kbuf.at[:, cols], ld.at[1, k]),
        )

    def start_chunk(k):
        for c in chunk_copies(k):
            c.start()

    loop(0, CHUNKS, start_chunk)

    def own_head(k):
        cols = pl.ds(pl.multiple_of(k * LANES, LANES), LANES)
        pltpu.make_async_copy(qi.at[h, :, :, cols], qall.at[0, k], qloc.at[0]).start()

    loop(0, PLANE, own_head)
    my_cols = pl.ds(pl.multiple_of(yx * LANES, LANES), LANES)
    fin_copy = pltpu.make_async_copy(qi.at[:, core, :, my_cols], qfin, qloc.at[1])
    fin_copy.start()

    for c in smalls:
        c.wait()
    for p in range(PAIRS):
        lse[p] = lse_t[2 * p:2 * p + 2, :] * LOG2E
    left8 = lax.broadcasted_iota(jnp.int32, (8, LANES), 1) < ROWS
    for t in range(2):
        both = hw_t[:, t * LANES:(t + 1) * LANES]
        even = jnp.concatenate([both[2 * p:2 * p + 1] for p in range(8)], axis=0)
        odd = jnp.concatenate([both[2 * p + 1:2 * p + 2] for p in range(8)], axis=0)
        wpack[2 * t] = jnp.where(left8, even, pltpu.roll(odd, ROWS, 1))
        wpack[2 * t + 1] = jnp.where(left8, pltpu.roll(even, ROWS, 1), odd)

    acc[...] = jnp.zeros_like(acc)
    scale = WIDE ** -0.5 * LOG2E

    def attend(k):
        for c in chunk_copies(k):
            c.wait()
        for j in range(CHUNK_PAIRS):
            pair = k * CHUNK_PAIRS + j
            base = pair * (2 * WIDE)
            lo = pl.ds(pl.multiple_of(base, LANES), 2 * LANES)
            hi = pl.ds(pl.multiple_of(base + LANES, LANES), 2 * LANES)
            lane = lax.broadcasted_iota(jnp.int32, (256, 2 * LANES), 1)
            q_a = jnp.where(lane < WIDE, qbuf[:, lo], 0).astype(BF16)
            q_b = jnp.where(lane >= 2 * LANES - WIDE, qbuf[:, hi], 0).astype(BF16)
            ls = lse[pair]
            s_a = dot(kbuf[:, lo], q_a, NT)
            s_b = dot(kbuf[:, hi], q_b, NT)
            acc[...] += jnp.exp2(s_a * scale - ls[0:1, :]) + jnp.exp2(s_b * scale - ls[1:2, :])

    loop(0, 4, attend)

    pl.semaphore_wait(bar, 2 + 2 * 15 + 6 + 1)
    wall[0] = wpack[h]
    for r in (3, 2, 1):
        g = (h + r) % GROUPS
        slot = GROUPS - r
        rc(qi.at[g, core, :, my_cols], qall.at[slot, yx, core], qz, at_head(r)).start()
        rc(wpack.at[g], wall.at[slot], wz, at_head(r)).start()
    left_with(qall.at[1:GROUPS, yx, core], qz)
    left_with(wall.at[1:GROUPS], wz)

    loop(4, CHUNKS, attend)

    left = lax.broadcasted_iota(jnp.int32, (256, LANES), 1) < ROWS

    for t in range(2):
        x = acc[0:256, t * LANES:(t + 1) * LANES]
        y = acc[256:512, t * LANES:(t + 1) * LANES]
        b0 = jnp.where(left, x, pltpu.roll(y, ROWS, 1))
        b1 = jnp.where(left, pltpu.roll(x, ROWS, 1), y)
        blk[2 * t] = b0
        blk[2 * t + 1] = b1
        att_s[2 * t] = b0.astype(BF16)
        att_s[2 * t + 1] = b1.astype(BF16)

    for r in (3, 2, 1):
        g = (h + r) % GROUPS
        rc(att_s.at[g], att_r.at[r], at, at_head(r)).start()
    left_with(att_s.at[1:GROUPS], at)

    came(qall.at[1:GROUPS, yx, core], qz)
    came(wall.at[1:GROUPS], wz)
    mine = qall.at[1:GROUPS, yx, core]
    for dy, dx in FAR_FIRST:
        rc(mine, mine, qx, at_plane(dy, dx), 1 + dy).start()
    left_with(qall.at[1:GROUPS, 1:PLANE, core], qx)

    lacc[...] = jnp.zeros_like(lacc)

    def index_quad(r, q):
        qq = qall[r, pl.ds(4 * q, 4)].reshape(4 * ROWS, LANES)
        d = dot(ki[...], qq, NT)
        cols = pl.ds(pl.multiple_of((r * 4 + q) * 2 * LANES, LANES), 2 * LANES)
        dots[:, cols] = d.astype(BF16)
        w0 = wall[r, pl.ds(2 * q, 1), :]
        w1 = wall[r, pl.ds(2 * q + 1, 1), :]
        lacc[...] += w0 * jnp.maximum(d[:, :LANES], 0.0) + w1 * jnp.maximum(d[:, LANES:], 0.0)

    pltpu.make_async_copy(qall.at[0], qall.at[0], qloc.at[0]).wait()
    for q in range(4):
        index_quad(0, q)

    def q_row(dy, c):
        return qall.at[1:GROUPS, pl.ds(((gy + 4 - dy) % 4) * 4, 4), c]

    def q_use(dy):
        came(q_row(dy, 1 - core), qc, 1 + dy)
        for r in range(1, GROUPS):
            index_quad(r, (gy + 4 - dy) % 4)

    for k, dy in enumerate(ROW_ORDER):
        came(q_row(dy, core) if dy else qall.at[1:GROUPS, 0:3, core], qx, 1 + dy)
        rc(q_row(dy, core), q_row(dy, core), qc, partner, 1 + dy).start()
        if k:
            q_use(ROW_ORDER[k - 1])
    q_use(ROW_ORDER[-1])
    left_with(qall.at[1:GROUPS, :, core], qc)

    came(att_r.at[1:GROUPS], at)
    a = blk[h] + att_r[1].astype(F32) + att_r[2].astype(F32) + att_r[3].astype(F32)
    ra = pltpu.roll(a, ROWS, 1)
    first = jnp.where(left, a, ra)
    second = jnp.where(left, ra, a)
    base = kb[0] * KEYS
    left1 = lax.broadcasted_iota(jnp.int32, (1, LANES), 1) < ROWS
    limit = jnp.where(h < 2, qpos[:, :LANES], qpos[:, LANES:])
    turned = pltpu.roll(limit, ROWS, 1)
    limit = jnp.where(left1 == (h % 2 == 0), limit, turned)
    for i, half in enumerate((first, second)):
        row = lax.broadcasted_iota(jnp.int32, (256, LANES), 0) + (base + i * 256)
        ok = row <= limit
        abuf[i * 256:(i + 1) * 256] = jnp.where(ok, half, 0.0)
        lg = lacc[i * 256:(i + 1) * 256]
        lg = lg + pltpu.roll(lg, ROWS, 1)
        lacc[i * 256:(i + 1) * 256] = jnp.where(ok, lg, -1e30)
    lm = lacc[...]
    peak = jnp.max(lm, axis=0, keepdims=True)
    rowid = lax.broadcasted_iota(jnp.int32, (KEYS, LANES), 0) + base
    ok = rowid <= limit
    rel = lm - peak
    e = jnp.where(ok, jnp.exp(rel), 0.0)
    ebuf[...] = e
    av = abuf[...]
    norm = jnp.sum(e, axis=0, keepdims=True)
    total = jnp.sum(av, axis=0, keepdims=True)
    cross = jnp.sum(
        jnp.where(ok, av * (jnp.log(jnp.where(ok, av, 1.0)) - rel), 0.0), axis=0, keepdims=True
    )
    tile = jnp.concatenate([peak, norm, total, cross], axis=0)
    my_seat = core * PLANE + yx
    st_all[my_seat] = tile

    mine = st_all.at[my_seat]
    for dy, dx in FAR_FIRST:
        rc(mine, mine, st1, at_plane(dy, dx, 1)).start()
        rc(mine, mine, st1, at_plane(dy, dx)).start()
    rc(mine, mine, st1, partner).start()
    left_with(st_all.at[1:], st1)

    hw[...] = jnp.transpose(hw_t[...]).reshape(GROUPS, 2, HALF, PLANE)

    wcol = jnp.transpose(wall[...].reshape(4 * 8, LANES))
    for r in range(GROUPS):
        for p in range(8):
            qq = qall[r, 2 * p:2 * p + 2].reshape(2 * ROWS, LANES).astype(F32)
            k = r * 8 + p
            wq[k * LANES:(k + 1) * LANES] = (qq * wcol[:, k:k + 1]).astype(BF16)

    def merge(t):
        pk = jnp.max(t[:, 0, :], axis=0, keepdims=True)
        nm = jnp.sum(t[:, 1, :] * jnp.exp(t[:, 0, :] - pk), axis=0, keepdims=True)
        tt = jnp.sum(t[:, 2, :], axis=0, keepdims=True)
        cr = jnp.sum(t[:, 3, :] + t[:, 2, :] * (pk - t[:, 0, :]), axis=0, keepdims=True)
        return pk, nm, tt, cr

    came(st_all.at[1:], st1)
    st_two[0] = jnp.concatenate(merge(st_all[...]), axis=0)
    rc(st_two.at[0], st_two.at[1], st2, (h, yx * 4 + (1 - zh) * 2 + core)).start()
    left_with(st_two.at[0], st2)
    came(st_two.at[1], st2)
    peak_g, norm_g, total_g, cross_g = merge(st_two[...])
    inv_t = 1.0 / total_g
    kl = cross_g * inv_t - jnp.log(total_g) + jnp.log(norm_g)
    klb[h] = jnp.broadcast_to(kl, (8, LANES))

    for r in range(1, GROUPS):
        rc(klb.at[h], klb.at[h], kls, at_head(r)).start()
    left_with(klb.at[1:GROUPS], kls)

    grow = jnp.exp(peak - peak_g) / norm_g
    dl = (ebuf[...] * grow - abuf[...] * inv_t).astype(BF16)
    dl2 = jnp.concatenate([dl, dl], axis=1)
    zero = jnp.zeros_like(dl2)

    def pair_sum(r):
        came(part.at[r], d1, 1 + r)
        g2[r] = (gb[core, r].astype(F32) + part[r].astype(F32)).astype(BF16)
        for k, (dy, dx) in enumerate(FAR_FIRST):
            rc(g2.at[r, seat(dy, dx)], r2.at[r, k], d2, at_plane(dy, dx), 1 + r).start()

    for r in range(GROUPS):
        for q in range(4):
            lo = (r * 4 + q) * 2 * LANES
            g = jnp.where(dots[:, lo:lo + 2 * LANES] > 0, dl2, zero)
            dots[:, lo:lo + 2 * LANES] = g
            big = dot(g, ki[...], TN).astype(BF16).reshape(4, 2, HALF, LANES)
            gb[0, r, 4 * q:4 * q + 4] = big[:, 0]
            gb[1, r, 4 * q:4 * q + 4] = big[:, 1]
        rc(gb.at[1 - core, r], part.at[r], d1, partner, 1 + r).start()
        if r > 1:
            pair_sum(r - 2)
    left_with(gb.at[0], d1)

    gk = jnp.zeros((KEYS, LANES), F32)
    for r in range(GROUPS):
        gk += dot(dots[:, r * 1024:(r + 1) * 1024], wq[r * 1024:(r + 1) * 1024], NN)
        if r < 2:
            pair_sum(r + 2)
    left_with(r2.at[:, 0:15], d2)
    gk_s[...] = gk.astype(BF16).reshape(4, LANES, LANES)
    for r in (3, 2, 1):
        rc(gk_s.at[(h + r) % GROUPS], gk_r.at[r], gks, at_head(r)).start()
    left_with(gk_s.at[1:GROUPS], gks)

    for r in range(GROUPS):
        came(r2.at[r, 0:15], d2, 1 + r)
        tot = g2[r, yx].astype(F32)
        for p in range(PLANE - 1):
            tot += r2[r, p].astype(F32)
        g3[r] = tot.astype(BF16)
        for other in (1, 0):
            if r or other:
                dev = ((h + r) % GROUPS, yx * 4 + ((zh + other) % 2) * 2 + core)
                rc(g3.at[r], r3.at[2 * r + other], d3, dev).start()
    left_with(r3.at[1:], d3)

    came(gk_r.at[1:GROUPS], gks)
    mine = gk_s[h].astype(F32)
    for r in range(1, GROUPS):
        mine += gk_r[r].astype(F32)
    gk_out[h] = mine.astype(BF16)
    for r in (3, 2, 1):
        rc(gk_out.at[h], gk_out.at[h], gkt, at_head(r)).start()
    left_with(gk_out.at[1:GROUPS], gkt)

    fin_copy.wait()
    came(r3.at[1:], d3)
    onehot = lax.broadcasted_iota(jnp.int32, (HALF, PLANE), 1) == yx
    for r in range(GROUPS):
        g = (h - r + GROUPS) % GROUPS
        near = g3[0] if r == 0 else r3[2 * r]
        full = near.astype(F32) + r3[2 * r + 1].astype(F32)
        w = jnp.sum(jnp.where(onehot, hw[g, core], 0.0), axis=1, keepdims=True)
        gq_out[g, core, :, my_cols] = (full * w).astype(BF16)
        prod[g] = full * qfin[g].astype(F32)

    mine = gq_out.at[:, core, :, my_cols]
    for dy, dx in FAR_FIRST:
        rc(mine, mine, d4, at_plane(dy, dx), 1 + dy).start()
    left_with(gq_out.at[:, core, :, LANES:], d4)

    gw_row = jnp.sum(jnp.transpose(prod[...].reshape(LANES, LANES)), axis=0, keepdims=True)
    gwb[my_seat] = gw_row
    mine = gwb.at[my_seat]
    for dy, dx in FAR_FIRST:
        rc(mine, mine, gws, at_plane(dy, dx, 1)).start()
        rc(mine, mine, gws, at_plane(dy, dx)).start()
    rc(mine, mine, gws, partner).start()
    left_with(gwb.at[1:], gws)

    def row_cols(dy):
        return pl.ds(pl.multiple_of(((gy + 4 - dy) % 4) * 4 * LANES, LANES), 4 * LANES)

    for dy in ROW_ORDER:
        row = gq_out.at[:, core, :, row_cols(dy)]
        came(row if dy else gq_out.at[:, core, :, 0:3 * LANES], d4, 1 + dy)
        rc(row, row, d4c, partner).start()
    left_with(gq_out.at[:, core], d4c)
    came(gwb.at[1:], gws)
    came(klb.at[1:GROUPS], kls)
    t0, t1 = gwb[0:PLANE, 0, :], gwb[PLANE:, 0, :]
    lane16 = lax.broadcasted_iota(jnp.int32, (PLANE, LANES), 1)
    for t in range(2):
        def back(v, n):
            return pltpu.roll(v, (n - t * ROWS) % LANES, 1)

        lo = jnp.where(lane16 < HALF, back(t0, 0), back(t1, HALF))
        up = jnp.where(lane16 < 3 * HALF, back(t0, HALF), back(t1, ROWS))
        gw_out[:, t * LANES:(t + 1) * LANES] = jnp.where(lane16 < ROWS, lo, up).astype(BF16)

    for t in range(2):
        pair = jnp.where(left1, klb[2 * t, 0:1, :], klb[2 * t + 1, 0:1, :])
        kl_out[:, t * LANES:(t + 1) * LANES] = pair.astype(BF16)

    came(gk_out.at[1:GROUPS], gkt)
    came(gq_out.at[:, 1 - core], d4c)

    for ref, sems in sent:
        rc(ref, ref, sems, partner).wait_send()


def finish(a, b, c, d, a_out, b_out, c_out, d_out, sem):
    copies = [
        pltpu.make_async_copy(src, dst, sem.at[k])
        for k, (src, dst) in enumerate(((b, b_out), (d, d_out), (c, c_out), (a, a_out)))
    ]
    for x in copies:
        x.start()
    for x in copies:
        x.wait()


def local(query_mla, key_mla, lse, query_index, key_index, head_weight, query_pos, key_block):
    hbm = pl.BlockSpec(memory_space=pltpu.HBM)
    vmem = pl.BlockSpec(memory_space=pltpu.VMEM)
    dma = pltpu.SemaphoreType.DMA
    V = pltpu.VMEM
    kl, gq, gw, gk = pl.pallas_call(
        body,
        out_shape=(
            jax.ShapeDtypeStruct((1, 256), BF16),
            jax.ShapeDtypeStruct((GROUPS, 2, HALF, PLANE * LANES), BF16),
            jax.ShapeDtypeStruct((PLANE, 256), BF16),
            jax.ShapeDtypeStruct((GROUPS, LANES, LANES), BF16),
        ),
        in_specs=[hbm] * 7 + [pl.BlockSpec(memory_space=pltpu.SMEM)],
        out_specs=(vmem, vmem, vmem, vmem),
        scratch_shapes=[
            V((256, 6144), BF16), V((KEYS, 6144), BF16), V((KEYS, 256), F32),
            V((GROUPS, 256, LANES), F32), V((GROUPS, 256, LANES), BF16), V((GROUPS, 256, LANES), BF16),
            V((GROUPS, PLANE, 2, HALF, LANES), BF16), V((GROUPS, 8, LANES), F32),
            V((KEYS, 64 * ROWS), BF16), V((64 * ROWS, LANES), BF16), V((KEYS, LANES), F32),
            V((KEYS, LANES), F32), V((KEYS, LANES), F32),
            V((2 * PLANE, 4, LANES), F32), V((2, 4, LANES), F32),
            V((2, GROUPS, PLANE, HALF, LANES), BF16), V((GROUPS, PLANE, HALF, LANES), BF16),
            V((GROUPS, PLANE, HALF, LANES), BF16), V((GROUPS, PLANE, HALF, LANES), BF16),
            V((GROUPS, HALF, LANES), BF16), V((8, HALF, LANES), BF16),
            V((GROUPS, HALF, LANES), BF16), V((GROUPS, HALF, LANES), F32),
            V((2 * PLANE, 1, LANES), F32), V((GROUPS, LANES, LANES), BF16), V((GROUPS, LANES, LANES), BF16),
            V((PAIRS, 2, 256), F32), V((GROUPS, 8, LANES), F32), V((GROUPS, 2, HALF, PLANE), F32), V((GROUPS, 8, LANES), F32),
            V((32, 256), F32), V((KEYS, LANES), BF16), V((PLANE, 256), F32), V((1, 256), jnp.int32),
            dma((4,)), dma((2, CHUNKS)), dma((2,)), dma((2,)), dma((2,)), dma((5,)), dma((5,)), dma((2,)), dma((2,)),
            dma((2,)), dma((2,)), dma((5,)), dma((5,)), dma((2,)), dma((5,)), dma((2,)), dma((2,)), dma((2,)), dma((2,)),
        ],
        compiler_params=pltpu.CompilerParams(
            collective_id=0, has_side_effects=True, vmem_limit_bytes=50 * 1024 * 1024
        ),
    )(*(pltpu.with_memory_space_constraint(x, pltpu.HBM) for x in (
        query_mla, key_mla, lse.T, query_index.reshape(GROUPS, 2, HALF, PLANE * LANES), key_index,
        head_weight.T, query_pos.reshape(1, 256),
    )), key_block)
    kl, gq, gw, gk = pl.pallas_call(
        finish,
        out_shape=(
            jax.ShapeDtypeStruct((1, 256), BF16),
            jax.ShapeDtypeStruct((GROUPS, 2, HALF, PLANE * LANES), BF16),
            jax.ShapeDtypeStruct((PLANE, 256), BF16),
            jax.ShapeDtypeStruct((GROUPS, LANES, LANES), BF16),
        ),
        in_specs=[vmem] * 4,
        out_specs=[hbm] * 4,
        scratch_shapes=[dma((4,))],
        compiler_params=pltpu.CompilerParams(vmem_limit_bytes=1024 * 1024),
    )(kl, gq, gw, gk)
    return kl.reshape(256), gq.reshape(256, PLANE * LANES), gw.T, gk.reshape(KEYS, LANES)


def solution(mesh):
    return jax.shard_map(
        local,
        mesh=mesh,
        in_specs=(
            P(None, "head"), P("seq", "head"), P(None, "head"), P(None, "head"),
            P("seq", None), P(None, "head"), P(), P("seq"),
        ),
        out_specs=(P(), P(None, "head"), P(None, "head"), P("seq", None)),
        check_vma=False,
    )
```

```python
import functools
import math

import jax
import jax.numpy as jnp
from jax import lax
from jax.experimental import pallas as pl
from jax.experimental.pallas import tpu as pltpu
from jax.sharding import PartitionSpec as P

MESH = pl.DeviceIdType.MESH
F32 = jnp.float32
BF16 = jnp.bfloat16

GROUPS = 4
PLANE = 16
ROWS = 64
HALF = 32
KEYS = 512
PAIRS = 16
WIDE = 192
LANES = 128
CHUNKS = 8
CHUNK_PAIRS = PAIRS // CHUNKS
CHUNK = CHUNK_PAIRS * 2 * WIDE
NT = (((1,), (1,)), ((), ()))
TN = (((0,), (0,)), ((), ()))
NN = (((1,), (0,)), ((), ()))
ROW_ORDER = (2, 1, 3, 0)
FAR_FIRST = tuple((dy, dx) for dy in ROW_ORDER for dx in (2, 1, 3, 0) if dy or dx)
LOG2E = math.log2(math.e)


def dot(a, b, dims):
    return lax.dot_general(a, b, dims, preferred_element_type=F32)


def body(
    qm, km, lse_h, qi, ki_h, hw_h, qpos_h, kb,
    kl_out, gq_out, gw_out, gk_out,
    qbuf, kbuf, acc, blk, att_s, att_r, qall, wall, kall, kbv, dots, wq, lacc, ebuf, abuf,
    st_all, st_two, g2, r2, g3, r3, qfin, prod, gwb, gk_s, gk_r, gk_p, gk_q,
    lse, wpack, hw, klb, lse_t, hw_t, qpos,
    small, ld, qloc, qz, wz, qx, kx, kvx, at, st1, st2, kls, d2, d3, d4, d4c, gws, gwc, gks, gkt, gkp,
):
    h = lax.axis_index("head")
    s = lax.axis_index("seq")
    core = s % 2
    zh = (s // 2) % 2
    yx = s // 4
    gy = yx // 4
    gx = yx % 4

    def seat(dy, dx):
        return ((gy + dy) % 4) * 4 + (gx + dx) % 4

    def at_plane(dy, dx, other_core=0):
        c = (core + other_core) % 2
        return (h, seat(dy, dx) * 4 + zh * 2 + c)

    def at_head(r, other_core=0, other_half=0):
        c = (core + other_core) % 2
        return ((h + r) % GROUPS, yx * 4 + ((zh + other_half) % 2) * 2 + c)

    partner = at_plane(0, 0, 1)

    def rc(src, dst, sems, dev, k=1):
        return pltpu.make_async_remote_copy(
            src_ref=src, dst_ref=dst, send_sem=sems.at[0], recv_sem=sems.at[k],
            device_id=dev, device_id_type=MESH,
        )

    def came(ref, sems, k=1):
        rc(ref, ref, sems, partner, k).wait_recv()

    sent = []

    def left_with(ref, sems):
        sent.append((ref, sems))

    bar = pltpu.get_barrier_semaphore()

    def hello(dev):
        pl.semaphore_signal(bar, inc=1, device_id=dev, device_id_type=MESH)

    for r in range(GROUPS):
        hello(at_head(r, 0, 1))
    for dy, dx in FAR_FIRST:
        hello(at_plane(dy, dx))
    for r in (3, 2, 1):
        hello(at_head(r, 1))
        hello(at_head(r))
    hello(partner)
    smalls = [
        pltpu.make_async_copy(src, dst, small.at[k])
        for k, (src, dst) in enumerate(
            ((lse_h, lse_t), (hw_h, hw_t), (ki_h, kall.at[0]), (qpos_h, qpos))
        )
    ]
    for c in smalls:
        c.start()

    def loop(lo, hi, f):
        def step(k, carry):
            f(k)
            return carry

        lax.fori_loop(lo, hi, step, 0)

    def chunk_copies(k):
        cols = pl.ds(pl.multiple_of(k * CHUNK, LANES), CHUNK)
        return (
            pltpu.make_async_copy(qm.at[:, cols], qbuf.at[:, cols], ld.at[0, k]),
            pltpu.make_async_copy(km.at[:, cols], kbuf.at[:, cols], ld.at[1, k]),
        )

    def start_chunk(k):
        for c in chunk_copies(k):
            c.start()

    loop(0, CHUNKS, start_chunk)

    def own_head(k):
        cols = pl.ds(pl.multiple_of(k * LANES, LANES), LANES)
        pltpu.make_async_copy(qi.at[h, core, :, cols], qall.at[0, k], qloc.at[0]).start()

    loop(0, PLANE, own_head)
    my_cols = pl.ds(pl.multiple_of(yx * LANES, LANES), LANES)
    fin_copy = pltpu.make_async_copy(qi.at[:, core, :, my_cols], qfin, qloc.at[1])
    fin_copy.start()

    for c in smalls:
        c.wait()
    for p in range(PAIRS):
        lse[p] = lse_t[2 * p:2 * p + 2, :] * LOG2E
    kbv[0] = jnp.full((1, LANES), kb[0] * KEYS, jnp.int32)
    group4 = lax.broadcasted_iota(jnp.int32, (4, LANES), 1) // HALF

    def moved(v, a, b):
        return v if a == b else pltpu.roll(v, ((a - b) * HALF) % LANES, 1)

    def side_by_side(parts, b, group):
        out = moved(parts[0], 0, b)
        for a in range(1, 4):
            out = jnp.where(group == a, moved(parts[a], a, b), out)
        return out

    for t in range(2):
        both = hw_t[:, t * LANES:(t + 1) * LANES]
        fours = [jnp.concatenate([both[4 * k + a:4 * k + a + 1] for k in range(4)], axis=0) for a in range(4)]
        for b in range(4):
            wpack[2 * t + b // 2, b % 2] = side_by_side(fours, b, group4)

    acc[...] = jnp.zeros_like(acc)
    scale = WIDE ** -0.5 * LOG2E

    def attend(k):
        for c in chunk_copies(k):
            c.wait()
        for j in range(CHUNK_PAIRS):
            pair = k * CHUNK_PAIRS + j
            base = pair * (2 * WIDE)
            lo = pl.ds(pl.multiple_of(base, LANES), 2 * LANES)
            hi = pl.ds(pl.multiple_of(base + LANES, LANES), 2 * LANES)
            lane = lax.broadcasted_iota(jnp.int32, (256, 2 * LANES), 1)
            q_a = jnp.where(lane < WIDE, qbuf[:, lo], 0).astype(BF16)
            q_b = jnp.where(lane >= 2 * LANES - WIDE, qbuf[:, hi], 0).astype(BF16)
            ls = lse[pair]
            s_a = dot(kbuf[:, lo], q_a, NT)
            s_b = dot(kbuf[:, hi], q_b, NT)
            acc[...] += jnp.exp2(s_a * scale - ls[0:1, :]) + jnp.exp2(s_b * scale - ls[1:2, :])

    loop(0, 4, attend)

    pl.semaphore_wait(bar, GROUPS + 15 + 6 + 1)
    wall[0] = wpack[h, core]
    for r in (3, 2, 1):
        g = (h + r) % GROUPS
        slot = GROUPS - r
        rc(qi.at[g, core, :, my_cols], qall.at[slot, yx], qz, at_head(r)).start()
        rc(wpack.at[g, core], wall.at[slot], wz, at_head(r)).start()
    left_with(qall.at[1:GROUPS, yx], qz)
    left_with(wall.at[1:GROUPS], wz)
    rc(ki_h, kall.at[1], kx, partner).start()
    rc(kbv.at[0], kbv.at[1], kvx, partner).start()
    left_with(kall.at[1], kx)
    left_with(kbv.at[1], kvx)

    loop(4, CHUNKS, attend)

    group = lax.broadcasted_iota(jnp.int32, (LANES, LANES), 1) // HALF
    for t in range(2):
        parts = [acc[q * LANES:(q + 1) * LANES, t * LANES:(t + 1) * LANES] for q in range(4)]
        for b in range(4):
            packed = side_by_side(parts, b, group)
            blk[2 * t + b // 2, b % 2] = packed
            att_s[2 * t + b // 2, b % 2] = packed.astype(BF16)

    for r in (3, 2, 1, 0):
        for k in range(2):
            if r or k:
                slot = k * 4 + (GROUPS - r) % GROUPS
                mine = att_s.at[(h + r) % GROUPS, (core + k) % 2]
                rc(mine, att_r.at[slot], at, at_head(r, k)).start()
    left_with(att_r.at[1:], at)

    came(qall.at[1:GROUPS, yx], qz)
    came(wall.at[1:GROUPS], wz)
    mine = qall.at[1:GROUPS, yx]
    for dy, dx in FAR_FIRST:
        rc(mine, mine, qx, at_plane(dy, dx), 1 + dy).start()
    left_with(qall.at[1:GROUPS, 1:PLANE], qx)

    lacc[...] = jnp.zeros_like(lacc)

    def index_part(slots, k, n):
        wide = n * LANES
        qq = qall[slots, pl.ds(4 * k, 4 * n)].reshape(-1, LANES)
        d = dot(keys(), qq, NT)
        add = None
        for i, r in enumerate(range(GROUPS)[slots]):
            part = d[:, i * wide:(i + 1) * wide]
            cols = pl.ds(pl.multiple_of(r * 512 + k * LANES, LANES), wide)
            dots[:, cols] = part.astype(BF16)
            for j in range(n):
                w = wall[r, pl.ds(k + j, 1), :]
                term = w * jnp.maximum(part[:, j * LANES:(j + 1) * LANES], 0.0)
                add = term if add is None else add + term
        lacc[...] += add

    def keys():
        return kall[...].reshape(2 * KEYS, LANES)

    pltpu.make_async_copy(qall.at[0], qall.at[0], qloc.at[0]).wait()
    came(kall.at[1], kx)
    came(kbv.at[1], kvx)
    for k in (0, 2):
        index_part(slice(0, 1), k, 2)

    for dy in ROW_ORDER:
        row = (gy + 4 - dy) % 4
        came(qall.at[1:GROUPS, 0:(4 if dy else 3)], qx, 1 + dy)
        index_part(slice(1, GROUPS), row, 1)

    came(att_r.at[1:], at)
    lane1 = lax.broadcasted_iota(jnp.int32, (1, LANES), 1) // HALF

    def spread(v, mask):
        v = jnp.where(mask, v, jnp.zeros_like(v))
        v = v + pltpu.roll(v, HALF, 1)
        return v + pltpu.roll(v, 2 * HALF, 1)

    limit = jnp.where(h < 2, qpos[:, :LANES], qpos[:, LANES:])
    limit = spread(limit, lane1 == (h % 2) * 2 + core)
    rowid = lax.broadcasted_iota(jnp.int32, (LANES, LANES), 0)

    def valid(c, q):
        return rowid + (kbv[c] + q * LANES) <= limit

    blocks = [(c, q, slice(c * KEYS + q * LANES, c * KEYS + (q + 1) * LANES)) for c in range(2) for q in range(4)]
    for c in range(2):
        a = blk[h, core] if c == 0 else att_r[4].astype(F32)
        for r in range(1, GROUPS):
            a += att_r[c * 4 + r].astype(F32)
        for q in range(4):
            abuf[c * KEYS + q * LANES:c * KEYS + (q + 1) * LANES] = spread(a, group == q)
    peak = None
    for c, q, at_rows in blocks:
        ok = valid(c, q)
        abuf[at_rows] = jnp.where(ok, abuf[at_rows], 0.0)
        lg = lacc[at_rows]
        lg = lg + pltpu.roll(lg, 2 * HALF, 1)
        lg = lg + pltpu.roll(lg, HALF, 1)
        lg = jnp.where(ok, lg, -1e30)
        lacc[at_rows] = lg
        top = jnp.max(lg, axis=0, keepdims=True)
        peak = top if peak is None else jnp.maximum(peak, top)
    norm = total = cross = jnp.zeros((1, LANES), F32)
    for c, q, at_rows in blocks:
        ok = valid(c, q)
        rel = lacc[at_rows] - peak
        e = jnp.where(ok, jnp.exp(rel), 0.0)
        ebuf[at_rows] = e
        av = abuf[at_rows]
        norm += jnp.sum(e, axis=0, keepdims=True)
        total += jnp.sum(av, axis=0, keepdims=True)
        cross += jnp.sum(
            jnp.where(ok, av * (jnp.log(jnp.where(ok, av, 1.0)) - rel), 0.0), axis=0, keepdims=True
        )
    tile = jnp.concatenate([peak, norm, total, cross], axis=0)
    st_all[yx] = tile

    mine = st_all.at[yx]
    for dy, dx in FAR_FIRST:
        rc(mine, mine, st1, at_plane(dy, dx)).start()
    left_with(st_all.at[1:], st1)

    hw[...] = jnp.transpose(hw_t[...]).reshape(GROUPS, 2, HALF, PLANE)

    wcol = jnp.transpose(wall[...].reshape(4 * 4, LANES))
    for r in range(GROUPS):
        for k in range(4):
            qq = qall[r, 4 * k:4 * k + 4].reshape(4 * HALF, LANES).astype(F32)
            n = r * 4 + k
            wq[n * LANES:(n + 1) * LANES] = (qq * wcol[:, n:n + 1]).astype(BF16)

    def merge(t):
        pk = jnp.max(t[:, 0, :], axis=0, keepdims=True)
        nm = jnp.sum(t[:, 1, :] * jnp.exp(t[:, 0, :] - pk), axis=0, keepdims=True)
        tt = jnp.sum(t[:, 2, :], axis=0, keepdims=True)
        cr = jnp.sum(t[:, 3, :] + t[:, 2, :] * (pk - t[:, 0, :]), axis=0, keepdims=True)
        return pk, nm, tt, cr

    came(st_all.at[1:], st1)
    st_two[0] = jnp.concatenate(merge(st_all[...]), axis=0)
    rc(st_two.at[0], st_two.at[1], st2, at_head(0, 0, 1)).start()
    left_with(st_two.at[0], st2)
    came(st_two.at[1], st2)
    peak_g, norm_g, total_g, cross_g = merge(st_two[...])
    inv_t = 1.0 / total_g
    kl = cross_g * inv_t - jnp.log(total_g) + jnp.log(norm_g)
    klb[2 * h + core] = kl
    mine = klb.at[2 * h + core]
    for r in (3, 2, 1, 0):
        for k in range(2):
            if r or k:
                rc(mine, mine, kls, at_head(r, k)).start()
    left_with(klb.at[1:], kls)

    grow = jnp.exp(peak - peak_g) / norm_g
    dl = (ebuf[...] * grow - abuf[...] * inv_t).astype(BF16)
    dl2 = jnp.concatenate([dl, dl], axis=1)
    zero = jnp.zeros_like(dl2)

    for r in range(GROUPS):
        for q in range(2):
            lo = r * 512 + q * 2 * LANES
            g = jnp.where(dots[:, lo:lo + 2 * LANES] > 0, dl2, zero)
            dots[:, lo:lo + 2 * LANES] = g
            g2[r, 8 * q:8 * q + 8] = dot(g, keys(), TN).astype(BF16).reshape(8, HALF, LANES)
        for k, (dy, dx) in enumerate(FAR_FIRST):
            rc(g2.at[r, seat(dy, dx)], r2.at[r, k], d2, at_plane(dy, dx), 1 + r).start()
    left_with(r2.at[:, 0:15], d2)

    gk = jnp.zeros((2 * KEYS, LANES), F32)
    for r in range(GROUPS):
        gk += dot(dots[:, r * 512:(r + 1) * 512], wq[r * 512:(r + 1) * 512], NN)
    gk_p[...] = gk[KEYS:].astype(BF16)
    rc(gk_p, gk_q, gkp, partner).start()
    left_with(gk_p, gkp)
    gk_own = gk[:KEYS]

    for r in range(GROUPS):
        if r == 1:
            came(gk_q, gkp)
            gk_s[...] = (gk_own + gk_q[...].astype(F32)).astype(BF16).reshape(4, LANES, LANES)
            for k in (3, 2, 1):
                rc(gk_s.at[(h + k) % GROUPS], gk_r.at[k], gks, at_head(k)).start()
            left_with(gk_s.at[1:GROUPS], gks)
        came(r2.at[r, 0:15], d2, 1 + r)
        tot = g2[r, yx].astype(F32)
        for p in range(PLANE - 1):
            tot += r2[r, p].astype(F32)
        g3[r] = tot.astype(BF16)
        for other in (1, 0):
            if r or other:
                rc(g3.at[r], r3.at[2 * r + other], d3, at_head(r, 0, other)).start()
    left_with(r3.at[1:], d3)

    came(gk_r.at[1:GROUPS], gks)
    mine = gk_s[h].astype(F32)
    for r in range(1, GROUPS):
        mine += gk_r[r].astype(F32)
    gk_out[h] = mine.astype(BF16)
    for r in (3, 2, 1):
        rc(gk_out.at[h], gk_out.at[h], gkt, at_head(r)).start()
    left_with(gk_out.at[1:GROUPS], gkt)

    fin_copy.wait()
    came(r3.at[1:], d3)
    onehot = lax.broadcasted_iota(jnp.int32, (HALF, PLANE), 1) == yx
    for r in range(GROUPS):
        g = (h - r + GROUPS) % GROUPS
        near = g3[0] if r == 0 else r3[2 * r]
        full = near.astype(F32) + r3[2 * r + 1].astype(F32)
        w = jnp.sum(jnp.where(onehot, hw[g, core], 0.0), axis=1, keepdims=True)
        gq_out[g, core, :, my_cols] = (full * w).astype(BF16)
        prod[g] = full * qfin[g].astype(F32)

    mine = gq_out.at[:, core, :, my_cols]
    for dy, dx in FAR_FIRST[:4]:
        rc(mine, mine, d4, at_plane(dy, dx), 1 + dy).start()
    gw_row = jnp.sum(jnp.transpose(prod[...].reshape(LANES, LANES)), axis=0, keepdims=True)
    my_seat = core * PLANE + yx
    gwb[my_seat] = gw_row
    tile = gwb.at[my_seat]
    for dy, dx in FAR_FIRST:
        rc(tile, tile, gws, at_plane(dy, dx)).start()
    left_with(gwb.at[1:PLANE], gws)
    for dy, dx in FAR_FIRST[4:]:
        rc(mine, mine, d4, at_plane(dy, dx), 1 + dy).start()
    left_with(gq_out.at[:, core, :, LANES:], d4)

    def row_cols(dy):
        return pl.ds(pl.multiple_of(((gy + 4 - dy) % 4) * 4 * LANES, LANES), 4 * LANES)

    for dy in ROW_ORDER:
        if dy == 0:
            came(gwb.at[1:PLANE], gws)
            tiles = gwb.at[pl.ds(core * PLANE, PLANE)]
            rc(tiles, tiles, gwc, partner).start()
            left_with(gwb.at[0:PLANE], gwc)
        row = gq_out.at[:, core, :, row_cols(dy)]
        came(row if dy else gq_out.at[:, core, :, 0:3 * LANES], d4, 1 + dy)
        rc(row, row, d4c, partner).start()
    left_with(gq_out.at[:, core], d4c)
    came(gwb.at[0:PLANE], gwc)
    came(klb.at[1:], kls)
    t0, t1 = gwb[0:PLANE, 0, :], gwb[PLANE:, 0, :]
    lane16 = lax.broadcasted_iota(jnp.int32, (PLANE, LANES), 1)
    for t in range(2):
        def back(v, n):
            return pltpu.roll(v, (n - t * ROWS) % LANES, 1)

        lo = jnp.where(lane16 < HALF, back(t0, 0), back(t1, HALF))
        up = jnp.where(lane16 < 3 * HALF, back(t0, HALF), back(t1, ROWS))
        gw_out[:, t * LANES:(t + 1) * LANES] = jnp.where(lane16 < ROWS, lo, up).astype(BF16)

    for t in range(2):
        pair = klb[4 * t]
        for b in range(1, 4):
            pair = jnp.where(lane1 == b, klb[4 * t + b], pair)
        kl_out[:, t * LANES:(t + 1) * LANES] = pair.astype(BF16)

    came(gk_out.at[1:GROUPS], gkt)
    came(gq_out.at[:, 1 - core], d4c)

    for ref, sems in sent:
        rc(ref, ref, sems, partner).wait_send()


def finish(a, b, c, d, a_out, b_out, c_out, d_out, sem):
    copies = [
        pltpu.make_async_copy(src, dst, sem.at[k])
        for k, (src, dst) in enumerate(((b, b_out), (d, d_out), (c, c_out), (a, a_out)))
    ]
    for x in copies:
        x.start()
    for x in copies:
        x.wait()


def local(query_mla, key_mla, lse, query_index, key_index, head_weight, query_pos, key_block):
    hbm = pl.BlockSpec(memory_space=pltpu.HBM)
    vmem = pl.BlockSpec(memory_space=pltpu.VMEM)
    dma = pltpu.SemaphoreType.DMA
    V = pltpu.VMEM
    kl, gq, gw, gk = pl.pallas_call(
        body,
        out_shape=(
            jax.ShapeDtypeStruct((1, 256), BF16),
            jax.ShapeDtypeStruct((GROUPS, 2, HALF, PLANE * LANES), BF16),
            jax.ShapeDtypeStruct((PLANE, 256), BF16),
            jax.ShapeDtypeStruct((GROUPS, LANES, LANES), BF16),
        ),
        in_specs=[hbm] * 7 + [pl.BlockSpec(memory_space=pltpu.SMEM)],
        out_specs=(vmem, vmem, vmem, vmem),
        scratch_shapes=[
            V((256, 6144), BF16), V((KEYS, 6144), BF16), V((KEYS, 256), F32),
            V((GROUPS, 2, LANES, LANES), F32), V((GROUPS, 2, LANES, LANES), BF16), V((8, LANES, LANES), BF16),
            V((GROUPS, PLANE, HALF, LANES), BF16), V((GROUPS, 4, LANES), F32),
            V((2, KEYS, LANES), BF16), V((2, 1, LANES), jnp.int32),
            V((2 * KEYS, 64 * HALF), BF16), V((64 * HALF, LANES), BF16), V((2 * KEYS, LANES), F32),
            V((2 * KEYS, LANES), F32), V((2 * KEYS, LANES), F32),
            V((PLANE, 4, LANES), F32), V((2, 4, LANES), F32),
            V((GROUPS, PLANE, HALF, LANES), BF16), V((GROUPS, PLANE, HALF, LANES), BF16),
            V((GROUPS, HALF, LANES), BF16), V((8, HALF, LANES), BF16),
            V((GROUPS, HALF, LANES), BF16), V((GROUPS, HALF, LANES), F32),
            V((2 * PLANE, 1, LANES), F32), V((GROUPS, LANES, LANES), BF16), V((GROUPS, LANES, LANES), BF16),
            V((KEYS, LANES), BF16), V((KEYS, LANES), BF16),
            V((PAIRS, 2, 256), F32), V((GROUPS, 2, 4, LANES), F32), V((GROUPS, 2, HALF, PLANE), F32), V((8, 1, LANES), F32),
            V((32, 256), F32), V((PLANE, 256), F32), V((1, 256), jnp.int32),
            dma((4,)), dma((2, CHUNKS)), dma((2,)), dma((2,)), dma((2,)), dma((5,)), dma((2,)), dma((2,)), dma((2,)), dma((2,)),
            dma((2,)), dma((2,)), dma((5,)), dma((2,)), dma((5,)), dma((2,)), dma((2,)), dma((2,)), dma((2,)), dma((2,)), dma((2,)),
        ],
        compiler_params=pltpu.CompilerParams(
            collective_id=0, has_side_effects=True, vmem_limit_bytes=50 * 1024 * 1024
        ),
    )(*(pltpu.with_memory_space_constraint(x, pltpu.HBM) for x in (
        query_mla, key_mla, lse.T, query_index.reshape(GROUPS, 2, HALF, PLANE * LANES), key_index,
        head_weight.T, query_pos.reshape(1, 256),
    )), key_block)
    kl, gq, gw, gk = pl.pallas_call(
        finish,
        out_shape=(
            jax.ShapeDtypeStruct((1, 256), BF16),
            jax.ShapeDtypeStruct((GROUPS, 2, HALF, PLANE * LANES), BF16),
            jax.ShapeDtypeStruct((PLANE, 256), BF16),
            jax.ShapeDtypeStruct((GROUPS, LANES, LANES), BF16),
        ),
        in_specs=[vmem] * 4,
        out_specs=[hbm] * 4,
        scratch_shapes=[dma((4,))],
        compiler_params=pltpu.CompilerParams(vmem_limit_bytes=1024 * 1024),
    )(kl, gq, gw, gk)
    return kl.reshape(256), gq.reshape(256, PLANE * LANES), gw.T, gk.reshape(KEYS, LANES)


def solution(mesh):
    return jax.shard_map(
        local,
        mesh=mesh,
        in_specs=(
            P(None, "head"), P("seq", "head"), P(None, "head"), P(None, "head"),
            P("seq", None), P(None, "head"), P(), P("seq"),
        ),
        out_specs=(P(), P(None, "head"), P(None, "head"), P("seq", None)),
        check_vma=False,
    )
```

```python
import functools
import math

import jax
import jax.numpy as jnp
from jax import lax
from jax.experimental import pallas as pl
from jax.experimental.pallas import tpu as pltpu
from jax.sharding import PartitionSpec as P

MESH = pl.DeviceIdType.MESH
F32 = jnp.float32
BF16 = jnp.bfloat16

GROUPS = 4
PLANE = 16
ROWS = 64
HALF = 32
KEYS = 512
PAIRS = 16
WIDE = 192
LANES = 128
CHUNKS = 8
CHUNK_PAIRS = PAIRS // CHUNKS
CHUNK = CHUNK_PAIRS * 2 * WIDE
NT = (((1,), (1,)), ((), ()))
TN = (((0,), (0,)), ((), ()))
NN = (((1,), (0,)), ((), ()))
ROW_ORDER = (2, 1, 3, 0)
FAR_FIRST = tuple((dy, dx) for dy in ROW_ORDER for dx in (2, 1, 3, 0) if dy or dx)
ROWS_NEAR = (0, 1, 3, 2)
NEAR_FIRST = tuple((dy, dx) for dy in ROWS_NEAR for dx in (0, 1, 3, 2) if dy or dx)
LOG2E = math.log2(math.e)


def dot(a, b, dims):
    return lax.dot_general(a, b, dims, preferred_element_type=F32)


def body(
    qm, km, lse_h, qi, ki_h, hw_h, qpos_h, kb,
    kl_out, gq_out, gw_out, gk_out,
    qbuf, kbuf, acc, blk, att_s, att_r, qall, wall, kall, kbv, dots, wq, lacc, ebuf, abuf, dlb,
    st_all, st_two, g2, r2, g3, r3, qfin, prod, gwb, gk_s, gk_r, gk_p, gk_q,
    lse, wpack, hw, klb, lse_t, hw_t, qpos,
    small, ld, qloc, qz, wz, qx, kx, kvx, at, st1, st2, kls, d2, d3, d4, d4c, gws, gwc, gks, gkt, gkp,
):
    h = lax.axis_index("head")
    s = lax.axis_index("seq")
    core = s % 2
    zh = (s // 2) % 2
    yx = s // 4
    gy = yx // 4
    gx = yx % 4

    def seat(dy, dx):
        return ((gy + dy) % 4) * 4 + (gx + dx) % 4

    def at_plane(dy, dx, other_core=0):
        c = (core + other_core) % 2
        return (h, seat(dy, dx) * 4 + zh * 2 + c)

    def at_head(r, other_core=0, other_half=0):
        c = (core + other_core) % 2
        return ((h + r) % GROUPS, yx * 4 + ((zh + other_half) % 2) * 2 + c)

    partner = at_plane(0, 0, 1)

    def rc(src, dst, sems, dev, k=1):
        return pltpu.make_async_remote_copy(
            src_ref=src, dst_ref=dst, send_sem=sems.at[0], recv_sem=sems.at[k],
            device_id=dev, device_id_type=MESH,
        )

    def came(ref, sems, k=1):
        rc(ref, ref, sems, partner, k).wait_recv()

    sent = []

    def left_with(ref, sems):
        sent.append((ref, sems))

    bar = pltpu.get_barrier_semaphore()

    def hello(dev):
        pl.semaphore_signal(bar, inc=1, device_id=dev, device_id_type=MESH)

    for r in range(GROUPS):
        hello(at_head(r, 0, 1))
    for dy, dx in FAR_FIRST:
        hello(at_plane(dy, dx))
    for r in (3, 2, 1):
        hello(at_head(r, 1))
        hello(at_head(r))
    hello(partner)
    smalls = [
        pltpu.make_async_copy(src, dst, small.at[k])
        for k, (src, dst) in enumerate(
            ((lse_h, lse_t), (hw_h, hw_t), (ki_h, kall.at[0]), (qpos_h, qpos))
        )
    ]
    for c in smalls:
        c.start()

    def loop(lo, hi, f):
        def step(k, carry):
            f(k)
            return carry

        lax.fori_loop(lo, hi, step, 0)

    def chunk_copies(k):
        cols = pl.ds(pl.multiple_of(k * CHUNK, LANES), CHUNK)
        return (
            pltpu.make_async_copy(qm.at[:, cols], qbuf.at[:, cols], ld.at[0, k]),
            pltpu.make_async_copy(km.at[:, cols], kbuf.at[:, cols], ld.at[1, k]),
        )

    def start_chunk(k):
        for c in chunk_copies(k):
            c.start()

    loop(0, CHUNKS, start_chunk)

    def own_head(k):
        cols = pl.ds(pl.multiple_of(k * LANES, LANES), LANES)
        pltpu.make_async_copy(qi.at[h, core, :, cols], qall.at[0, k], qloc.at[0]).start()

    loop(0, PLANE, own_head)
    my_cols = pl.ds(pl.multiple_of(yx * LANES, LANES), LANES)
    fin_copy = pltpu.make_async_copy(qi.at[:, core, :, my_cols], qfin, qloc.at[1])
    fin_copy.start()

    for c in smalls:
        c.wait()
    for p in range(PAIRS):
        lse[p] = lse_t[2 * p:2 * p + 2, :] * LOG2E
    kbv[0] = jnp.full((1, LANES), kb[0] * KEYS, jnp.int32)
    group4 = lax.broadcasted_iota(jnp.int32, (4, LANES), 1) // HALF

    def moved(v, a, b):
        return v if a == b else pltpu.roll(v, ((a - b) * HALF) % LANES, 1)

    def side_by_side(parts, b, group):
        out = moved(parts[0], 0, b)
        for a in range(1, 4):
            out = jnp.where(group == a, moved(parts[a], a, b), out)
        return out

    for t in range(2):
        both = hw_t[:, t * LANES:(t + 1) * LANES]
        fours = [jnp.concatenate([both[4 * k + a:4 * k + a + 1] for k in range(4)], axis=0) for a in range(4)]
        for b in range(4):
            wpack[2 * t + b // 2, b % 2] = side_by_side(fours, b, group4)

    acc[...] = jnp.zeros_like(acc)
    scale = WIDE ** -0.5 * LOG2E

    def attend(k):
        for c in chunk_copies(k):
            c.wait()
        for j in range(CHUNK_PAIRS):
            pair = k * CHUNK_PAIRS + j
            base = pair * (2 * WIDE)
            lo = pl.ds(pl.multiple_of(base, LANES), 2 * LANES)
            hi = pl.ds(pl.multiple_of(base + LANES, LANES), 2 * LANES)
            lane = lax.broadcasted_iota(jnp.int32, (256, 2 * LANES), 1)
            q_a = jnp.where(lane < WIDE, qbuf[:, lo], 0).astype(BF16)
            q_b = jnp.where(lane >= 2 * LANES - WIDE, qbuf[:, hi], 0).astype(BF16)
            ls = lse[pair]
            s_a = dot(kbuf[:, lo], q_a, NT)
            s_b = dot(kbuf[:, hi], q_b, NT)
            acc[...] += jnp.exp2(s_a * scale - ls[0:1, :]) + jnp.exp2(s_b * scale - ls[1:2, :])

    loop(0, 4, attend)

    pl.semaphore_wait(bar, GROUPS + 15 + 6 + 1)
    wall[0] = wpack[h, core]
    for r in (3, 2, 1):
        g = (h + r) % GROUPS
        slot = GROUPS - r
        rc(qi.at[g, core, :, my_cols], qall.at[slot, yx], qz, at_head(r)).start()
        rc(wpack.at[g, core], wall.at[slot], wz, at_head(r)).start()
    left_with(qall.at[1:GROUPS, yx], qz)
    left_with(wall.at[1:GROUPS], wz)
    rc(ki_h, kall.at[1], kx, partner).start()
    rc(kbv.at[0], kbv.at[1], kvx, partner).start()
    left_with(kall.at[1], kx)
    left_with(kbv.at[1], kvx)

    loop(4, CHUNKS, attend)

    group = lax.broadcasted_iota(jnp.int32, (LANES, LANES), 1) // HALF
    for t in range(2):
        parts = [acc[q * LANES:(q + 1) * LANES, t * LANES:(t + 1) * LANES] for q in range(4)]
        for b in range(4):
            packed = side_by_side(parts, b, group)
            blk[2 * t + b // 2, b % 2] = packed
            att_s[2 * t + b // 2, b % 2] = packed.astype(BF16)

    for r in (3, 2, 1, 0):
        for k in range(2):
            if r or k:
                slot = k * 4 + (GROUPS - r) % GROUPS
                mine = att_s.at[(h + r) % GROUPS, (core + k) % 2]
                rc(mine, att_r.at[slot], at, at_head(r, k)).start()
    left_with(att_r.at[1:], at)

    came(qall.at[1:GROUPS, yx], qz)
    came(wall.at[1:GROUPS], wz)
    mine = qall.at[1:GROUPS, yx]
    for dy, dx in NEAR_FIRST:
        rc(mine, mine, qx, at_plane(dy, dx), 1 + dy).start()
    left_with(qall.at[1:GROUPS, 1:PLANE], qx)

    lacc[...] = jnp.zeros_like(lacc)

    def index_part(slots, k, n):
        wide = n * LANES
        qq = qall[slots, pl.ds(4 * k, 4 * n)].reshape(-1, LANES)
        d = dot(keys(), qq, NT)
        add = None
        for i, r in enumerate(range(GROUPS)[slots]):
            part = d[:, i * wide:(i + 1) * wide]
            cols = pl.ds(pl.multiple_of(r * 512 + k * LANES, LANES), wide)
            dots[:, cols] = part.astype(BF16)
            for j in range(n):
                w = wall[r, pl.ds(k + j, 1), :]
                term = w * jnp.maximum(part[:, j * LANES:(j + 1) * LANES], 0.0)
                add = term if add is None else add + term
        lacc[...] += add

    def keys():
        return kall[...].reshape(2 * KEYS, LANES)

    pltpu.make_async_copy(qall.at[0], qall.at[0], qloc.at[0]).wait()
    came(kall.at[1], kx)
    came(kbv.at[1], kvx)
    for k in (0, 2):
        index_part(slice(0, 1), k, 2)

    for dy in ROWS_NEAR:
        if dy == ROWS_NEAR[-1]:
            came(att_r.at[1:], at)
            for c in range(2):
                a = blk[h, core] if c == 0 else att_r[4].astype(F32)
                for r in range(1, GROUPS):
                    a += att_r[c * 4 + r].astype(F32)
                abuf[c] = a
        came(qall.at[1:GROUPS, 0:(4 if dy else 3)], qx, 1 + dy)
        index_part(slice(1, GROUPS), (gy + 4 - dy) % 4, 1)

    lane1 = lax.broadcasted_iota(jnp.int32, (1, LANES), 1) // HALF

    def spread(v, mask):
        v = jnp.where(mask, v, jnp.zeros_like(v))
        v = v + pltpu.roll(v, HALF, 1)
        return v + pltpu.roll(v, 2 * HALF, 1)

    limit = jnp.where(h < 2, qpos[:, :LANES], qpos[:, LANES:])
    limit = spread(limit, lane1 == (h % 2) * 2 + core)
    rowid = lax.broadcasted_iota(jnp.int32, (LANES, LANES), 0)

    def fold(v, op):
        v = op(v, pltpu.roll(v, 2 * HALF, 1))
        return op(v, pltpu.roll(v, HALF, 1))

    peak = None
    for c in range(2):
        logit = None
        for q in range(4):
            lg = fold(lacc[c * KEYS + q * LANES:c * KEYS + (q + 1) * LANES], jnp.add)
            logit = lg if q == 0 else jnp.where(group == q, lg, logit)
        ok = rowid + (kbv[c] + group * LANES) <= limit
        logit = jnp.where(ok, logit, -1e30)
        ebuf[c] = logit
        abuf[c] = jnp.where(ok, abuf[c], 0.0)
        top = jnp.max(logit, axis=0, keepdims=True)
        peak = top if c == 0 else jnp.maximum(peak, top)
    peak = fold(peak, jnp.maximum)
    norm = total = cross = jnp.zeros((1, LANES), F32)
    for c in range(2):
        ok = rowid + (kbv[c] + group * LANES) <= limit
        rel = ebuf[c] - peak
        e = jnp.where(ok, jnp.exp(rel), 0.0)
        ebuf[c] = e
        av = abuf[c]
        norm += jnp.sum(e, axis=0, keepdims=True)
        total += jnp.sum(av, axis=0, keepdims=True)
        cross += jnp.sum(
            jnp.where(ok, av * (jnp.log(jnp.where(ok, av, 1.0)) - rel), 0.0), axis=0, keepdims=True
        )
    norm, total, cross = (fold(v, jnp.add) for v in (norm, total, cross))
    tile = jnp.concatenate([peak, norm, total, cross], axis=0)
    st_all[yx] = tile

    mine = st_all.at[yx]
    for dy, dx in FAR_FIRST:
        rc(mine, mine, st1, at_plane(dy, dx)).start()
    left_with(st_all.at[1:], st1)

    hw[...] = jnp.transpose(hw_t[...]).reshape(GROUPS, 2, HALF, PLANE)

    wcol = jnp.transpose(wall[...].reshape(4 * 4, LANES))
    for r in range(GROUPS):
        for k in range(4):
            qq = qall[r, 4 * k:4 * k + 4].reshape(4 * HALF, LANES).astype(F32)
            n = r * 4 + k
            wq[n * LANES:(n + 1) * LANES] = (qq * wcol[:, n:n + 1]).astype(BF16)

    def merge(t):
        pk = jnp.max(t[:, 0, :], axis=0, keepdims=True)
        nm = jnp.sum(t[:, 1, :] * jnp.exp(t[:, 0, :] - pk), axis=0, keepdims=True)
        tt = jnp.sum(t[:, 2, :], axis=0, keepdims=True)
        cr = jnp.sum(t[:, 3, :] + t[:, 2, :] * (pk - t[:, 0, :]), axis=0, keepdims=True)
        return pk, nm, tt, cr

    came(st_all.at[1:], st1)
    st_two[0] = jnp.concatenate(merge(st_all[...]), axis=0)
    rc(st_two.at[0], st_two.at[1], st2, at_head(0, 0, 1)).start()
    left_with(st_two.at[0], st2)
    came(st_two.at[1], st2)
    peak_g, norm_g, total_g, cross_g = merge(st_two[...])
    inv_t = 1.0 / total_g
    kl = cross_g * inv_t - jnp.log(total_g) + jnp.log(norm_g)
    klb[2 * h + core] = kl
    mine = klb.at[2 * h + core]
    for r in (3, 2, 1, 0):
        for k in range(2):
            if r or k:
                rc(mine, mine, kls, at_head(r, k)).start()
    left_with(klb.at[1:], kls)

    grow = jnp.exp(peak - peak_g) / norm_g
    for c in range(2):
        packed = ebuf[c] * grow - abuf[c] * inv_t
        for q in range(4):
            dlb[c * KEYS + q * LANES:c * KEYS + (q + 1) * LANES] = spread(packed, group == q).astype(BF16)
    dl = dlb[...]
    dl2 = jnp.concatenate([dl, dl], axis=1)
    zero = jnp.zeros_like(dl2)

    for r in range(GROUPS):
        for q in range(2):
            lo = r * 512 + q * 2 * LANES
            g = jnp.where(dots[:, lo:lo + 2 * LANES] > 0, dl2, zero)
            dots[:, lo:lo + 2 * LANES] = g
            g2[r, 8 * q:8 * q + 8] = dot(g, keys(), TN).astype(BF16).reshape(8, HALF, LANES)
        for k, (dy, dx) in enumerate(FAR_FIRST):
            rc(g2.at[r, seat(dy, dx)], r2.at[r, k], d2, at_plane(dy, dx), 1 + r).start()
    left_with(r2.at[:, 0:15], d2)

    gk = jnp.zeros((2 * KEYS, LANES), F32)
    for r in range(GROUPS):
        gk += dot(dots[:, r * 512:(r + 1) * 512], wq[r * 512:(r + 1) * 512], NN)
    gk_p[...] = gk[KEYS:].astype(BF16)
    rc(gk_p, gk_q, gkp, partner).start()
    left_with(gk_p, gkp)
    gk_own = gk[:KEYS]

    for r in range(GROUPS):
        if r == 1:
            came(gk_q, gkp)
            gk_s[...] = (gk_own + gk_q[...].astype(F32)).astype(BF16).reshape(4, LANES, LANES)
            for k in (3, 2, 1):
                rc(gk_s.at[(h + k) % GROUPS], gk_r.at[k], gks, at_head(k)).start()
            left_with(gk_s.at[1:GROUPS], gks)
        came(r2.at[r, 0:15], d2, 1 + r)
        tot = g2[r, yx].astype(F32)
        for p in range(PLANE - 1):
            tot += r2[r, p].astype(F32)
        g3[r] = tot.astype(BF16)
        for other in (1, 0):
            if r or other:
                rc(g3.at[r], r3.at[2 * r + other], d3, at_head(r, 0, other)).start()
    left_with(r3.at[1:], d3)

    fin_copy.wait()
    came(r3.at[1:], d3)
    onehot = lax.broadcasted_iota(jnp.int32, (HALF, PLANE), 1) == yx
    for r in range(GROUPS):
        g = (h - r + GROUPS) % GROUPS
        near = g3[0] if r == 0 else r3[2 * r]
        full = near.astype(F32) + r3[2 * r + 1].astype(F32)
        w = jnp.sum(jnp.where(onehot, hw[g, core], 0.0), axis=1, keepdims=True)
        gq_out[g, core, :, my_cols] = (full * w).astype(BF16)
        prod[g] = full * qfin[g].astype(F32)

    mine = gq_out.at[:, core, :, my_cols]
    for dy, dx in NEAR_FIRST[:4]:
        rc(mine, mine, d4, at_plane(dy, dx), 1 + dy).start()
    gw_row = jnp.sum(jnp.transpose(prod[...].reshape(LANES, LANES)), axis=0, keepdims=True)
    my_seat = core * PLANE + yx
    gwb[my_seat] = gw_row
    tile = gwb.at[my_seat]
    for dy, dx in FAR_FIRST:
        rc(tile, tile, gws, at_plane(dy, dx)).start()
    left_with(gwb.at[1:PLANE], gws)
    for dy, dx in NEAR_FIRST[4:]:
        rc(mine, mine, d4, at_plane(dy, dx), 1 + dy).start()
    left_with(gq_out.at[:, core, :, LANES:], d4)

    came(gk_r.at[1:GROUPS], gks)
    own = gk_s[h].astype(F32)
    for r in range(1, GROUPS):
        own += gk_r[r].astype(F32)
    gk_out[h] = own.astype(BF16)
    for r in (3, 2, 1):
        rc(gk_out.at[h], gk_out.at[h], gkt, at_head(r)).start()
    left_with(gk_out.at[1:GROUPS], gkt)

    def row_cols(dy):
        return pl.ds(pl.multiple_of(((gy + 4 - dy) % 4) * 4 * LANES, LANES), 4 * LANES)

    for dy in ROWS_NEAR:
        if dy == ROWS_NEAR[-1]:
            came(gwb.at[1:PLANE], gws)
            tiles = gwb.at[pl.ds(core * PLANE, PLANE)]
            rc(tiles, tiles, gwc, partner).start()
            left_with(gwb.at[0:PLANE], gwc)
        row = gq_out.at[:, core, :, row_cols(dy)]
        came(row if dy else gq_out.at[:, core, :, 0:3 * LANES], d4, 1 + dy)
        rc(row, row, d4c, partner).start()
    left_with(gq_out.at[:, core], d4c)
    came(gwb.at[0:PLANE], gwc)
    came(klb.at[1:], kls)
    t0, t1 = gwb[0:PLANE, 0, :], gwb[PLANE:, 0, :]
    lane16 = lax.broadcasted_iota(jnp.int32, (PLANE, LANES), 1)
    for t in range(2):
        def back(v, n):
            return pltpu.roll(v, (n - t * ROWS) % LANES, 1)

        lo = jnp.where(lane16 < HALF, back(t0, 0), back(t1, HALF))
        up = jnp.where(lane16 < 3 * HALF, back(t0, HALF), back(t1, ROWS))
        gw_out[:, t * LANES:(t + 1) * LANES] = jnp.where(lane16 < ROWS, lo, up).astype(BF16)

    for t in range(2):
        pair = klb[4 * t]
        for b in range(1, 4):
            pair = jnp.where(lane1 == b, klb[4 * t + b], pair)
        kl_out[:, t * LANES:(t + 1) * LANES] = pair.astype(BF16)

    came(gk_out.at[1:GROUPS], gkt)
    came(gq_out.at[:, 1 - core], d4c)

    for ref, sems in sent:
        rc(ref, ref, sems, partner).wait_send()


def finish(a, b, c, d, a_out, b_out, c_out, d_out, sem):
    copies = [
        pltpu.make_async_copy(src, dst, sem.at[k])
        for k, (src, dst) in enumerate(((b, b_out), (d, d_out), (c, c_out), (a, a_out)))
    ]
    for x in copies:
        x.start()
    for x in copies:
        x.wait()


def local(query_mla, key_mla, lse, query_index, key_index, head_weight, query_pos, key_block):
    hbm = pl.BlockSpec(memory_space=pltpu.HBM)
    vmem = pl.BlockSpec(memory_space=pltpu.VMEM)
    dma = pltpu.SemaphoreType.DMA
    V = pltpu.VMEM
    kl, gq, gw, gk = pl.pallas_call(
        body,
        out_shape=(
            jax.ShapeDtypeStruct((1, 256), BF16),
            jax.ShapeDtypeStruct((GROUPS, 2, HALF, PLANE * LANES), BF16),
            jax.ShapeDtypeStruct((PLANE, 256), BF16),
            jax.ShapeDtypeStruct((GROUPS, LANES, LANES), BF16),
        ),
        in_specs=[hbm] * 7 + [pl.BlockSpec(memory_space=pltpu.SMEM)],
        out_specs=(vmem, vmem, vmem, vmem),
        scratch_shapes=[
            V((256, 6144), BF16), V((KEYS, 6144), BF16), V((KEYS, 256), F32),
            V((GROUPS, 2, LANES, LANES), F32), V((GROUPS, 2, LANES, LANES), BF16), V((8, LANES, LANES), BF16),
            V((GROUPS, PLANE, HALF, LANES), BF16), V((GROUPS, 4, LANES), F32),
            V((2, KEYS, LANES), BF16), V((2, 1, LANES), jnp.int32),
            V((2 * KEYS, 64 * HALF), BF16), V((64 * HALF, LANES), BF16), V((2 * KEYS, LANES), F32),
            V((2, LANES, LANES), F32), V((2, LANES, LANES), F32), V((2 * KEYS, LANES), BF16),
            V((PLANE, 4, LANES), F32), V((2, 4, LANES), F32),
            V((GROUPS, PLANE, HALF, LANES), BF16), V((GROUPS, PLANE, HALF, LANES), BF16),
            V((GROUPS, HALF, LANES), BF16), V((8, HALF, LANES), BF16),
            V((GROUPS, HALF, LANES), BF16), V((GROUPS, HALF, LANES), F32),
            V((2 * PLANE, 1, LANES), F32), V((GROUPS, LANES, LANES), BF16), V((GROUPS, LANES, LANES), BF16),
            V((KEYS, LANES), BF16), V((KEYS, LANES), BF16),
            V((PAIRS, 2, 256), F32), V((GROUPS, 2, 4, LANES), F32), V((GROUPS, 2, HALF, PLANE), F32), V((8, 1, LANES), F32),
            V((32, 256), F32), V((PLANE, 256), F32), V((1, 256), jnp.int32),
            dma((4,)), dma((2, CHUNKS)), dma((2,)), dma((2,)), dma((2,)), dma((5,)), dma((2,)), dma((2,)), dma((2,)), dma((2,)),
            dma((2,)), dma((2,)), dma((5,)), dma((2,)), dma((5,)), dma((2,)), dma((2,)), dma((2,)), dma((2,)), dma((2,)), dma((2,)),
        ],
        compiler_params=pltpu.CompilerParams(
            collective_id=0, has_side_effects=True, vmem_limit_bytes=50 * 1024 * 1024
        ),
    )(*(pltpu.with_memory_space_constraint(x, pltpu.HBM) for x in (
        query_mla, key_mla, lse.T, query_index.reshape(GROUPS, 2, HALF, PLANE * LANES), key_index,
        head_weight.T, query_pos.reshape(1, 256),
    )), key_block)
    kl, gq, gw, gk = pl.pallas_call(
        finish,
        out_shape=(
            jax.ShapeDtypeStruct((1, 256), BF16),
            jax.ShapeDtypeStruct((GROUPS, 2, HALF, PLANE * LANES), BF16),
            jax.ShapeDtypeStruct((PLANE, 256), BF16),
            jax.ShapeDtypeStruct((GROUPS, LANES, LANES), BF16),
        ),
        in_specs=[vmem] * 4,
        out_specs=[hbm] * 4,
        scratch_shapes=[dma((4,))],
        compiler_params=pltpu.CompilerParams(vmem_limit_bytes=1024 * 1024),
    )(kl, gq, gw, gk)
    return kl.reshape(256), gq.reshape(256, PLANE * LANES), gw.T, gk.reshape(KEYS, LANES)


def solution(mesh):
    return jax.shard_map(
        local,
        mesh=mesh,
        in_specs=(
            P(None, "head"), P("seq", "head"), P(None, "head"), P(None, "head"),
            P("seq", None), P(None, "head"), P(), P("seq"),
        ),
        out_specs=(P(), P(None, "head"), P(None, "head"), P("seq", None)),
        check_vma=False,
    )
```

```python
import functools
import math

import jax
import jax.numpy as jnp
from jax import lax
from jax.experimental import pallas as pl
from jax.experimental.pallas import tpu as pltpu
from jax.sharding import PartitionSpec as P

MESH = pl.DeviceIdType.MESH
F32 = jnp.float32
BF16 = jnp.bfloat16

GROUPS = 4
PLANE = 16
ROWS = 64
HALF = 32
KEYS = 512
PAIRS = 16
WIDE = 192
LANES = 128
CHUNKS = 8
CHUNK_PAIRS = PAIRS // CHUNKS
CHUNK = CHUNK_PAIRS * 2 * WIDE
NT = (((1,), (1,)), ((), ()))
TN = (((0,), (0,)), ((), ()))
NN = (((1,), (0,)), ((), ()))
ROW_ORDER = (2, 1, 3, 0)
FAR_FIRST = tuple((dy, dx) for dy in ROW_ORDER for dx in (2, 1, 3, 0) if dy or dx)
ROWS_NEAR = (0, 1, 3, 2)
NEAR_FIRST = tuple((dy, dx) for dy in ROWS_NEAR for dx in (0, 1, 3, 2) if dy or dx)
LOG2E = math.log2(math.e)


def dot(a, b, dims):
    return lax.dot_general(a, b, dims, preferred_element_type=F32)


def body(
    qm, km, lse_h, qi, ki_h, hw_h, qpos_h, kb,
    kl_out, gq_out, gw_out, gk_out,
    qbuf, kbuf, acc, blk, att_s, att_r, qall, wall, kall, kbv, dots, wq, lacc, ebuf, abuf, dlb,
    st_all, st_two, g2, r2, g3, r3, qfin, prod, gwb, gk_s, gk_r, gk_p, gk_q,
    lse, wpack, hw, klb, lse_t, hw_t, qpos,
    small, ld, qloc, qz, wz, qx, kx, kvx, at, st1, st2, kls, d2, d3, d4, d4c, gws, gwc, gks, gkt, gkp,
):
    h = lax.axis_index("head")
    s = lax.axis_index("seq")
    core = s % 2
    zh = (s // 2) % 2
    yx = s // 4
    gy = yx // 4
    gx = yx % 4

    def seat(dy, dx):
        return ((gy + dy) % 4) * 4 + (gx + dx) % 4

    def at_plane(dy, dx, other_core=0):
        c = (core + other_core) % 2
        return (h, seat(dy, dx) * 4 + zh * 2 + c)

    def at_head(r, other_core=0, other_half=0):
        c = (core + other_core) % 2
        return ((h + r) % GROUPS, yx * 4 + ((zh + other_half) % 2) * 2 + c)

    partner = at_plane(0, 0, 1)

    def rc(src, dst, sems, dev, k=1):
        return pltpu.make_async_remote_copy(
            src_ref=src, dst_ref=dst, send_sem=sems.at[0], recv_sem=sems.at[k],
            device_id=dev, device_id_type=MESH,
        )

    def came(ref, sems, k=1):
        rc(ref, ref, sems, partner, k).wait_recv()

    sent = []

    def left_with(ref, sems):
        sent.append((ref, sems))

    bar = pltpu.get_barrier_semaphore()

    def hello(dev):
        pl.semaphore_signal(bar, inc=1, device_id=dev, device_id_type=MESH)

    for r in range(GROUPS):
        hello(at_head(r, 0, 1))
    for dy, dx in FAR_FIRST:
        hello(at_plane(dy, dx))
    for r in (3, 2, 1):
        hello(at_head(r, 1))
        hello(at_head(r))
    hello(partner)
    smalls = [
        pltpu.make_async_copy(src, dst, small.at[k])
        for k, (src, dst) in enumerate(
            ((lse_h, lse_t), (hw_h, hw_t), (ki_h, kall.at[0]), (qpos_h, qpos))
        )
    ]
    for c in smalls:
        c.start()

    def loop(lo, hi, f):
        def step(k, carry):
            f(k)
            return carry

        lax.fori_loop(lo, hi, step, 0)

    def chunk_copies(k):
        cols = pl.ds(pl.multiple_of(k * CHUNK, LANES), CHUNK)
        return (
            pltpu.make_async_copy(qm.at[:, cols], qbuf.at[:, cols], ld.at[0, k]),
            pltpu.make_async_copy(km.at[:, cols], kbuf.at[:, cols], ld.at[1, k]),
        )

    def start_chunk(k):
        for c in chunk_copies(k):
            c.start()

    loop(0, CHUNKS, start_chunk)

    def own_head(k):
        cols = pl.ds(pl.multiple_of(k * LANES, LANES), LANES)
        pltpu.make_async_copy(qi.at[h, core, :, cols], qall.at[0, k], qloc.at[0]).start()

    loop(0, PLANE, own_head)
    my_cols = pl.ds(pl.multiple_of(yx * LANES, LANES), LANES)
    fin_copy = pltpu.make_async_copy(qi.at[:, core, :, my_cols], qfin, qloc.at[1])
    fin_copy.start()

    for c in smalls:
        c.wait()
    for p in range(PAIRS):
        lse[p] = lse_t[2 * p:2 * p + 2, :] * LOG2E
    kbv[0] = jnp.full((1, LANES), kb[0] * KEYS, jnp.int32)
    group4 = lax.broadcasted_iota(jnp.int32, (4, LANES), 1) // HALF

    def moved(v, a, b):
        return v if a == b else pltpu.roll(v, ((a - b) * HALF) % LANES, 1)

    def side_by_side(parts, b, group):
        out = moved(parts[0], 0, b)
        for a in range(1, 4):
            out = jnp.where(group == a, moved(parts[a], a, b), out)
        return out

    for t in range(2):
        both = hw_t[:, t * LANES:(t + 1) * LANES]
        fours = [jnp.concatenate([both[4 * k + a:4 * k + a + 1] for k in range(4)], axis=0) for a in range(4)]
        for b in range(4):
            wpack[2 * t + b // 2, b % 2] = side_by_side(fours, b, group4)

    acc[...] = jnp.zeros_like(acc)
    scale = WIDE ** -0.5 * LOG2E

    def attend(k):
        for c in chunk_copies(k):
            c.wait()
        for j in range(CHUNK_PAIRS):
            pair = k * CHUNK_PAIRS + j
            base = pair * (2 * WIDE)
            lo = pl.ds(pl.multiple_of(base, LANES), 2 * LANES)
            hi = pl.ds(pl.multiple_of(base + LANES, LANES), 2 * LANES)
            lane = lax.broadcasted_iota(jnp.int32, (256, 2 * LANES), 1)
            q_a = jnp.where(lane < WIDE, qbuf[:, lo], 0).astype(BF16)
            q_b = jnp.where(lane >= 2 * LANES - WIDE, qbuf[:, hi], 0).astype(BF16)
            ls = lse[pair]
            s_a = dot(kbuf[:, lo], q_a, NT)
            s_b = dot(kbuf[:, hi], q_b, NT)
            acc[...] += jnp.exp2(s_a * scale - ls[0:1, :]) + jnp.exp2(s_b * scale - ls[1:2, :])

    loop(0, 4, attend)

    pl.semaphore_wait(bar, GROUPS + 15 + 6 + 1)
    wall[0] = wpack[h, core]
    for r in (3, 2, 1):
        g = (h + r) % GROUPS
        slot = GROUPS - r
        rc(qi.at[g, core, :, my_cols], qall.at[slot, yx], qz, at_head(r)).start()
        rc(wpack.at[g, core], wall.at[slot], wz, at_head(r)).start()
    left_with(qall.at[1:GROUPS, yx], qz)
    left_with(wall.at[1:GROUPS], wz)
    rc(ki_h, kall.at[1], kx, partner).start()
    rc(kbv.at[0], kbv.at[1], kvx, partner).start()
    left_with(kall.at[1], kx)
    left_with(kbv.at[1], kvx)

    loop(4, CHUNKS, attend)

    group = lax.broadcasted_iota(jnp.int32, (LANES, LANES), 1) // HALF
    for t in range(2):
        parts = [acc[q * LANES:(q + 1) * LANES, t * LANES:(t + 1) * LANES] for q in range(4)]
        for b in range(4):
            packed = side_by_side(parts, b, group)
            blk[2 * t + b // 2, b % 2] = packed
            att_s[2 * t + b // 2, b % 2] = packed.astype(BF16)

    for r in (3, 2, 1, 0):
        for k in range(2):
            if r or k:
                slot = k * 4 + (GROUPS - r) % GROUPS
                mine = att_s.at[(h + r) % GROUPS, (core + k) % 2]
                rc(mine, att_r.at[slot], at, at_head(r, k)).start()
    left_with(att_r.at[1:], at)

    came(qall.at[1:GROUPS, yx], qz)
    came(wall.at[1:GROUPS], wz)
    mine = qall.at[1:GROUPS, yx]
    for dy, dx in NEAR_FIRST:
        rc(mine, mine, qx, at_plane(dy, dx), 1 + dy).start()
    left_with(qall.at[1:GROUPS, 1:PLANE], qx)

    lacc[...] = jnp.zeros_like(lacc)

    def index_part(slots, k, n):
        wide = n * LANES
        qq = qall[slots, pl.ds(4 * k, 4 * n)].reshape(-1, LANES)
        d = dot(keys(), qq, NT)
        add = None
        for i, r in enumerate(range(GROUPS)[slots]):
            part = d[:, i * wide:(i + 1) * wide]
            cols = pl.ds(pl.multiple_of(r * 512 + k * LANES, LANES), wide)
            dots[:, cols] = part.astype(BF16)
            for j in range(n):
                w = wall[r, pl.ds(k + j, 1), :]
                term = w * jnp.maximum(part[:, j * LANES:(j + 1) * LANES], 0.0)
                add = term if add is None else add + term
        lacc[...] += add

    def keys():
        return kall[...].reshape(2 * KEYS, LANES)

    pltpu.make_async_copy(qall.at[0], qall.at[0], qloc.at[0]).wait()
    came(kall.at[1], kx)
    came(kbv.at[1], kvx)
    for k in (0, 2):
        index_part(slice(0, 1), k, 2)

    for dy in ROWS_NEAR:
        if dy == ROWS_NEAR[-1]:
            came(att_r.at[1:], at)
            for c in range(2):
                a = blk[h, core] if c == 0 else att_r[4].astype(F32)
                for r in range(1, GROUPS):
                    a += att_r[c * 4 + r].astype(F32)
                abuf[c] = a
        came(qall.at[1:GROUPS, 0:(4 if dy else 3)], qx, 1 + dy)
        index_part(slice(1, GROUPS), (gy + 4 - dy) % 4, 1)

    lane1 = lax.broadcasted_iota(jnp.int32, (1, LANES), 1) // HALF

    def spread(v, mask):
        v = jnp.where(mask, v, jnp.zeros_like(v))
        v = v + pltpu.roll(v, HALF, 1)
        return v + pltpu.roll(v, 2 * HALF, 1)

    limit = jnp.where(h < 2, qpos[:, :LANES], qpos[:, LANES:])
    limit = spread(limit, lane1 == (h % 2) * 2 + core)
    rowid = lax.broadcasted_iota(jnp.int32, (LANES, LANES), 0)

    def fold(v, op):
        v = op(v, pltpu.roll(v, 2 * HALF, 1))
        return op(v, pltpu.roll(v, HALF, 1))

    peak = None
    for c in range(2):
        logit = None
        for q in range(4):
            lg = fold(lacc[c * KEYS + q * LANES:c * KEYS + (q + 1) * LANES], jnp.add)
            logit = lg if q == 0 else jnp.where(group == q, lg, logit)
        ok = rowid + (kbv[c] + group * LANES) <= limit
        logit = jnp.where(ok, logit, -1e30)
        ebuf[c] = logit
        abuf[c] = jnp.where(ok, abuf[c], 0.0)
        top = jnp.max(logit, axis=0, keepdims=True)
        peak = top if c == 0 else jnp.maximum(peak, top)
    peak = fold(peak, jnp.maximum)
    norm = total = cross = jnp.zeros((1, LANES), F32)
    for c in range(2):
        ok = rowid + (kbv[c] + group * LANES) <= limit
        rel = ebuf[c] - peak
        e = jnp.where(ok, jnp.exp(rel), 0.0)
        ebuf[c] = e
        av = abuf[c]
        norm += jnp.sum(e, axis=0, keepdims=True)
        total += jnp.sum(av, axis=0, keepdims=True)
        cross += jnp.sum(
            jnp.where(ok, av * (jnp.log(jnp.where(ok, av, 1.0)) - rel), 0.0), axis=0, keepdims=True
        )
    norm, total, cross = (fold(v, jnp.add) for v in (norm, total, cross))
    tile = jnp.concatenate([peak, norm, total, cross], axis=0)
    st_all[yx] = tile

    mine = st_all.at[yx]
    for dy, dx in FAR_FIRST:
        rc(mine, mine, st1, at_plane(dy, dx)).start()
    left_with(st_all.at[1:], st1)

    hw[...] = jnp.transpose(hw_t[...]).reshape(GROUPS, 2, HALF, PLANE)

    wcol = jnp.transpose(wall[...].reshape(4 * 4, LANES))
    for r in range(GROUPS):
        for k in range(4):
            qq = qall[r, 4 * k:4 * k + 4].reshape(4 * HALF, LANES).astype(F32)
            n = r * 4 + k
            wq[n * LANES:(n + 1) * LANES] = (qq * wcol[:, n:n + 1]).astype(BF16)

    def merge(t):
        pk = jnp.max(t[:, 0, :], axis=0, keepdims=True)
        nm = jnp.sum(t[:, 1, :] * jnp.exp(t[:, 0, :] - pk), axis=0, keepdims=True)
        tt = jnp.sum(t[:, 2, :], axis=0, keepdims=True)
        cr = jnp.sum(t[:, 3, :] + t[:, 2, :] * (pk - t[:, 0, :]), axis=0, keepdims=True)
        return pk, nm, tt, cr

    came(st_all.at[1:], st1)
    st_two[0] = jnp.concatenate(merge(st_all[...]), axis=0)
    rc(st_two.at[0], st_two.at[1], st2, at_head(0, 0, 1)).start()
    left_with(st_two.at[0], st2)
    came(st_two.at[1], st2)
    peak_g, norm_g, total_g, cross_g = merge(st_two[...])
    inv_t = 1.0 / total_g
    kl = cross_g * inv_t - jnp.log(total_g) + jnp.log(norm_g)
    klb[2 * h + core] = kl
    mine = klb.at[2 * h + core]
    for r in (3, 2, 1, 0):
        for k in range(2):
            if r or k:
                rc(mine, mine, kls, at_head(r, k)).start()
    left_with(klb.at[1:], kls)

    grow = jnp.exp(peak - peak_g) / norm_g
    for c in range(2):
        packed = ebuf[c] * grow - abuf[c] * inv_t
        for q in range(4):
            dlb[c * KEYS + q * LANES:c * KEYS + (q + 1) * LANES] = spread(packed, group == q).astype(BF16)
    dl = dlb[...]
    dl2 = jnp.concatenate([dl, dl], axis=1)
    zero = jnp.zeros_like(dl2)

    for r in range(GROUPS):
        for q in range(2):
            lo = r * 512 + q * 2 * LANES
            g = jnp.where(dots[:, lo:lo + 2 * LANES] > 0, dl2, zero)
            dots[:, lo:lo + 2 * LANES] = g
            g2[r, 8 * q:8 * q + 8] = dot(g, keys(), TN).astype(BF16).reshape(8, HALF, LANES)
        for k, (dy, dx) in enumerate(FAR_FIRST):
            rc(g2.at[r, seat(dy, dx)], r2.at[r, k], d2, at_plane(dy, dx), 1 + r).start()
    left_with(r2.at[:, 0:15], d2)

    gk = jnp.zeros((2 * KEYS, LANES), F32)
    for r in range(GROUPS):
        gk += dot(dots[:, r * 512:(r + 1) * 512], wq[r * 512:(r + 1) * 512], NN)
    gk_p[...] = gk[KEYS:].astype(BF16)
    rc(gk_p, gk_q, gkp, partner).start()
    left_with(gk_p, gkp)
    gk_own = gk[:KEYS]

    for r in range(GROUPS):
        came(r2.at[r, 0:15], d2, 1 + r)
        tot = g2[r, yx].astype(F32)
        for p in range(PLANE - 1):
            tot += r2[r, p].astype(F32)
        g3[r] = tot.astype(BF16)
        for other in (1, 0):
            if r or other:
                rc(g3.at[r], r3.at[2 * r + other], d3, at_head(r, 0, other)).start()
    left_with(r3.at[1:], d3)
    came(gk_q, gkp)
    gk_s[...] = (gk_own + gk_q[...].astype(F32)).astype(BF16).reshape(4, LANES, LANES)
    for k in (3, 2, 1):
        rc(gk_s.at[(h + k) % GROUPS], gk_r.at[k], gks, at_head(k)).start()
    left_with(gk_s.at[1:GROUPS], gks)

    fin_copy.wait()
    came(r3.at[1:], d3)
    onehot = lax.broadcasted_iota(jnp.int32, (HALF, PLANE), 1) == yx
    for r in range(GROUPS):
        g = (h - r + GROUPS) % GROUPS
        near = g3[0] if r == 0 else r3[2 * r]
        full = near.astype(F32) + r3[2 * r + 1].astype(F32)
        w = jnp.sum(jnp.where(onehot, hw[g, core], 0.0), axis=1, keepdims=True)
        gq_out[g, core, :, my_cols] = (full * w).astype(BF16)
        prod[g] = full * qfin[g].astype(F32)

    first, last = gq_out.at[0:2, core, :, my_cols], gq_out.at[2:4, core, :, my_cols]
    for k in (2, 1, 3):
        rc(first, first, d4, at_plane(0, k), 1).start()
        rc(last, last, d4, at_plane(k, 0), 2).start()
    gw_row = jnp.sum(jnp.transpose(prod[...].reshape(LANES, LANES)), axis=0, keepdims=True)
    my_seat = core * PLANE + yx
    gwb[my_seat] = gw_row
    tile = gwb.at[my_seat]
    for dy, dx in FAR_FIRST:
        rc(tile, tile, gws, at_plane(dy, dx)).start()
    left_with(gwb.at[1:PLANE], gws)
    left_with(gq_out.at[:, core, :, LANES:], d4)

    def row_of(dy):
        cols = pl.ds(pl.multiple_of(((gy + 4 - dy) % 4) * 4 * LANES, LANES), 4 * LANES)
        return gq_out.at[0:2, core, :, cols]

    def column_of(dx):
        return [
            gq_out.at[2:4, core, :, pl.ds(pl.multiple_of((4 * k + (gx + 4 - dx) % 4) * LANES, LANES), LANES)]
            for k in range(4)
        ]

    def on(refs):
        for ref in refs:
            rc(ref, ref, d4c, partner).start()

    came(gq_out.at[0:2, core, :, 0:3 * LANES], d4, 1)
    for k in (2, 1, 3):
        rc(row_of(0), row_of(0), d4, at_plane(k, 0), 2 + k).start()
    came(gq_out.at[2:4, core, :, 0:3 * LANES], d4, 2)
    for k in (2, 1, 3):
        for ref in column_of(0):
            rc(ref, ref, d4, at_plane(0, k), 5 + k).start()
    on([row_of(0)])
    on(column_of(0))

    came(gk_r.at[1:GROUPS], gks)
    own = gk_s[h].astype(F32)
    for r in range(1, GROUPS):
        own += gk_r[r].astype(F32)
    gk_out[h] = own.astype(BF16)
    for r in (3, 2, 1):
        rc(gk_out.at[h], gk_out.at[h], gkt, at_head(r)).start()
    left_with(gk_out.at[1:GROUPS], gkt)

    for k in (1, 3, 2):
        if k == 2:
            came(gwb.at[1:PLANE], gws)
            tiles = gwb.at[pl.ds(core * PLANE, PLANE)]
            rc(tiles, tiles, gwc, partner).start()
            left_with(gwb.at[0:PLANE], gwc)
        came(row_of(k), d4, 2 + k)
        on([row_of(k)])
        came(gq_out.at[2:4, core, :, 0:4 * LANES], d4, 5 + k)
        on(column_of(k))
    left_with(gq_out.at[:, core], d4c)
    came(gwb.at[0:PLANE], gwc)
    came(klb.at[1:], kls)
    t0, t1 = gwb[0:PLANE, 0, :], gwb[PLANE:, 0, :]
    lane16 = lax.broadcasted_iota(jnp.int32, (PLANE, LANES), 1)
    for t in range(2):
        def back(v, n):
            return pltpu.roll(v, (n - t * ROWS) % LANES, 1)

        lo = jnp.where(lane16 < HALF, back(t0, 0), back(t1, HALF))
        up = jnp.where(lane16 < 3 * HALF, back(t0, HALF), back(t1, ROWS))
        gw_out[:, t * LANES:(t + 1) * LANES] = jnp.where(lane16 < ROWS, lo, up).astype(BF16)

    for t in range(2):
        pair = klb[4 * t]
        for b in range(1, 4):
            pair = jnp.where(lane1 == b, klb[4 * t + b], pair)
        kl_out[:, t * LANES:(t + 1) * LANES] = pair.astype(BF16)

    came(gk_out.at[1:GROUPS], gkt)
    came(gq_out.at[:, 1 - core], d4c)

    for ref, sems in sent:
        rc(ref, ref, sems, partner).wait_send()


def finish(a, b, c, d, a_out, b_out, c_out, d_out, sem):
    copies = [
        pltpu.make_async_copy(src, dst, sem.at[k])
        for k, (src, dst) in enumerate(((b, b_out), (d, d_out), (c, c_out)))
    ]
    for x in copies:
        x.start()
    a_out[...] = a[0, :]
    for x in copies:
        x.wait()


def local(query_mla, key_mla, lse, query_index, key_index, head_weight, query_pos, key_block):
    hbm = pl.BlockSpec(memory_space=pltpu.HBM)
    vmem = pl.BlockSpec(memory_space=pltpu.VMEM)
    dma = pltpu.SemaphoreType.DMA
    V = pltpu.VMEM
    kl, gq, gw, gk = pl.pallas_call(
        body,
        out_shape=(
            jax.ShapeDtypeStruct((1, 256), BF16),
            jax.ShapeDtypeStruct((GROUPS, 2, HALF, PLANE * LANES), BF16),
            jax.ShapeDtypeStruct((PLANE, 256), BF16),
            jax.ShapeDtypeStruct((GROUPS, LANES, LANES), BF16),
        ),
        in_specs=[hbm] * 7 + [pl.BlockSpec(memory_space=pltpu.SMEM)],
        out_specs=(vmem, vmem, vmem, vmem),
        scratch_shapes=[
            V((256, 6144), BF16), V((KEYS, 6144), BF16), V((KEYS, 256), F32),
            V((GROUPS, 2, LANES, LANES), F32), V((GROUPS, 2, LANES, LANES), BF16), V((8, LANES, LANES), BF16),
            V((GROUPS, PLANE, HALF, LANES), BF16), V((GROUPS, 4, LANES), F32),
            V((2, KEYS, LANES), BF16), V((2, 1, LANES), jnp.int32),
            V((2 * KEYS, 64 * HALF), BF16), V((64 * HALF, LANES), BF16), V((2 * KEYS, LANES), F32),
            V((2, LANES, LANES), F32), V((2, LANES, LANES), F32), V((2 * KEYS, LANES), BF16),
            V((PLANE, 4, LANES), F32), V((2, 4, LANES), F32),
            V((GROUPS, PLANE, HALF, LANES), BF16), V((GROUPS, PLANE, HALF, LANES), BF16),
            V((GROUPS, HALF, LANES), BF16), V((8, HALF, LANES), BF16),
            V((GROUPS, HALF, LANES), BF16), V((GROUPS, HALF, LANES), F32),
            V((2 * PLANE, 1, LANES), F32), V((GROUPS, LANES, LANES), BF16), V((GROUPS, LANES, LANES), BF16),
            V((KEYS, LANES), BF16), V((KEYS, LANES), BF16),
            V((PAIRS, 2, 256), F32), V((GROUPS, 2, 4, LANES), F32), V((GROUPS, 2, HALF, PLANE), F32), V((8, 1, LANES), F32),
            V((32, 256), F32), V((PLANE, 256), F32), V((1, 256), jnp.int32),
            dma((4,)), dma((2, CHUNKS)),
            dma((2,)), dma((2,)), dma((2,)), dma((5,)), dma((2,)), dma((2,)), dma((2,)), dma((2,)), dma((2,)), dma((2,)), dma((5,)), dma((2,)), dma((9,)), dma((2,)), dma((2,)), dma((2,)), dma((2,)), dma((2,)), dma((2,)),
        ],
        compiler_params=pltpu.CompilerParams(
            collective_id=0, has_side_effects=True, vmem_limit_bytes=50 * 1024 * 1024
        ),
    )(*(pltpu.with_memory_space_constraint(x, pltpu.HBM) for x in (
        query_mla, key_mla, lse.T, query_index.reshape(GROUPS, 2, HALF, PLANE * LANES), key_index,
        head_weight.T, query_pos.reshape(1, 256),
    )), key_block)
    kl, gq, gw, gk = pl.pallas_call(
        finish,
        out_shape=(
            jax.ShapeDtypeStruct((256,), BF16),
            jax.ShapeDtypeStruct((GROUPS, 2, HALF, PLANE * LANES), BF16),
            jax.ShapeDtypeStruct((PLANE, 256), BF16),
            jax.ShapeDtypeStruct((GROUPS, LANES, LANES), BF16),
        ),
        in_specs=[vmem] * 4,
        out_specs=[vmem] + [hbm] * 3,
        scratch_shapes=[dma((3,))],
        compiler_params=pltpu.CompilerParams(vmem_limit_bytes=1024 * 1024),
    )(kl, gq, gw, gk)
    return kl, gq.reshape(256, PLANE * LANES), gw.T, gk.reshape(KEYS, LANES)


def solution(mesh):
    return jax.shard_map(
        local,
        mesh=mesh,
        in_specs=(
            P(None, "head"), P("seq", "head"), P(None, "head"), P(None, "head"),
            P("seq", None), P(None, "head"), P(), P("seq"),
        ),
        out_specs=(P(), P(None, "head"), P(None, "head"), P("seq", None)),
        check_vma=False,
    )
```

```python
import functools
import math

import jax
import jax.numpy as jnp
from jax import lax
from jax.experimental import pallas as pl
from jax.experimental.pallas import tpu as pltpu
from jax.sharding import PartitionSpec as P

MESH = pl.DeviceIdType.MESH
F32 = jnp.float32
BF16 = jnp.bfloat16

GROUPS = 4
PLANE = 16
ROWS = 64
HALF = 32
KEYS = 512
PAIRS = 16
WIDE = 192
LANES = 128
CHUNKS = 8
CHUNK_PAIRS = PAIRS // CHUNKS
CHUNK = CHUNK_PAIRS * 2 * WIDE
NT = (((1,), (1,)), ((), ()))
TN = (((0,), (0,)), ((), ()))
NN = (((1,), (0,)), ((), ()))
ROW_ORDER = (2, 1, 3, 0)
FAR_FIRST = tuple((dy, dx) for dy in ROW_ORDER for dx in (2, 1, 3, 0) if dy or dx)
ROWS_NEAR = (0, 1, 3, 2)
NEAR_FIRST = tuple((dy, dx) for dy in ROWS_NEAR for dx in (0, 1, 3, 2) if dy or dx)
LOG2E = math.log2(math.e)


def dot(a, b, dims):
    return lax.dot_general(a, b, dims, preferred_element_type=F32)


def body(
    qm, km, lse_h, qi, ki_h, hw_h, qpos_h, kb,
    kl_out, gq_out, gw_out, gk_out,
    qbuf, kbuf, acc, blk, att_s, att_r, qall, wall, kall, kbv, dots, wq, lacc, ebuf, abuf, dlb,
    st_all, st_two, g2, r2, g3, r3, qfin, prod, gwb, gk_s, gk_r, gk_p, gk_q,
    lse, wpack, hw, klb, lse_t, hw_t, qpos, kt,
    small, ld, qloc, qz, wz, qx, kx, kvx, at, st1, st2, kls, d2, d3, d4, d4c, gws, gwc, gks, gkt, gkp,
):
    h = lax.axis_index("head")
    s = lax.axis_index("seq")
    core = s % 2
    zh = (s // 2) % 2
    yx = s // 4
    gy = yx // 4
    gx = yx % 4

    def seat(dy, dx):
        return ((gy + dy) % 4) * 4 + (gx + dx) % 4

    def at_plane(dy, dx, other_core=0):
        c = (core + other_core) % 2
        return (h, seat(dy, dx) * 4 + zh * 2 + c)

    def at_head(r, other_core=0, other_half=0):
        c = (core + other_core) % 2
        return ((h + r) % GROUPS, yx * 4 + ((zh + other_half) % 2) * 2 + c)

    partner = at_plane(0, 0, 1)

    def rc(src, dst, sems, dev, k=1):
        return pltpu.make_async_remote_copy(
            src_ref=src, dst_ref=dst, send_sem=sems.at[0], recv_sem=sems.at[k],
            device_id=dev, device_id_type=MESH,
        )

    def came(ref, sems, k=1):
        rc(ref, ref, sems, partner, k).wait_recv()

    sent = []

    def left_with(ref, sems):
        sent.append((ref, sems))

    bar = pltpu.get_barrier_semaphore()

    def hello(dev):
        pl.semaphore_signal(bar, inc=1, device_id=dev, device_id_type=MESH)

    for r in range(GROUPS):
        hello(at_head(r, 0, 1))
    for dy, dx in FAR_FIRST:
        hello(at_plane(dy, dx))
    for r in (3, 2, 1):
        hello(at_head(r, 1))
        hello(at_head(r))
    hello(partner)
    smalls = [
        pltpu.make_async_copy(src, dst, small.at[k])
        for k, (src, dst) in enumerate(
            ((lse_h, lse_t), (hw_h, hw_t), (ki_h, kall.at[0]), (qpos_h, qpos))
        )
    ]
    for c in smalls:
        c.start()

    def loop(lo, hi, f):
        def step(k, carry):
            f(k)
            return carry

        lax.fori_loop(lo, hi, step, 0)

    def chunk_copies(k):
        cols = pl.ds(pl.multiple_of(k * CHUNK, LANES), CHUNK)
        return (
            pltpu.make_async_copy(qm.at[:, cols], qbuf.at[:, cols], ld.at[0, k]),
            pltpu.make_async_copy(km.at[:, cols], kbuf.at[:, cols], ld.at[1, k]),
        )

    def start_chunk(k):
        for c in chunk_copies(k):
            c.start()

    loop(0, CHUNKS, start_chunk)

    def own_head(k):
        cols = pl.ds(pl.multiple_of(k * LANES, LANES), LANES)
        pltpu.make_async_copy(qi.at[h, core, :, cols], qall.at[0, k], qloc.at[0]).start()

    loop(0, PLANE, own_head)
    my_cols = pl.ds(pl.multiple_of(yx * LANES, LANES), LANES)
    fin_copy = pltpu.make_async_copy(qi.at[:, core, :, my_cols], qfin, qloc.at[1])
    fin_copy.start()

    for c in smalls:
        c.wait()
    for p in range(PAIRS):
        lse[p] = lse_t[2 * p:2 * p + 2, :] * LOG2E
    kbv[0] = jnp.full((1, LANES), kb[0] * KEYS, jnp.int32)
    group4 = lax.broadcasted_iota(jnp.int32, (4, LANES), 1) // HALF

    def moved(v, a, b):
        return v if a == b else pltpu.roll(v, ((a - b) * HALF) % LANES, 1)

    def side_by_side(parts, b, group):
        out = moved(parts[0], 0, b)
        for a in range(1, 4):
            out = jnp.where(group == a, moved(parts[a], a, b), out)
        return out

    for t in range(2):
        both = hw_t[:, t * LANES:(t + 1) * LANES]
        fours = [jnp.concatenate([both[4 * k + a:4 * k + a + 1] for k in range(4)], axis=0) for a in range(4)]
        for b in range(4):
            wpack[2 * t + b // 2, b % 2] = side_by_side(fours, b, group4)

    acc[...] = jnp.zeros_like(acc)
    scale = WIDE ** -0.5 * LOG2E

    def attend(k):
        for c in chunk_copies(k):
            c.wait()
        for j in range(CHUNK_PAIRS):
            pair = k * CHUNK_PAIRS + j
            base = pair * (2 * WIDE)
            lo = pl.ds(pl.multiple_of(base, LANES), 2 * LANES)
            hi = pl.ds(pl.multiple_of(base + LANES, LANES), 2 * LANES)
            lane = lax.broadcasted_iota(jnp.int32, (256, 2 * LANES), 1)
            q_a = jnp.where(lane < WIDE, qbuf[:, lo], 0).astype(BF16)
            q_b = jnp.where(lane >= 2 * LANES - WIDE, qbuf[:, hi], 0).astype(BF16)
            ls = lse[pair]
            s_a = dot(kbuf[:, lo], q_a, NT)
            s_b = dot(kbuf[:, hi], q_b, NT)
            acc[...] += jnp.exp2(s_a * scale - ls[0:1, :]) + jnp.exp2(s_b * scale - ls[1:2, :])

    loop(0, 4, attend)

    pl.semaphore_wait(bar, GROUPS + 15 + 6 + 1)
    wall[0] = wpack[h, core]
    for r in (3, 2, 1):
        g = (h + r) % GROUPS
        slot = GROUPS - r
        rc(qi.at[g, core, :, my_cols], qall.at[slot, yx], qz, at_head(r)).start()
        rc(wpack.at[g, core], wall.at[slot], wz, at_head(r)).start()
    left_with(qall.at[1:GROUPS, yx], qz)
    left_with(wall.at[1:GROUPS], wz)
    rc(ki_h, kall.at[1], kx, partner).start()
    rc(kbv.at[0], kbv.at[1], kvx, partner).start()
    left_with(kall.at[1], kx)
    left_with(kbv.at[1], kvx)

    loop(4, CHUNKS, attend)

    group = lax.broadcasted_iota(jnp.int32, (LANES, LANES), 1) // HALF
    for t in range(2):
        parts = [acc[q * LANES:(q + 1) * LANES, t * LANES:(t + 1) * LANES] for q in range(4)]
        for b in range(4):
            packed = side_by_side(parts, b, group)
            blk[2 * t + b // 2, b % 2] = packed
            att_s[2 * t + b // 2, b % 2] = packed.astype(BF16)

    for r in (3, 2, 1, 0):
        for k in range(2):
            if r or k:
                slot = k * 4 + (GROUPS - r) % GROUPS
                mine = att_s.at[(h + r) % GROUPS, (core + k) % 2]
                rc(mine, att_r.at[slot], at, at_head(r, k)).start()
    left_with(att_r.at[1:], at)

    came(qall.at[1:GROUPS, yx], qz)
    came(wall.at[1:GROUPS], wz)
    mine = qall.at[1:GROUPS, yx]
    for dy, dx in NEAR_FIRST:
        rc(mine, mine, qx, at_plane(dy, dx), 1 + dy).start()
    left_with(qall.at[1:GROUPS, 1:PLANE], qx)

    lacc[...] = jnp.zeros_like(lacc)

    def index_part(slots, k, n):
        wide = n * LANES
        qq = qall[slots, pl.ds(4 * k, 4 * n)].reshape(-1, LANES)
        d = dot(keys(), qq, NT)
        add = None
        for i, r in enumerate(range(GROUPS)[slots]):
            part = d[:, i * wide:(i + 1) * wide]
            cols = pl.ds(pl.multiple_of(r * 512 + k * LANES, LANES), wide)
            dots[:, cols] = part.astype(BF16)
            for j in range(n):
                w = wall[r, pl.ds(k + j, 1), :]
                term = w * jnp.maximum(part[:, j * LANES:(j + 1) * LANES], 0.0)
                add = term if add is None else add + term
        lacc[...] += add

    def keys():
        return kall[...].reshape(2 * KEYS, LANES)

    pltpu.make_async_copy(qall.at[0], qall.at[0], qloc.at[0]).wait()
    came(kall.at[1], kx)
    came(kbv.at[1], kvx)
    for k in (0, 2):
        index_part(slice(0, 1), k, 2)

    for dy in ROWS_NEAR:
        if dy == ROWS_NEAR[-1]:
            came(att_r.at[1:], at)
            for c in range(2):
                a = blk[h, core] if c == 0 else att_r[4].astype(F32)
                for r in range(1, GROUPS):
                    a += att_r[c * 4 + r].astype(F32)
                abuf[c] = a
        came(qall.at[1:GROUPS, 0:(4 if dy else 3)], qx, 1 + dy)
        index_part(slice(1, GROUPS), (gy + 4 - dy) % 4, 1)

    lane1 = lax.broadcasted_iota(jnp.int32, (1, LANES), 1) // HALF

    def spread(v, mask):
        v = jnp.where(mask, v, jnp.zeros_like(v))
        v = v + pltpu.roll(v, HALF, 1)
        return v + pltpu.roll(v, 2 * HALF, 1)

    limit = jnp.where(h < 2, qpos[:, :LANES], qpos[:, LANES:])
    limit = spread(limit, lane1 == (h % 2) * 2 + core)
    rowid = lax.broadcasted_iota(jnp.int32, (LANES, LANES), 0)

    def fold(v, op):
        v = op(v, pltpu.roll(v, 2 * HALF, 1))
        return op(v, pltpu.roll(v, HALF, 1))

    peak = None
    for c in range(2):
        logit = None
        for q in range(4):
            lg = fold(lacc[c * KEYS + q * LANES:c * KEYS + (q + 1) * LANES], jnp.add)
            logit = lg if q == 0 else jnp.where(group == q, lg, logit)
        ok = rowid + (kbv[c] + group * LANES) <= limit
        logit = jnp.where(ok, logit, -1e30)
        ebuf[c] = logit
        abuf[c] = jnp.where(ok, abuf[c], 0.0)
        top = jnp.max(logit, axis=0, keepdims=True)
        peak = top if c == 0 else jnp.maximum(peak, top)
    peak = fold(peak, jnp.maximum)
    norm = total = cross = jnp.zeros((1, LANES), F32)
    for c in range(2):
        ok = rowid + (kbv[c] + group * LANES) <= limit
        rel = ebuf[c] - peak
        e = jnp.where(ok, jnp.exp(rel), 0.0)
        ebuf[c] = e
        av = abuf[c]
        norm += jnp.sum(e, axis=0, keepdims=True)
        total += jnp.sum(av, axis=0, keepdims=True)
        cross += jnp.sum(
            jnp.where(ok, av * (jnp.log(jnp.where(ok, av, 1.0)) - rel), 0.0), axis=0, keepdims=True
        )
    norm, total, cross = (fold(v, jnp.add) for v in (norm, total, cross))
    tile = jnp.concatenate([peak, norm, total, cross], axis=0)
    st_all[yx] = tile

    mine = st_all.at[yx]
    for dy, dx in FAR_FIRST:
        rc(mine, mine, st1, at_plane(dy, dx)).start()
    left_with(st_all.at[1:], st1)

    kt[...] = jnp.transpose(keys())
    hw[...] = jnp.transpose(hw_t[...]).reshape(GROUPS, 2, HALF, PLANE)

    wcol = jnp.transpose(wall[...].reshape(4 * 4, LANES))
    for r in range(GROUPS):
        for k in range(4):
            qq = qall[r, 4 * k:4 * k + 4].reshape(4 * HALF, LANES).astype(F32)
            n = r * 4 + k
            wq[n * LANES:(n + 1) * LANES] = (qq * wcol[:, n:n + 1]).astype(BF16)

    def merge(t):
        pk = jnp.max(t[:, 0, :], axis=0, keepdims=True)
        nm = jnp.sum(t[:, 1, :] * jnp.exp(t[:, 0, :] - pk), axis=0, keepdims=True)
        tt = jnp.sum(t[:, 2, :], axis=0, keepdims=True)
        cr = jnp.sum(t[:, 3, :] + t[:, 2, :] * (pk - t[:, 0, :]), axis=0, keepdims=True)
        return pk, nm, tt, cr

    came(st_all.at[1:], st1)
    st_two[0] = jnp.concatenate(merge(st_all[...]), axis=0)
    rc(st_two.at[0], st_two.at[1], st2, at_head(0, 0, 1)).start()
    left_with(st_two.at[0], st2)
    came(st_two.at[1], st2)
    peak_g, norm_g, total_g, cross_g = merge(st_two[...])
    inv_t = 1.0 / total_g
    kl = cross_g * inv_t - jnp.log(total_g) + jnp.log(norm_g)
    klb[2 * h + core] = kl
    mine = klb.at[2 * h + core]
    for r in (3, 2, 1, 0):
        for k in range(2):
            if r or k:
                rc(mine, mine, kls, at_head(r, k)).start()
    left_with(klb.at[1:], kls)

    grow = jnp.exp(peak - peak_g) / norm_g
    for c in range(2):
        packed = ebuf[c] * grow - abuf[c] * inv_t
        for q in range(4):
            dlb[c * KEYS + q * LANES:c * KEYS + (q + 1) * LANES] = spread(packed, group == q).astype(BF16)
    dl = dlb[...]
    dl2 = jnp.concatenate([dl, dl], axis=1)
    zero = jnp.zeros_like(dl2)

    for r in range(GROUPS):
        for q in range(2):
            lo = r * 512 + q * 2 * LANES
            g = jnp.where(dots[:, lo:lo + 2 * LANES] > 0, dl2, zero)
            dots[:, lo:lo + 2 * LANES] = g
            g2[r, 8 * q:8 * q + 8] = jnp.transpose(dot(kt[...], g, NN)).astype(BF16).reshape(8, HALF, LANES)
        for k, (dy, dx) in enumerate(FAR_FIRST):
            rc(g2.at[r, seat(dy, dx)], r2.at[r, k], d2, at_plane(dy, dx), 1 + r).start()
    left_with(r2.at[:, 0:15], d2)

    gk = jnp.zeros((2 * KEYS, LANES), F32)
    for r in range(GROUPS):
        gk += dot(dots[:, r * 512:(r + 1) * 512], wq[r * 512:(r + 1) * 512], NN)
    gk_p[...] = gk[KEYS:].astype(BF16)
    rc(gk_p, gk_q, gkp, partner).start()
    left_with(gk_p, gkp)
    gk_own = gk[:KEYS]

    for r in range(GROUPS):
        came(r2.at[r, 0:15], d2, 1 + r)
        tot = g2[r, yx].astype(F32)
        for p in range(PLANE - 1):
            tot += r2[r, p].astype(F32)
        g3[r] = tot.astype(BF16)
        for other in (1, 0):
            if r or other:
                rc(g3.at[r], r3.at[2 * r + other], d3, at_head(r, 0, other)).start()
    left_with(r3.at[1:], d3)
    came(gk_q, gkp)
    gk_s[...] = (gk_own + gk_q[...].astype(F32)).astype(BF16).reshape(4, LANES, LANES)
    for k in (3, 2, 1):
        rc(gk_s.at[(h + k) % GROUPS], gk_r.at[k], gks, at_head(k)).start()
    left_with(gk_s.at[1:GROUPS], gks)

    fin_copy.wait()
    came(r3.at[1:], d3)
    onehot = lax.broadcasted_iota(jnp.int32, (HALF, PLANE), 1) == yx
    for r in range(GROUPS):
        g = (h - r + GROUPS) % GROUPS
        near = g3[0] if r == 0 else r3[2 * r]
        full = near.astype(F32) + r3[2 * r + 1].astype(F32)
        w = jnp.sum(jnp.where(onehot, hw[g, core], 0.0), axis=1, keepdims=True)
        gq_out[g, core, :, my_cols] = (full * w).astype(BF16)
        prod[g] = full * qfin[g].astype(F32)

    first, last = gq_out.at[0:2, core, :, my_cols], gq_out.at[2:4, core, :, my_cols]
    for k in (2, 1, 3):
        rc(first, first, d4, at_plane(0, k), 1).start()
        rc(last, last, d4, at_plane(k, 0), 2).start()
    gw_row = jnp.sum(jnp.transpose(prod[...].reshape(LANES, LANES)), axis=0, keepdims=True)
    my_seat = core * PLANE + yx
    gwb[my_seat] = gw_row
    tile = gwb.at[my_seat]
    for dy, dx in FAR_FIRST:
        rc(tile, tile, gws, at_plane(dy, dx)).start()
    left_with(gwb.at[1:PLANE], gws)
    left_with(gq_out.at[:, core, :, LANES:], d4)

    def row_of(dy):
        cols = pl.ds(pl.multiple_of(((gy + 4 - dy) % 4) * 4 * LANES, LANES), 4 * LANES)
        return gq_out.at[0:2, core, :, cols]

    def column_of(dx):
        return [
            gq_out.at[2:4, core, :, pl.ds(pl.multiple_of((4 * k + (gx + 4 - dx) % 4) * LANES, LANES), LANES)]
            for k in range(4)
        ]

    def on(refs):
        for ref in refs:
            rc(ref, ref, d4c, partner).start()

    came(gq_out.at[0:2, core, :, 0:3 * LANES], d4, 1)
    for k in (2, 1, 3):
        rc(row_of(0), row_of(0), d4, at_plane(k, 0), 2 + k).start()
    came(gq_out.at[2:4, core, :, 0:3 * LANES], d4, 2)
    for k in (2, 1, 3):
        for ref in column_of(0):
            rc(ref, ref, d4, at_plane(0, k), 5 + k).start()
    on([row_of(0)])
    on(column_of(0))

    came(gk_r.at[1:GROUPS], gks)
    own = gk_s[h].astype(F32)
    for r in range(1, GROUPS):
        own += gk_r[r].astype(F32)
    gk_out[h] = own.astype(BF16)
    for r in (3, 2, 1):
        rc(gk_out.at[h], gk_out.at[h], gkt, at_head(r)).start()
    left_with(gk_out.at[1:GROUPS], gkt)

    for k in (1, 3, 2):
        if k == 2:
            came(gwb.at[1:PLANE], gws)
            tiles = gwb.at[pl.ds(core * PLANE, PLANE)]
            rc(tiles, tiles, gwc, partner).start()
            left_with(gwb.at[0:PLANE], gwc)
        came(row_of(k), d4, 2 + k)
        on([row_of(k)])
        came(gq_out.at[2:4, core, :, 0:4 * LANES], d4, 5 + k)
        on(column_of(k))
    left_with(gq_out.at[:, core], d4c)
    came(gwb.at[0:PLANE], gwc)
    came(klb.at[1:], kls)
    t0, t1 = gwb[0:PLANE, 0, :], gwb[PLANE:, 0, :]
    lane16 = lax.broadcasted_iota(jnp.int32, (PLANE, LANES), 1)
    for t in range(2):
        def back(v, n):
            return pltpu.roll(v, (n - t * ROWS) % LANES, 1)

        lo = jnp.where(lane16 < HALF, back(t0, 0), back(t1, HALF))
        up = jnp.where(lane16 < 3 * HALF, back(t0, HALF), back(t1, ROWS))
        gw_out[:, t * LANES:(t + 1) * LANES] = jnp.where(lane16 < ROWS, lo, up).astype(BF16)

    for t in range(2):
        pair = klb[4 * t]
        for b in range(1, 4):
            pair = jnp.where(lane1 == b, klb[4 * t + b], pair)
        kl_out[:, t * LANES:(t + 1) * LANES] = pair.astype(BF16)

    came(gk_out.at[1:GROUPS], gkt)
    came(gq_out.at[:, 1 - core], d4c)

    for ref, sems in sent:
        rc(ref, ref, sems, partner).wait_send()


def finish(a, b, c, d, a_out, b_out, c_out, d_out, line, sem):
    copies = [
        pltpu.make_async_copy(src, dst, sem.at[k])
        for k, (src, dst) in enumerate(((b, b_out), (d, d_out), (c, c_out), (line, a_out)))
    ]
    for x in copies[:3]:
        x.start()
    line[...] = a[0, :]
    copies[3].start()
    for x in copies:
        x.wait()


def local(query_mla, key_mla, lse, query_index, key_index, head_weight, query_pos, key_block):
    hbm = pl.BlockSpec(memory_space=pltpu.HBM)
    vmem = pl.BlockSpec(memory_space=pltpu.VMEM)
    dma = pltpu.SemaphoreType.DMA
    V = pltpu.VMEM
    kl, gq, gw, gk = pl.pallas_call(
        body,
        out_shape=(
            jax.ShapeDtypeStruct((1, 256), BF16),
            jax.ShapeDtypeStruct((GROUPS, 2, HALF, PLANE * LANES), BF16),
            jax.ShapeDtypeStruct((PLANE, 256), BF16),
            jax.ShapeDtypeStruct((GROUPS, LANES, LANES), BF16),
        ),
        in_specs=[hbm] * 7 + [pl.BlockSpec(memory_space=pltpu.SMEM)],
        out_specs=(vmem, vmem, vmem, vmem),
        scratch_shapes=[
            V((256, 6144), BF16), V((KEYS, 6144), BF16), V((KEYS, 256), F32),
            V((GROUPS, 2, LANES, LANES), F32), V((GROUPS, 2, LANES, LANES), BF16), V((8, LANES, LANES), BF16),
            V((GROUPS, PLANE, HALF, LANES), BF16), V((GROUPS, 4, LANES), F32),
            V((2, KEYS, LANES), BF16), V((2, 1, LANES), jnp.int32),
            V((2 * KEYS, 64 * HALF), BF16), V((64 * HALF, LANES), BF16), V((2 * KEYS, LANES), F32),
            V((2, LANES, LANES), F32), V((2, LANES, LANES), F32), V((2 * KEYS, LANES), BF16),
            V((PLANE, 4, LANES), F32), V((2, 4, LANES), F32),
            V((GROUPS, PLANE, HALF, LANES), BF16), V((GROUPS, PLANE, HALF, LANES), BF16),
            V((GROUPS, HALF, LANES), BF16), V((8, HALF, LANES), BF16),
            V((GROUPS, HALF, LANES), BF16), V((GROUPS, HALF, LANES), F32),
            V((2 * PLANE, 1, LANES), F32), V((GROUPS, LANES, LANES), BF16), V((GROUPS, LANES, LANES), BF16),
            V((KEYS, LANES), BF16), V((KEYS, LANES), BF16),
            V((PAIRS, 2, 256), F32), V((GROUPS, 2, 4, LANES), F32), V((GROUPS, 2, HALF, PLANE), F32), V((8, 1, LANES), F32),
            V((32, 256), F32), V((PLANE, 256), F32), V((1, 256), jnp.int32), V((LANES, 2 * KEYS), BF16),
            dma((4,)), dma((2, CHUNKS)),
            dma((2,)), dma((2,)), dma((2,)), dma((5,)), dma((2,)), dma((2,)), dma((2,)), dma((2,)), dma((2,)), dma((2,)), dma((5,)), dma((2,)), dma((9,)), dma((2,)), dma((2,)), dma((2,)), dma((2,)), dma((2,)), dma((2,)),
        ],
        compiler_params=pltpu.CompilerParams(
            collective_id=0, has_side_effects=True, vmem_limit_bytes=50 * 1024 * 1024
        ),
    )(*(pltpu.with_memory_space_constraint(x, pltpu.HBM) for x in (
        query_mla, key_mla, lse.T, query_index.reshape(GROUPS, 2, HALF, PLANE * LANES), key_index,
        head_weight.T, query_pos.reshape(1, 256),
    )), key_block)
    kl, gq, gw, gk = pl.pallas_call(
        finish,
        out_shape=(
            jax.ShapeDtypeStruct((256,), BF16),
            jax.ShapeDtypeStruct((GROUPS, 2, HALF, PLANE * LANES), BF16),
            jax.ShapeDtypeStruct((PLANE, 256), BF16),
            jax.ShapeDtypeStruct((GROUPS, LANES, LANES), BF16),
        ),
        in_specs=[vmem] * 4,
        out_specs=[hbm] * 4,
        scratch_shapes=[V((256,), BF16), dma((4,))],
        compiler_params=pltpu.CompilerParams(vmem_limit_bytes=1024 * 1024),
    )(kl, gq, gw, gk)
    return kl, gq.reshape(256, PLANE * LANES), gw.T, gk.reshape(KEYS, LANES)


def solution(mesh):
    return jax.shard_map(
        local,
        mesh=mesh,
        in_specs=(
            P(None, "head"), P("seq", "head"), P(None, "head"), P(None, "head"),
            P("seq", None), P(None, "head"), P(), P("seq"),
        ),
        out_specs=(P(), P(None, "head"), P(None, "head"), P("seq", None)),
        check_vma=False,
    )
```

```python
import functools
import math

import jax
import jax.numpy as jnp
from jax import lax
from jax.experimental import pallas as pl
from jax.experimental.pallas import tpu as pltpu
from jax.sharding import PartitionSpec as P

MESH = pl.DeviceIdType.MESH
F32 = jnp.float32
BF16 = jnp.bfloat16

GROUPS = 4
PLANE = 16
ROWS = 64
HALF = 32
KEYS = 512
PAIRS = 16
WIDE = 192
LANES = 128
CHUNKS = 8
CHUNK_PAIRS = PAIRS // CHUNKS
CHUNK = CHUNK_PAIRS * 2 * WIDE
NT = (((1,), (1,)), ((), ()))
TN = (((0,), (0,)), ((), ()))
NN = (((1,), (0,)), ((), ()))
ROW_ORDER = (2, 1, 3, 0)
FAR_FIRST = tuple((dy, dx) for dy in ROW_ORDER for dx in (2, 1, 3, 0) if dy or dx)
ROWS_NEAR = (0, 1, 3, 2)
NEAR_FIRST = tuple((dy, dx) for dy in ROWS_NEAR for dx in (0, 1, 3, 2) if dy or dx)
LOG2E = math.log2(math.e)


def dot(a, b, dims):
    return lax.dot_general(a, b, dims, preferred_element_type=F32)


def body(
    qm, km, lse_h, qi, ki_h, hw_h, qpos_h, kb,
    kl_out, gq_out, gw_out, gk_out,
    qbuf, kbuf, acc, blk, att_s, att_r, qall, wall, kall, kbv, dots, wq, lacc, ebuf, abuf, dlb,
    st_all, st_two, g2, r2, gh, rh, g3, r3, qfin, prod, gwb, gk_s, gk_r, gk_p, gk_q,
    lse, wpack, hw, klb, lse_t, hw_t, qpos, kt,
    small, ld, qloc, qz, wz, qx, kx, kvx, at, st1, st2, kls, d2, dh, d3, d4, d4c, gws, gwc, gks, gkt, gkp,
):
    h = lax.axis_index("head")
    s = lax.axis_index("seq")
    core = s % 2
    zh = (s // 2) % 2
    yx = s // 4
    gy = yx // 4
    gx = yx % 4

    def seat(dy, dx):
        return ((gy + dy) % 4) * 4 + (gx + dx) % 4

    def at_plane(dy, dx, other_core=0):
        c = (core + other_core) % 2
        return (h, seat(dy, dx) * 4 + zh * 2 + c)

    def at_head(r, other_core=0, other_half=0):
        c = (core + other_core) % 2
        return ((h + r) % GROUPS, yx * 4 + ((zh + other_half) % 2) * 2 + c)

    partner = at_plane(0, 0, 1)

    def rc(src, dst, sems, dev, k=1):
        return pltpu.make_async_remote_copy(
            src_ref=src, dst_ref=dst, send_sem=sems.at[0], recv_sem=sems.at[k],
            device_id=dev, device_id_type=MESH,
        )

    def came(ref, sems, k=1):
        rc(ref, ref, sems, partner, k).wait_recv()

    sent = []

    def left_with(ref, sems):
        sent.append((ref, sems))

    bar = pltpu.get_barrier_semaphore()

    def hello(dev):
        pl.semaphore_signal(bar, inc=1, device_id=dev, device_id_type=MESH)

    for r in range(GROUPS):
        hello(at_head(r, 0, 1))
    for dy, dx in FAR_FIRST:
        hello(at_plane(dy, dx))
    for r in (3, 2, 1):
        hello(at_head(r, 1))
        hello(at_head(r))
    hello(partner)
    smalls = [
        pltpu.make_async_copy(src, dst, small.at[k])
        for k, (src, dst) in enumerate(
            ((lse_h, lse_t), (hw_h, hw_t), (ki_h, kall.at[0]), (qpos_h, qpos))
        )
    ]
    for c in smalls:
        c.start()

    def loop(lo, hi, f):
        def step(k, carry):
            f(k)
            return carry

        lax.fori_loop(lo, hi, step, 0)

    def chunk_copies(k):
        cols = pl.ds(pl.multiple_of(k * CHUNK, LANES), CHUNK)
        return (
            pltpu.make_async_copy(qm.at[:, cols], qbuf.at[:, cols], ld.at[0, k]),
            pltpu.make_async_copy(km.at[:, cols], kbuf.at[:, cols], ld.at[1, k]),
        )

    def start_chunk(k):
        for c in chunk_copies(k):
            c.start()

    loop(0, CHUNKS, start_chunk)

    def own_head(k):
        cols = pl.ds(pl.multiple_of(k * LANES, LANES), LANES)
        pltpu.make_async_copy(qi.at[h, core, :, cols], qall.at[0, k], qloc.at[0]).start()

    loop(0, PLANE, own_head)
    my_cols = pl.ds(pl.multiple_of(yx * LANES, LANES), LANES)
    fin_copy = pltpu.make_async_copy(qi.at[:, core, :, my_cols], qfin, qloc.at[1])
    fin_copy.start()

    for c in smalls:
        c.wait()
    for p in range(PAIRS):
        lse[p] = lse_t[2 * p:2 * p + 2, :] * LOG2E
    kbv[0] = jnp.full((1, LANES), kb[0] * KEYS, jnp.int32)
    group4 = lax.broadcasted_iota(jnp.int32, (4, LANES), 1) // HALF

    def moved(v, a, b):
        return v if a == b else pltpu.roll(v, ((a - b) * HALF) % LANES, 1)

    def side_by_side(parts, b, group):
        out = moved(parts[0], 0, b)
        for a in range(1, 4):
            out = jnp.where(group == a, moved(parts[a], a, b), out)
        return out

    for t in range(2):
        both = hw_t[:, t * LANES:(t + 1) * LANES]
        fours = [jnp.concatenate([both[4 * k + a:4 * k + a + 1] for k in range(4)], axis=0) for a in range(4)]
        for b in range(4):
            wpack[2 * t + b // 2, b % 2] = side_by_side(fours, b, group4)

    acc[...] = jnp.zeros_like(acc)
    scale = WIDE ** -0.5 * LOG2E

    def attend(k):
        for c in chunk_copies(k):
            c.wait()
        for j in range(CHUNK_PAIRS):
            pair = k * CHUNK_PAIRS + j
            base = pair * (2 * WIDE)
            lo = pl.ds(pl.multiple_of(base, LANES), 2 * LANES)
            hi = pl.ds(pl.multiple_of(base + LANES, LANES), 2 * LANES)
            lane = lax.broadcasted_iota(jnp.int32, (256, 2 * LANES), 1)
            q_a = jnp.where(lane < WIDE, qbuf[:, lo], 0).astype(BF16)
            q_b = jnp.where(lane >= 2 * LANES - WIDE, qbuf[:, hi], 0).astype(BF16)
            ls = lse[pair]
            s_a = dot(kbuf[:, lo], q_a, NT)
            s_b = dot(kbuf[:, hi], q_b, NT)
            acc[...] += jnp.exp2(s_a * scale - ls[0:1, :]) + jnp.exp2(s_b * scale - ls[1:2, :])

    loop(0, 4, attend)

    pl.semaphore_wait(bar, GROUPS + 15 + 6 + 1)
    wall[0] = wpack[h, core]
    for r in (3, 2, 1):
        g = (h + r) % GROUPS
        slot = GROUPS - r
        rc(qi.at[g, core, :, my_cols], qall.at[slot, yx], qz, at_head(r)).start()
        rc(wpack.at[g, core], wall.at[slot], wz, at_head(r)).start()
    left_with(qall.at[1:GROUPS, yx], qz)
    left_with(wall.at[1:GROUPS], wz)
    rc(ki_h, kall.at[1], kx, partner).start()
    rc(kbv.at[0], kbv.at[1], kvx, partner).start()
    left_with(kall.at[1], kx)
    left_with(kbv.at[1], kvx)

    loop(4, CHUNKS, attend)

    group = lax.broadcasted_iota(jnp.int32, (LANES, LANES), 1) // HALF
    for t in range(2):
        parts = [acc[q * LANES:(q + 1) * LANES, t * LANES:(t + 1) * LANES] for q in range(4)]
        for b in range(4):
            packed = side_by_side(parts, b, group)
            blk[2 * t + b // 2, b % 2] = packed
            att_s[2 * t + b // 2, b % 2] = packed.astype(BF16)

    for r in (3, 2, 1, 0):
        for k in range(2):
            if r or k:
                slot = k * 4 + (GROUPS - r) % GROUPS
                mine = att_s.at[(h + r) % GROUPS, (core + k) % 2]
                rc(mine, att_r.at[slot], at, at_head(r, k)).start()
    left_with(att_r.at[1:], at)

    came(qall.at[1:GROUPS, yx], qz)
    came(wall.at[1:GROUPS], wz)
    mine = qall.at[1:GROUPS, yx]
    for dy, dx in NEAR_FIRST:
        rc(mine, mine, qx, at_plane(dy, dx), 1 + dy).start()
    left_with(qall.at[1:GROUPS, 1:PLANE], qx)

    lacc[...] = jnp.zeros_like(lacc)

    def index_part(slots, k, n):
        wide = n * LANES
        qq = qall[slots, pl.ds(4 * k, 4 * n)].reshape(-1, LANES)
        d = dot(keys(), qq, NT)
        add = None
        for i, r in enumerate(range(GROUPS)[slots]):
            part = d[:, i * wide:(i + 1) * wide]
            cols = pl.ds(pl.multiple_of(r * 512 + k * LANES, LANES), wide)
            dots[:, cols] = part.astype(BF16)
            for j in range(n):
                w = wall[r, pl.ds(k + j, 1), :]
                term = w * jnp.maximum(part[:, j * LANES:(j + 1) * LANES], 0.0)
                add = term if add is None else add + term
        lacc[...] += add

    def keys():
        return kall[...].reshape(2 * KEYS, LANES)

    pltpu.make_async_copy(qall.at[0], qall.at[0], qloc.at[0]).wait()
    came(kall.at[1], kx)
    came(kbv.at[1], kvx)
    for k in (0, 2):
        index_part(slice(0, 1), k, 2)

    for dy in ROWS_NEAR:
        if dy == ROWS_NEAR[-1]:
            came(att_r.at[1:], at)
            for c in range(2):
                a = blk[h, core] if c == 0 else att_r[4].astype(F32)
                for r in range(1, GROUPS):
                    a += att_r[c * 4 + r].astype(F32)
                abuf[c] = a
        came(qall.at[1:GROUPS, 0:(4 if dy else 3)], qx, 1 + dy)
        index_part(slice(1, GROUPS), (gy + 4 - dy) % 4, 1)

    lane1 = lax.broadcasted_iota(jnp.int32, (1, LANES), 1) // HALF

    def spread(v, mask):
        v = jnp.where(mask, v, jnp.zeros_like(v))
        v = v + pltpu.roll(v, HALF, 1)
        return v + pltpu.roll(v, 2 * HALF, 1)

    limit = jnp.where(h < 2, qpos[:, :LANES], qpos[:, LANES:])
    limit = spread(limit, lane1 == (h % 2) * 2 + core)
    rowid = lax.broadcasted_iota(jnp.int32, (LANES, LANES), 0)

    def fold(v, op):
        v = op(v, pltpu.roll(v, 2 * HALF, 1))
        return op(v, pltpu.roll(v, HALF, 1))

    peak = None
    for c in range(2):
        logit = None
        for q in range(4):
            lg = fold(lacc[c * KEYS + q * LANES:c * KEYS + (q + 1) * LANES], jnp.add)
            logit = lg if q == 0 else jnp.where(group == q, lg, logit)
        ok = rowid + (kbv[c] + group * LANES) <= limit
        logit = jnp.where(ok, logit, -1e30)
        ebuf[c] = logit
        abuf[c] = jnp.where(ok, abuf[c], 0.0)
        top = jnp.max(logit, axis=0, keepdims=True)
        peak = top if c == 0 else jnp.maximum(peak, top)
    peak = fold(peak, jnp.maximum)
    norm = total = cross = jnp.zeros((1, LANES), F32)
    for c in range(2):
        ok = rowid + (kbv[c] + group * LANES) <= limit
        rel = ebuf[c] - peak
        e = jnp.where(ok, jnp.exp(rel), 0.0)
        ebuf[c] = e
        av = abuf[c]
        norm += jnp.sum(e, axis=0, keepdims=True)
        total += jnp.sum(av, axis=0, keepdims=True)
        cross += jnp.sum(
            jnp.where(ok, av * (jnp.log(jnp.where(ok, av, 1.0)) - rel), 0.0), axis=0, keepdims=True
        )
    norm, total, cross = (fold(v, jnp.add) for v in (norm, total, cross))
    tile = jnp.concatenate([peak, norm, total, cross], axis=0)
    st_all[yx] = tile

    mine = st_all.at[yx]
    for dy, dx in FAR_FIRST:
        rc(mine, mine, st1, at_plane(dy, dx)).start()
    left_with(st_all.at[1:], st1)

    kt[...] = jnp.transpose(keys())
    hw[...] = jnp.transpose(hw_t[...]).reshape(GROUPS, 2, HALF, PLANE)

    wcol = jnp.transpose(wall[...].reshape(4 * 4, LANES))
    for r in range(GROUPS):
        for k in range(4):
            qq = qall[r, 4 * k:4 * k + 4].reshape(4 * HALF, LANES).astype(F32)
            n = r * 4 + k
            wq[n * LANES:(n + 1) * LANES] = (qq * wcol[:, n:n + 1]).astype(BF16)

    def merge(t):
        pk = jnp.max(t[:, 0, :], axis=0, keepdims=True)
        nm = jnp.sum(t[:, 1, :] * jnp.exp(t[:, 0, :] - pk), axis=0, keepdims=True)
        tt = jnp.sum(t[:, 2, :], axis=0, keepdims=True)
        cr = jnp.sum(t[:, 3, :] + t[:, 2, :] * (pk - t[:, 0, :]), axis=0, keepdims=True)
        return pk, nm, tt, cr

    came(st_all.at[1:], st1)
    st_two[0] = jnp.concatenate(merge(st_all[...]), axis=0)
    rc(st_two.at[0], st_two.at[1], st2, at_head(0, 0, 1)).start()
    left_with(st_two.at[0], st2)
    came(st_two.at[1], st2)
    peak_g, norm_g, total_g, cross_g = merge(st_two[...])
    inv_t = 1.0 / total_g
    kl = cross_g * inv_t - jnp.log(total_g) + jnp.log(norm_g)
    klb[2 * h + core] = kl
    mine = klb.at[2 * h + core]
    for r in (3, 2, 1, 0):
        for k in range(2):
            if r or k:
                rc(mine, mine, kls, at_head(r, k)).start()
    left_with(klb.at[1:], kls)

    grow = jnp.exp(peak - peak_g) / norm_g
    for c in range(2):
        packed = ebuf[c] * grow - abuf[c] * inv_t
        for q in range(4):
            dlb[c * KEYS + q * LANES:c * KEYS + (q + 1) * LANES] = spread(packed, group == q).astype(BF16)
    dl = dlb[...]
    dl2 = jnp.concatenate([dl, dl], axis=1)
    zero = jnp.zeros_like(dl2)

    def line_of(r, k):
        return g2.at[r, :, (gx + k) % 4] if r % 2 == 0 else g2.at[r, (gy + k) % 4]

    def step_to(r, k):
        return at_plane(0, k) if r % 2 == 0 else at_plane(k, 0)

    def g_first(r):
        for k in (2, 1, 3):
            rc(line_of(r, k), r2.at[r, k], d2, step_to(r, k), 1 + r).start()

    def g_second(r):
        came(r2.at[r, 1:4], d2, 1 + r)
        tot = line_of(r, 0)[...].astype(F32)
        for k in range(1, 4):
            tot += r2[r, k].astype(F32)
        gh[r] = tot.astype(BF16)
        for k in (2, 1, 3):
            to = ((gy if r % 2 == 0 else gx) + k) % 4
            rc(gh.at[r, to], rh.at[r, k], dh, step_to(r + 1, k), 1 + r).start()

    for r in range(GROUPS):
        for q in range(2):
            lo = r * 512 + q * 2 * LANES
            g = jnp.where(dots[:, lo:lo + 2 * LANES] > 0, dl2, zero)
            dots[:, lo:lo + 2 * LANES] = g
            g2[r, 2 * q:2 * q + 2] = jnp.transpose(dot(kt[...], g, NN)).astype(BF16).reshape(2, 4, HALF, LANES)
        g_first(r)
        if r > 1:
            g_second(r - 2)

    gk = jnp.zeros((2 * KEYS, LANES), F32)
    for r in range(GROUPS):
        gk += dot(dots[:, r * 512:(r + 1) * 512], wq[r * 512:(r + 1) * 512], NN)
        if r < 2:
            g_second(r + 2)
    gk_p[...] = gk[KEYS:].astype(BF16)
    rc(gk_p, gk_q, gkp, partner).start()
    left_with(gk_p, gkp)
    gk_own = gk[:KEYS]

    for r in range(GROUPS):
        came(rh.at[r, 1:4], dh, 1 + r)
        tot = gh[r, gy if r % 2 == 0 else gx].astype(F32)
        for k in range(1, 4):
            tot += rh[r, k].astype(F32)
        g3[r] = tot.astype(BF16)
        for other in (1, 0):
            if r or other:
                rc(g3.at[r], r3.at[2 * r + other], d3, at_head(r, 0, other)).start()
    left_with(r2.at[:, 1:4], d2)
    left_with(rh.at[:, 1:4], dh)
    left_with(r3.at[1:], d3)
    came(gk_q, gkp)
    gk_s[...] = (gk_own + gk_q[...].astype(F32)).astype(BF16).reshape(4, LANES, LANES)
    for k in (3, 2, 1):
        rc(gk_s.at[(h + k) % GROUPS], gk_r.at[k], gks, at_head(k)).start()
    left_with(gk_s.at[1:GROUPS], gks)

    fin_copy.wait()
    came(r3.at[1:], d3)
    onehot = lax.broadcasted_iota(jnp.int32, (HALF, PLANE), 1) == yx
    for r in range(GROUPS):
        g = (h - r + GROUPS) % GROUPS
        near = g3[0] if r == 0 else r3[2 * r]
        full = near.astype(F32) + r3[2 * r + 1].astype(F32)
        w = jnp.sum(jnp.where(onehot, hw[g, core], 0.0), axis=1, keepdims=True)
        gq_out[g, core, :, my_cols] = (full * w).astype(BF16)
        prod[g] = full * qfin[g].astype(F32)

    first, last = gq_out.at[0:2, core, :, my_cols], gq_out.at[2:4, core, :, my_cols]
    for k in (2, 1, 3):
        rc(first, first, d4, at_plane(0, k), 1).start()
        rc(last, last, d4, at_plane(k, 0), 2).start()
    gw_row = jnp.sum(jnp.transpose(prod[...].reshape(LANES, LANES)), axis=0, keepdims=True)
    my_seat = core * PLANE + yx
    gwb[my_seat] = gw_row
    tile = gwb.at[my_seat]
    for dy, dx in FAR_FIRST:
        rc(tile, tile, gws, at_plane(dy, dx)).start()
    left_with(gwb.at[1:PLANE], gws)
    left_with(gq_out.at[:, core, :, LANES:], d4)

    def row_of(dy):
        cols = pl.ds(pl.multiple_of(((gy + 4 - dy) % 4) * 4 * LANES, LANES), 4 * LANES)
        return gq_out.at[0:2, core, :, cols]

    def column_of(dx):
        return [
            gq_out.at[2:4, core, :, pl.ds(pl.multiple_of((4 * k + (gx + 4 - dx) % 4) * LANES, LANES), LANES)]
            for k in range(4)
        ]

    def on(refs):
        for ref in refs:
            rc(ref, ref, d4c, partner).start()

    came(gq_out.at[0:2, core, :, 0:3 * LANES], d4, 1)
    for k in (2, 1, 3):
        rc(row_of(0), row_of(0), d4, at_plane(k, 0), 2 + k).start()
    came(gq_out.at[2:4, core, :, 0:3 * LANES], d4, 2)
    for k in (2, 1, 3):
        for ref in column_of(0):
            rc(ref, ref, d4, at_plane(0, k), 5 + k).start()
    on([row_of(0)])
    on(column_of(0))

    came(gk_r.at[1:GROUPS], gks)
    own = gk_s[h].astype(F32)
    for r in range(1, GROUPS):
        own += gk_r[r].astype(F32)
    gk_out[h] = own.astype(BF16)
    for r in (3, 2, 1):
        rc(gk_out.at[h], gk_out.at[h], gkt, at_head(r)).start()
    left_with(gk_out.at[1:GROUPS], gkt)

    for k in (1, 3, 2):
        if k == 2:
            came(gwb.at[1:PLANE], gws)
            tiles = gwb.at[pl.ds(core * PLANE, PLANE)]
            rc(tiles, tiles, gwc, partner).start()
            left_with(gwb.at[0:PLANE], gwc)
        came(row_of(k), d4, 2 + k)
        on([row_of(k)])
        came(gq_out.at[2:4, core, :, 0:4 * LANES], d4, 5 + k)
        on(column_of(k))
    left_with(gq_out.at[:, core], d4c)
    came(gwb.at[0:PLANE], gwc)
    came(klb.at[1:], kls)
    t0, t1 = gwb[0:PLANE, 0, :], gwb[PLANE:, 0, :]
    lane16 = lax.broadcasted_iota(jnp.int32, (PLANE, LANES), 1)
    for t in range(2):
        def back(v, n):
            return pltpu.roll(v, (n - t * ROWS) % LANES, 1)

        lo = jnp.where(lane16 < HALF, back(t0, 0), back(t1, HALF))
        up = jnp.where(lane16 < 3 * HALF, back(t0, HALF), back(t1, ROWS))
        gw_out[:, t * LANES:(t + 1) * LANES] = jnp.where(lane16 < ROWS, lo, up).astype(BF16)

    for t in range(2):
        pair = klb[4 * t]
        for b in range(1, 4):
            pair = jnp.where(lane1 == b, klb[4 * t + b], pair)
        kl_out[:, t * LANES:(t + 1) * LANES] = pair.astype(BF16)

    came(gk_out.at[1:GROUPS], gkt)
    came(gq_out.at[:, 1 - core], d4c)

    for ref, sems in sent:
        rc(ref, ref, sems, partner).wait_send()


def finish(a, b, c, d, a_out, b_out, c_out, d_out, line, sem):
    copies = [
        pltpu.make_async_copy(src, dst, sem.at[k])
        for k, (src, dst) in enumerate(((b, b_out), (d, d_out), (c, c_out), (line, a_out)))
    ]
    for x in copies[:3]:
        x.start()
    line[...] = a[0, :]
    copies[3].start()
    for x in copies:
        x.wait()


def local(query_mla, key_mla, lse, query_index, key_index, head_weight, query_pos, key_block):
    hbm = pl.BlockSpec(memory_space=pltpu.HBM)
    vmem = pl.BlockSpec(memory_space=pltpu.VMEM)
    dma = pltpu.SemaphoreType.DMA
    V = pltpu.VMEM
    kl, gq, gw, gk = pl.pallas_call(
        body,
        out_shape=(
            jax.ShapeDtypeStruct((1, 256), BF16),
            jax.ShapeDtypeStruct((GROUPS, 2, HALF, PLANE * LANES), BF16),
            jax.ShapeDtypeStruct((PLANE, 256), BF16),
            jax.ShapeDtypeStruct((GROUPS, LANES, LANES), BF16),
        ),
        in_specs=[hbm] * 7 + [pl.BlockSpec(memory_space=pltpu.SMEM)],
        out_specs=(vmem, vmem, vmem, vmem),
        scratch_shapes=[
            V((256, 6144), BF16), V((KEYS, 6144), BF16), V((KEYS, 256), F32),
            V((GROUPS, 2, LANES, LANES), F32), V((GROUPS, 2, LANES, LANES), BF16), V((8, LANES, LANES), BF16),
            V((GROUPS, PLANE, HALF, LANES), BF16), V((GROUPS, 4, LANES), F32),
            V((2, KEYS, LANES), BF16), V((2, 1, LANES), jnp.int32),
            V((2 * KEYS, 64 * HALF), BF16), V((64 * HALF, LANES), BF16), V((2 * KEYS, LANES), F32),
            V((2, LANES, LANES), F32), V((2, LANES, LANES), F32), V((2 * KEYS, LANES), BF16),
            V((PLANE, 4, LANES), F32), V((2, 4, LANES), F32),
            V((GROUPS, 4, 4, HALF, LANES), BF16), V((GROUPS, 4, 4, HALF, LANES), BF16),
            V((GROUPS, 4, HALF, LANES), BF16), V((GROUPS, 4, HALF, LANES), BF16),
            V((GROUPS, HALF, LANES), BF16), V((8, HALF, LANES), BF16),
            V((GROUPS, HALF, LANES), BF16), V((GROUPS, HALF, LANES), F32),
            V((2 * PLANE, 1, LANES), F32), V((GROUPS, LANES, LANES), BF16), V((GROUPS, LANES, LANES), BF16),
            V((KEYS, LANES), BF16), V((KEYS, LANES), BF16),
            V((PAIRS, 2, 256), F32), V((GROUPS, 2, 4, LANES), F32), V((GROUPS, 2, HALF, PLANE), F32), V((8, 1, LANES), F32),
            V((32, 256), F32), V((PLANE, 256), F32), V((1, 256), jnp.int32), V((LANES, 2 * KEYS), BF16),
            dma((4,)), dma((2, CHUNKS)),
            dma((2,)), dma((2,)), dma((2,)), dma((5,)), dma((2,)), dma((2,)), dma((2,)), dma((2,)), dma((2,)), dma((2,)), dma((5,)), dma((5,)), dma((2,)), dma((9,)), dma((2,)), dma((2,)), dma((2,)), dma((2,)), dma((2,)), dma((2,)),
        ],
        compiler_params=pltpu.CompilerParams(
            collective_id=0, has_side_effects=True, vmem_limit_bytes=50 * 1024 * 1024
        ),
    )(*(pltpu.with_memory_space_constraint(x, pltpu.HBM) for x in (
        query_mla, key_mla, lse.T, query_index.reshape(GROUPS, 2, HALF, PLANE * LANES), key_index,
        head_weight.T, query_pos.reshape(1, 256),
    )), key_block)
    kl, gq, gw, gk = pl.pallas_call(
        finish,
        out_shape=(
            jax.ShapeDtypeStruct((256,), BF16),
            jax.ShapeDtypeStruct((GROUPS, 2, HALF, PLANE * LANES), BF16),
            jax.ShapeDtypeStruct((PLANE, 256), BF16),
            jax.ShapeDtypeStruct((GROUPS, LANES, LANES), BF16),
        ),
        in_specs=[vmem] * 4,
        out_specs=[hbm] * 4,
        scratch_shapes=[V((256,), BF16), dma((4,))],
        compiler_params=pltpu.CompilerParams(vmem_limit_bytes=1024 * 1024),
    )(kl, gq, gw, gk)
    return kl, gq.reshape(256, PLANE * LANES), gw.T, gk.reshape(KEYS, LANES)


def solution(mesh):
    return jax.shard_map(
        local,
        mesh=mesh,
        in_specs=(
            P(None, "head"), P("seq", "head"), P(None, "head"), P(None, "head"),
            P("seq", None), P(None, "head"), P(), P("seq"),
        ),
        out_specs=(P(), P(None, "head"), P(None, "head"), P("seq", None)),
        check_vma=False,
    )
```

```python
import functools
import math

import jax
import jax.numpy as jnp
from jax import lax
from jax.experimental import pallas as pl
from jax.experimental.pallas import tpu as pltpu
from jax.sharding import PartitionSpec as P

MESH = pl.DeviceIdType.MESH
F32 = jnp.float32
BF16 = jnp.bfloat16

GROUPS = 4
PLANE = 16
ROWS = 64
HALF = 32
KEYS = 512
PAIRS = 16
WIDE = 192
LANES = 128
CHUNKS = 4
CHUNK_PAIRS = PAIRS // CHUNKS
CHUNK = CHUNK_PAIRS * 2 * WIDE
NT = (((1,), (1,)), ((), ()))
TN = (((0,), (0,)), ((), ()))
NN = (((1,), (0,)), ((), ()))
ROW_ORDER = (2, 1, 3, 0)
FAR_FIRST = tuple((dy, dx) for dy in ROW_ORDER for dx in (2, 1, 3, 0) if dy or dx)
ROWS_NEAR = (0, 1, 3, 2)
NEAR_FIRST = tuple((dy, dx) for dy in ROWS_NEAR for dx in (0, 1, 3, 2) if dy or dx)
LOG2E = math.log2(math.e)


def dot(a, b, dims):
    return lax.dot_general(a, b, dims, preferred_element_type=F32)


def body(
    qm, km, lse_h, qi, ki_h, hw_h, qpos_h, kb,
    kl_out, gq_out, gw_out, gk_out,
    qbuf, kbuf, acc, blk, att_s, att_r, qall, wall, kall, kbv, dots, wq, lacc, ebuf, abuf, dlb,
    st_all, st_two, g2, r2, g3, r3, qfin, prod, gwb, gk_s, gk_r, gk_p, gk_q,
    lse, wpack, hw, klb, lse_t, hw_t, qpos, kt,
    small, ld, qloc, qz, wz, qx, kx, kvx, at, st1, st2, kls, d2, d3, d4, d4c, gws, gwc, gks, gkt, gkp,
):
    h = lax.axis_index("head")
    s = lax.axis_index("seq")
    core = s % 2
    zh = (s // 2) % 2
    yx = s // 4
    gy = yx // 4
    gx = yx % 4

    def seat(dy, dx):
        return ((gy + dy) % 4) * 4 + (gx + dx) % 4

    def at_plane(dy, dx, other_core=0):
        c = (core + other_core) % 2
        return (h, seat(dy, dx) * 4 + zh * 2 + c)

    def at_head(r, other_core=0, other_half=0):
        c = (core + other_core) % 2
        return ((h + r) % GROUPS, yx * 4 + ((zh + other_half) % 2) * 2 + c)

    partner = at_plane(0, 0, 1)

    def rc(src, dst, sems, dev, k=1):
        return pltpu.make_async_remote_copy(
            src_ref=src, dst_ref=dst, send_sem=sems.at[0], recv_sem=sems.at[k],
            device_id=dev, device_id_type=MESH,
        )

    def came(ref, sems, k=1):
        rc(ref, ref, sems, partner, k).wait_recv()

    sent = []

    def left_with(ref, sems):
        sent.append((ref, sems))

    bar = pltpu.get_barrier_semaphore()

    def hello(dev):
        pl.semaphore_signal(bar, inc=1, device_id=dev, device_id_type=MESH)

    for r in range(GROUPS):
        hello(at_head(r, 0, 1))
    for dy, dx in FAR_FIRST:
        hello(at_plane(dy, dx))
    for r in (3, 2, 1):
        hello(at_head(r, 1))
        hello(at_head(r))
    hello(partner)
    smalls = [
        pltpu.make_async_copy(src, dst, small.at[k])
        for k, (src, dst) in enumerate(
            ((lse_h, lse_t), (hw_h, hw_t), (ki_h, kall.at[0]), (qpos_h, qpos))
        )
    ]
    for c in smalls:
        c.start()

    def loop(lo, hi, f):
        def step(k, carry):
            f(k)
            return carry

        lax.fori_loop(lo, hi, step, 0)

    def chunk_copies(k):
        cols = pl.ds(pl.multiple_of(k * CHUNK, LANES), CHUNK)
        return (
            pltpu.make_async_copy(qm.at[:, cols], qbuf.at[:, cols], ld.at[0, k]),
            pltpu.make_async_copy(km.at[:, cols], kbuf.at[:, cols], ld.at[1, k]),
        )

    def start_chunk(k):
        for c in chunk_copies(k):
            c.start()

    loop(0, CHUNKS, start_chunk)

    def own_head(k):
        cols = pl.ds(pl.multiple_of(k * LANES, LANES), LANES)
        pltpu.make_async_copy(qi.at[h, core, :, cols], qall.at[0, k], qloc.at[0]).start()

    loop(0, PLANE, own_head)
    my_cols = pl.ds(pl.multiple_of(yx * LANES, LANES), LANES)
    fin_copy = pltpu.make_async_copy(qi.at[:, core, :, my_cols], qfin, qloc.at[1])
    fin_copy.start()

    for c in smalls:
        c.wait()
    for p in range(PAIRS):
        lse[p] = lse_t[2 * p:2 * p + 2, :] * LOG2E
    kbv[0] = jnp.full((1, LANES), kb[0] * KEYS, jnp.int32)
    group4 = lax.broadcasted_iota(jnp.int32, (4, LANES), 1) // HALF

    def moved(v, a, b):
        return v if a == b else pltpu.roll(v, ((a - b) * HALF) % LANES, 1)

    def side_by_side(parts, b, group):
        out = moved(parts[0], 0, b)
        for a in range(1, 4):
            out = jnp.where(group == a, moved(parts[a], a, b), out)
        return out

    for t in range(2):
        both = hw_t[:, t * LANES:(t + 1) * LANES]
        fours = [jnp.concatenate([both[4 * k + a:4 * k + a + 1] for k in range(4)], axis=0) for a in range(4)]
        for b in range(4):
            wpack[2 * t + b // 2, b % 2] = side_by_side(fours, b, group4)

    acc[...] = jnp.zeros_like(acc)
    scale = WIDE ** -0.5 * LOG2E

    def attend(k):
        for c in chunk_copies(k):
            c.wait()
        for j in range(CHUNK_PAIRS):
            pair = k * CHUNK_PAIRS + j
            base = pair * (2 * WIDE)
            lo = pl.ds(pl.multiple_of(base, LANES), 2 * LANES)
            hi = pl.ds(pl.multiple_of(base + LANES, LANES), 2 * LANES)
            lane = lax.broadcasted_iota(jnp.int32, (256, 2 * LANES), 1)
            q_a = jnp.where(lane < WIDE, qbuf[:, lo], 0).astype(BF16)
            q_b = jnp.where(lane >= 2 * LANES - WIDE, qbuf[:, hi], 0).astype(BF16)
            ls = lse[pair]
            s_a = dot(kbuf[:, lo], q_a, NT)
            s_b = dot(kbuf[:, hi], q_b, NT)
            acc[...] += jnp.exp2(s_a * scale - ls[0:1, :]) + jnp.exp2(s_b * scale - ls[1:2, :])

    loop(0, 2, attend)

    pl.semaphore_wait(bar, GROUPS + 15 + 6 + 1)
    wall[0] = wpack[h, core]
    for r in (3, 2, 1):
        g = (h + r) % GROUPS
        slot = GROUPS - r
        rc(qi.at[g, core, :, my_cols], qall.at[slot, yx], qz, at_head(r)).start()
        rc(wpack.at[g, core], wall.at[slot], wz, at_head(r)).start()
    left_with(qall.at[1:GROUPS, yx], qz)
    left_with(wall.at[1:GROUPS], wz)
    rc(ki_h, kall.at[1], kx, partner).start()
    rc(kbv.at[0], kbv.at[1], kvx, partner).start()
    left_with(kall.at[1], kx)
    left_with(kbv.at[1], kvx)

    loop(2, CHUNKS, attend)

    group = lax.broadcasted_iota(jnp.int32, (LANES, LANES), 1) // HALF
    for t in range(2):
        parts = [acc[q * LANES:(q + 1) * LANES, t * LANES:(t + 1) * LANES] for q in range(4)]
        for b in range(4):
            packed = side_by_side(parts, b, group)
            blk[2 * t + b // 2, b % 2] = packed
            att_s[2 * t + b // 2, b % 2] = packed.astype(BF16)

    for r in (3, 2, 1, 0):
        for k in range(2):
            if r or k:
                slot = k * 4 + (GROUPS - r) % GROUPS
                mine = att_s.at[(h + r) % GROUPS, (core + k) % 2]
                rc(mine, att_r.at[slot], at, at_head(r, k)).start()
    left_with(att_r.at[1:], at)

    came(qall.at[1:GROUPS, yx], qz)
    came(wall.at[1:GROUPS], wz)
    mine = qall.at[1:GROUPS, yx]
    for dy, dx in NEAR_FIRST:
        rc(mine, mine, qx, at_plane(dy, dx), 1 + dy).start()
    left_with(qall.at[1:GROUPS, 1:PLANE], qx)

    lacc[...] = jnp.zeros_like(lacc)

    def index_part(slots, k, n):
        wide = n * LANES
        qq = qall[slots, pl.ds(4 * k, 4 * n)].reshape(-1, LANES)
        d = dot(keys(), qq, NT)
        add = None
        for i, r in enumerate(range(GROUPS)[slots]):
            part = d[:, i * wide:(i + 1) * wide]
            cols = pl.ds(pl.multiple_of(r * 512 + k * LANES, LANES), wide)
            dots[:, cols] = part.astype(BF16)
            for j in range(n):
                w = wall[r, pl.ds(k + j, 1), :]
                term = w * jnp.maximum(part[:, j * LANES:(j + 1) * LANES], 0.0)
                add = term if add is None else add + term
        lacc[...] += add

    def keys():
        return kall[...].reshape(2 * KEYS, LANES)

    pltpu.make_async_copy(qall.at[0], qall.at[0], qloc.at[0]).wait()
    came(kall.at[1], kx)
    came(kbv.at[1], kvx)
    for k in (0, 2):
        index_part(slice(0, 1), k, 2)

    for dy in ROWS_NEAR:
        if dy == ROWS_NEAR[-1]:
            came(att_r.at[1:], at)
            for c in range(2):
                a = blk[h, core] if c == 0 else att_r[4].astype(F32)
                for r in range(1, GROUPS):
                    a += att_r[c * 4 + r].astype(F32)
                abuf[c] = a
        came(qall.at[1:GROUPS, 0:(4 if dy else 3)], qx, 1 + dy)
        index_part(slice(1, GROUPS), (gy + 4 - dy) % 4, 1)

    lane1 = lax.broadcasted_iota(jnp.int32, (1, LANES), 1) // HALF

    def spread(v, mask):
        v = jnp.where(mask, v, jnp.zeros_like(v))
        v = v + pltpu.roll(v, HALF, 1)
        return v + pltpu.roll(v, 2 * HALF, 1)

    limit = jnp.where(h < 2, qpos[:, :LANES], qpos[:, LANES:])
    limit = spread(limit, lane1 == (h % 2) * 2 + core)
    rowid = lax.broadcasted_iota(jnp.int32, (LANES, LANES), 0)

    def fold(v, op):
        v = op(v, pltpu.roll(v, 2 * HALF, 1))
        return op(v, pltpu.roll(v, HALF, 1))

    peak = None
    for c in range(2):
        logit = None
        for q in range(4):
            lg = fold(lacc[c * KEYS + q * LANES:c * KEYS + (q + 1) * LANES], jnp.add)
            logit = lg if q == 0 else jnp.where(group == q, lg, logit)
        ok = rowid + (kbv[c] + group * LANES) <= limit
        logit = jnp.where(ok, logit, -1e30)
        ebuf[c] = logit
        abuf[c] = jnp.where(ok, abuf[c], 0.0)
        top = jnp.max(logit, axis=0, keepdims=True)
        peak = top if c == 0 else jnp.maximum(peak, top)
    peak = fold(peak, jnp.maximum)
    norm = total = cross = jnp.zeros((1, LANES), F32)
    for c in range(2):
        ok = rowid + (kbv[c] + group * LANES) <= limit
        rel = ebuf[c] - peak
        e = jnp.where(ok, jnp.exp(rel), 0.0)
        ebuf[c] = e
        av = abuf[c]
        norm += jnp.sum(e, axis=0, keepdims=True)
        total += jnp.sum(av, axis=0, keepdims=True)
        cross += jnp.sum(
            jnp.where(ok, av * (jnp.log(jnp.where(ok, av, 1.0)) - rel), 0.0), axis=0, keepdims=True
        )
    norm, total, cross = (fold(v, jnp.add) for v in (norm, total, cross))
    tile = jnp.concatenate([peak, norm, total, cross], axis=0)
    st_all[yx] = tile

    mine = st_all.at[yx]
    for dy, dx in FAR_FIRST:
        rc(mine, mine, st1, at_plane(dy, dx)).start()
    left_with(st_all.at[1:], st1)

    kt[...] = jnp.transpose(keys())
    hw[...] = jnp.transpose(hw_t[...]).reshape(GROUPS, 2, HALF, PLANE)

    wcol = jnp.transpose(wall[...].reshape(4 * 4, LANES))
    for r in range(GROUPS):
        for k in range(4):
            qq = qall[r, 4 * k:4 * k + 4].reshape(4 * HALF, LANES).astype(F32)
            n = r * 4 + k
            wq[n * LANES:(n + 1) * LANES] = (qq * wcol[:, n:n + 1]).astype(BF16)

    def merge(t):
        pk = jnp.max(t[:, 0, :], axis=0, keepdims=True)
        nm = jnp.sum(t[:, 1, :] * jnp.exp(t[:, 0, :] - pk), axis=0, keepdims=True)
        tt = jnp.sum(t[:, 2, :], axis=0, keepdims=True)
        cr = jnp.sum(t[:, 3, :] + t[:, 2, :] * (pk - t[:, 0, :]), axis=0, keepdims=True)
        return pk, nm, tt, cr

    came(st_all.at[1:], st1)
    st_two[0] = jnp.concatenate(merge(st_all[...]), axis=0)
    rc(st_two.at[0], st_two.at[1], st2, at_head(0, 0, 1)).start()
    left_with(st_two.at[0], st2)
    came(st_two.at[1], st2)
    peak_g, norm_g, total_g, cross_g = merge(st_two[...])
    inv_t = 1.0 / total_g
    kl = cross_g * inv_t - jnp.log(total_g) + jnp.log(norm_g)
    klb[2 * h + core] = kl
    mine = klb.at[2 * h + core]
    for r in (3, 2, 1, 0):
        for k in range(2):
            if r or k:
                rc(mine, mine, kls, at_head(r, k)).start()
    left_with(klb.at[1:], kls)

    grow = jnp.exp(peak - peak_g) / norm_g
    for c in range(2):
        packed = ebuf[c] * grow - abuf[c] * inv_t
        for q in range(4):
            dlb[c * KEYS + q * LANES:c * KEYS + (q + 1) * LANES] = spread(packed, group == q).astype(BF16)
    dl = dlb[...]
    dl2 = jnp.concatenate([dl, dl], axis=1)
    zero = jnp.zeros_like(dl2)

    for r in range(GROUPS):
        for q in range(2):
            lo = r * 512 + q * 2 * LANES
            g = jnp.where(dots[:, lo:lo + 2 * LANES] > 0, dl2, zero)
            dots[:, lo:lo + 2 * LANES] = g
            g2[r, 8 * q:8 * q + 8] = jnp.transpose(dot(kt[...], g, NN)).astype(BF16).reshape(8, HALF, LANES)
        for k, (dy, dx) in enumerate(FAR_FIRST):
            rc(g2.at[r, seat(dy, dx)], r2.at[r, k], d2, at_plane(dy, dx), 1 + r).start()
    left_with(r2.at[:, 0:15], d2)

    gk = jnp.zeros((2 * KEYS, LANES), F32)
    for r in range(GROUPS):
        gk += dot(dots[:, r * 512:(r + 1) * 512], wq[r * 512:(r + 1) * 512], NN)
    gk_p[...] = gk[KEYS:].astype(BF16)
    rc(gk_p, gk_q, gkp, partner).start()
    left_with(gk_p, gkp)
    gk_own = gk[:KEYS]

    for r in range(GROUPS):
        came(r2.at[r, 0:15], d2, 1 + r)
        tot = g2[r, yx].astype(F32)
        for p in range(PLANE - 1):
            tot += r2[r, p].astype(F32)
        g3[r] = tot.astype(BF16)
        for other in (1, 0):
            if r or other:
                rc(g3.at[r], r3.at[2 * r + other], d3, at_head(r, 0, other)).start()
    left_with(r3.at[1:], d3)
    came(gk_q, gkp)
    gk_s[...] = (gk_own + gk_q[...].astype(F32)).astype(BF16).reshape(4, LANES, LANES)
    for k in (3, 2, 1):
        rc(gk_s.at[(h + k) % GROUPS], gk_r.at[k], gks, at_head(k)).start()
    left_with(gk_s.at[1:GROUPS], gks)

    fin_copy.wait()
    came(r3.at[1:], d3)
    onehot = lax.broadcasted_iota(jnp.int32, (HALF, PLANE), 1) == yx
    for r in range(GROUPS):
        g = (h - r + GROUPS) % GROUPS
        near = g3[0] if r == 0 else r3[2 * r]
        full = near.astype(F32) + r3[2 * r + 1].astype(F32)
        w = jnp.sum(jnp.where(onehot, hw[g, core], 0.0), axis=1, keepdims=True)
        gq_out[g, core, :, my_cols] = (full * w).astype(BF16)
        prod[g] = full * qfin[g].astype(F32)

    first, last = gq_out.at[0:2, core, :, my_cols], gq_out.at[2:4, core, :, my_cols]
    for k in (2, 1, 3):
        rc(first, first, d4, at_plane(0, k), 1).start()
        rc(last, last, d4, at_plane(k, 0), 2).start()
    gw_row = jnp.sum(jnp.transpose(prod[...].reshape(LANES, LANES)), axis=0, keepdims=True)
    my_seat = core * PLANE + yx
    gwb[my_seat] = gw_row
    tile = gwb.at[my_seat]
    for dy, dx in FAR_FIRST:
        rc(tile, tile, gws, at_plane(dy, dx)).start()
    left_with(gwb.at[1:PLANE], gws)
    left_with(gq_out.at[:, core, :, LANES:], d4)

    def row_of(dy):
        cols = pl.ds(pl.multiple_of(((gy + 4 - dy) % 4) * 4 * LANES, LANES), 4 * LANES)
        return gq_out.at[0:2, core, :, cols]

    def column_of(dx):
        return [
            gq_out.at[2:4, core, :, pl.ds(pl.multiple_of((4 * k + (gx + 4 - dx) % 4) * LANES, LANES), LANES)]
            for k in range(4)
        ]

    def on(refs):
        for ref in refs:
            rc(ref, ref, d4c, partner).start()

    came(gq_out.at[0:2, core, :, 0:3 * LANES], d4, 1)
    for k in (2, 1, 3):
        rc(row_of(0), row_of(0), d4, at_plane(k, 0), 2 + k).start()
    came(gq_out.at[2:4, core, :, 0:3 * LANES], d4, 2)
    for k in (2, 1, 3):
        for ref in column_of(0):
            rc(ref, ref, d4, at_plane(0, k), 5 + k).start()
    on([row_of(0)])
    on(column_of(0))

    came(gk_r.at[1:GROUPS], gks)
    own = gk_s[h].astype(F32)
    for r in range(1, GROUPS):
        own += gk_r[r].astype(F32)
    gk_out[h] = own.astype(BF16)
    for r in (3, 2, 1):
        rc(gk_out.at[h], gk_out.at[h], gkt, at_head(r)).start()
    left_with(gk_out.at[1:GROUPS], gkt)

    for k in (1, 3, 2):
        if k == 2:
            came(gwb.at[1:PLANE], gws)
            tiles = gwb.at[pl.ds(core * PLANE, PLANE)]
            rc(tiles, tiles, gwc, partner).start()
            left_with(gwb.at[0:PLANE], gwc)
        came(row_of(k), d4, 2 + k)
        on([row_of(k)])
        came(gq_out.at[2:4, core, :, 0:4 * LANES], d4, 5 + k)
        on(column_of(k))
    left_with(gq_out.at[:, core], d4c)
    came(gwb.at[0:PLANE], gwc)
    came(klb.at[1:], kls)
    t0, t1 = gwb[0:PLANE, 0, :], gwb[PLANE:, 0, :]
    lane16 = lax.broadcasted_iota(jnp.int32, (PLANE, LANES), 1)
    for t in range(2):
        def back(v, n):
            return pltpu.roll(v, (n - t * ROWS) % LANES, 1)

        lo = jnp.where(lane16 < HALF, back(t0, 0), back(t1, HALF))
        up = jnp.where(lane16 < 3 * HALF, back(t0, HALF), back(t1, ROWS))
        gw_out[:, t * LANES:(t + 1) * LANES] = jnp.where(lane16 < ROWS, lo, up).astype(BF16)

    for t in range(2):
        pair = klb[4 * t]
        for b in range(1, 4):
            pair = jnp.where(lane1 == b, klb[4 * t + b], pair)
        kl_out[:, t * LANES:(t + 1) * LANES] = pair.astype(BF16)

    came(gk_out.at[1:GROUPS], gkt)
    came(gq_out.at[:, 1 - core], d4c)

    for ref, sems in sent:
        rc(ref, ref, sems, partner).wait_send()


def finish(a, b, c, d, a_out, b_out, c_out, d_out, line, sem):
    copies = [
        pltpu.make_async_copy(src, dst, sem.at[k])
        for k, (src, dst) in enumerate(((b, b_out), (d, d_out), (c, c_out), (line, a_out)))
    ]
    for x in copies[:3]:
        x.start()
    line[...] = a[0, :]
    copies[3].start()
    for x in copies:
        x.wait()


def local(query_mla, key_mla, lse, query_index, key_index, head_weight, query_pos, key_block):
    hbm = pl.BlockSpec(memory_space=pltpu.HBM)
    vmem = pl.BlockSpec(memory_space=pltpu.VMEM)
    dma = pltpu.SemaphoreType.DMA
    V = pltpu.VMEM
    kl, gq, gw, gk = pl.pallas_call(
        body,
        out_shape=(
            jax.ShapeDtypeStruct((1, 256), BF16),
            jax.ShapeDtypeStruct((GROUPS, 2, HALF, PLANE * LANES), BF16),
            jax.ShapeDtypeStruct((PLANE, 256), BF16),
            jax.ShapeDtypeStruct((GROUPS, LANES, LANES), BF16),
        ),
        in_specs=[hbm] * 7 + [pl.BlockSpec(memory_space=pltpu.SMEM)],
        out_specs=(vmem, vmem, vmem, vmem),
        scratch_shapes=[
            V((256, 6144), BF16), V((KEYS, 6144), BF16), V((KEYS, 256), F32),
            V((GROUPS, 2, LANES, LANES), F32), V((GROUPS, 2, LANES, LANES), BF16), V((8, LANES, LANES), BF16),
            V((GROUPS, PLANE, HALF, LANES), BF16), V((GROUPS, 4, LANES), F32),
            V((2, KEYS, LANES), BF16), V((2, 1, LANES), jnp.int32),
            V((2 * KEYS, 64 * HALF), BF16), V((64 * HALF, LANES), BF16), V((2 * KEYS, LANES), F32),
            V((2, LANES, LANES), F32), V((2, LANES, LANES), F32), V((2 * KEYS, LANES), BF16),
            V((PLANE, 4, LANES), F32), V((2, 4, LANES), F32),
            V((GROUPS, PLANE, HALF, LANES), BF16), V((GROUPS, PLANE, HALF, LANES), BF16),
            V((GROUPS, HALF, LANES), BF16), V((8, HALF, LANES), BF16),
            V((GROUPS, HALF, LANES), BF16), V((GROUPS, HALF, LANES), F32),
            V((2 * PLANE, 1, LANES), F32), V((GROUPS, LANES, LANES), BF16), V((GROUPS, LANES, LANES), BF16),
            V((KEYS, LANES), BF16), V((KEYS, LANES), BF16),
            V((PAIRS, 2, 256), F32), V((GROUPS, 2, 4, LANES), F32), V((GROUPS, 2, HALF, PLANE), F32), V((8, 1, LANES), F32),
            V((32, 256), F32), V((PLANE, 256), F32), V((1, 256), jnp.int32), V((LANES, 2 * KEYS), BF16),
            dma((4,)), dma((2, CHUNKS)),
            dma((2,)), dma((2,)), dma((2,)), dma((5,)), dma((2,)), dma((2,)), dma((2,)), dma((2,)), dma((2,)), dma((2,)), dma((5,)), dma((2,)), dma((9,)), dma((2,)), dma((2,)), dma((2,)), dma((2,)), dma((2,)), dma((2,)),
        ],
        compiler_params=pltpu.CompilerParams(
            collective_id=0, has_side_effects=True, vmem_limit_bytes=50 * 1024 * 1024
        ),
    )(*(pltpu.with_memory_space_constraint(x, pltpu.HBM) for x in (
        query_mla, key_mla, lse.T, query_index.reshape(GROUPS, 2, HALF, PLANE * LANES), key_index,
        head_weight.T, query_pos.reshape(1, 256),
    )), key_block)
    kl, gq, gw, gk = pl.pallas_call(
        finish,
        out_shape=(
            jax.ShapeDtypeStruct((256,), BF16),
            jax.ShapeDtypeStruct((GROUPS, 2, HALF, PLANE * LANES), BF16),
            jax.ShapeDtypeStruct((PLANE, 256), BF16),
            jax.ShapeDtypeStruct((GROUPS, LANES, LANES), BF16),
        ),
        in_specs=[vmem] * 4,
        out_specs=[hbm] * 4,
        scratch_shapes=[V((256,), BF16), dma((4,))],
        compiler_params=pltpu.CompilerParams(vmem_limit_bytes=1024 * 1024),
    )(kl, gq, gw, gk)
    return kl, gq.reshape(256, PLANE * LANES), gw.T, gk.reshape(KEYS, LANES)


def solution(mesh):
    return jax.shard_map(
        local,
        mesh=mesh,
        in_specs=(
            P(None, "head"), P("seq", "head"), P(None, "head"), P(None, "head"),
            P("seq", None), P(None, "head"), P(), P("seq"),
        ),
        out_specs=(P(), P(None, "head"), P(None, "head"), P("seq", None)),
        check_vma=False,
    )
```
